32 devices in a mesh: shard: 4 (over y, x), replica: 8 (over z, core).
Axes of the slice: x: 2, y: 2, z: 4, core: 2. Of those that a mesh axis runs over, the one named last changes fastest.
Arguments:
- tokens: bfloat16 [4096, 896], P(('shard', 'replica')), may hold values from -6 to 6
- seg_ids: int32 [32, 128], P(('shard', 'replica')), may hold values from 0 to 7, never falling along the last dimension, each value on 1 to 64 neighbouring positions
- norm1_gain: bfloat16 [896], P('shard'), may hold values from 0.25 to 1.75
- w_qkv: bfloat16 [896, 1152], P('shard'), may hold values from -0.1875 to 0.1875
- b_qkv: bfloat16 [1152], P('shard'), may hold values from -3 to 3
- w_out: bfloat16 [896, 896], P('shard'), may hold values from -0.75 to 0.75
- norm2_gain: bfloat16 [896], P('shard'), may hold values from 0.25 to 1.75
- w_gate: bfloat16 [896, 4864], P('shard'), may hold values from -0.1875 to 0.1875
- w_up: bfloat16 [896, 4864], P('shard'), may hold values from -0.1875 to 0.1875
- w_down: bfloat16 [4864, 896], P('shard'), may hold values from -0.15625 to 0.15625
- cotangent: bfloat16 [4096, 896], P(('shard', 'replica')), may hold values from -6 to 6
Outputs:
- layer_out: bfloat16 [4096, 896], P(('shard', 'replica'))
- grad_tokens: float32 [4096, 896], P(('shard', 'replica'))
- grad_norm1: float32 [896], P('shard')
- grad_qkv: float32 [896, 1152], P('shard')
- grad_bias: float32 [1152], P('shard')
- grad_out: float32 [896, 896], P('shard')
- grad_norm2: float32 [896], P('shard')
- grad_gate: float32 [896, 4864], P('shard')
- grad_up: float32 [896, 4864], P('shard')
- grad_down: float32 [4864, 896], P('shard')
The draws below stay inside these ranges and needn't reach their ends.
Inputs may be any that keep to these rules, and one draw needn't show every extreme that they name: `seg_ids`: within a row, ids never fall; each document has 1 to 64 tokens and one has exactly 64.
All inputs are finite; a program needn't handle non-finite values.
Results may differ from the reference program's by a relative error of at most 0.01.
Values may be sent and summed in bfloat16 or wider, within the bound.
No kernel may reach another device: no remote copies, remote signals or barrier semaphores. Data moves between devices by JAX's collectives and lax.ppermute only.
A program may use at most 256 MiB of HBM per device.

```python
import math
import jax
import jax.numpy as jnp
import numpy as np
from jax import lax

D = 896
QUERY_HEADS = 14
KEY_VALUE_HEADS = 2
HEAD_SIZE = 64
FF = 4864
TOK_DEV = 128
QKV = 1152
SEQS = 32
TOKENS = 4096


def levels(rng, shape, cuts, low, top_value):
    def one(dim, parts):
        draws = jax.random.uniform(jax.random.fold_in(jax.random.fold_in(rng, 6), dim), (parts,), jnp.float32, low / len(cuts), top_value / len(cuts))
        return jnp.repeat(jnp.exp(draws), shape[dim] // parts).reshape((-1,) + (1,) * (len(shape) - dim - 1))

    level = one(*cuts[0])
    for cut in cuts[1:]:
        level = level * one(*cut)
    return level


def split_up(number_of, total, reach, lean):
    loads = [(1 << 20) // math.isqrt(grade ** lean) + 1 for grade in range(2, number_of + 1)]
    surplus, given = total - reach - (number_of - 1), [1] * (number_of - 1)
    while surplus > 0:
        movable = [i for i in range(number_of - 1) if given[i] < reach]
        whole, remaining = sum([loads[i] for i in movable]), surplus
        for i in movable:
            addition = min(reach - given[i], max(1, remaining * loads[i] // whole), surplus)
            given[i] = given[i] + addition
            surplus = surplus - addition
    return np.array([reach] + given)


def uneven_parts(stream_key, amount, total, most, skew):
    if amount == 2:
        one = jax.random.randint(stream_key, (), max(1, total - most), min(most, total - 1) + 1)
        return jnp.stack([one, total - one])
    sizes = jnp.asarray(split_up(amount, total, most, skew), jnp.int32)
    couples = (amount - 1) // 2
    source_of, sink = sizes[1:1 + 2 * couples:2], sizes[2:2 + 2 * couples:2]
    room = jnp.minimum(source_of - 1, most - sink)
    moved = jax.random.randint(jax.random.fold_in(stream_key, 1), (couples,), 0, 1 << 20) % (room + 1)
    sizes = sizes.at[1:1 + 2 * couples:2].set(source_of - moved).at[2:2 + 2 * couples:2].set(sink + moved)
    return sizes[jax.random.permutation(jax.random.fold_in(stream_key, 2), amount)]


def scatter_about(stream_key, shape, deviation, limit, pieces=(), held_as=jnp.bfloat16):
    result = jax.random.normal(stream_key, shape, jnp.float32) * deviation
    if len(pieces) > 0:
        result = levels(stream_key, shape, pieces, -0.22, 0.18) * result
    return jnp.clip(result, min=-limit, max=limit).astype(held_as)


def setup_inputs(seed: int = 0) -> dict:
    splits = jax.random.split(jax.random.key(seed), 12)
    return {
        "tokens": scatter_about(splits[0], (TOKENS, D), 1.0, 6.0, ((0, 32),)),
        "seg_ids": jax.vmap(lambda own: jnp.searchsorted(jnp.cumsum(uneven_parts(own, 8, TOK_DEV, TOK_DEV // 2, 1)), jnp.arange(TOK_DEV), side="right"))(jax.random.split(splits[1], SEQS)).reshape((SEQS, TOK_DEV)).astype(jnp.int32),
        "norm1_gain": jnp.clip(1.0 + 0.15 * jax.random.normal(splits[2], (D,), jnp.float32), 0.25, 1.75).astype(jnp.bfloat16),
        "w_qkv": scatter_about(splits[3], (D, QKV), D ** -0.5, 0.1875, ((0, 4),)),
        "b_qkv": scatter_about(splits[4], (QKV,), 0.5, 3.0, ((0, 4),)),
        "w_out": scatter_about(splits[5], (QUERY_HEADS * HEAD_SIZE, D), (QUERY_HEADS * HEAD_SIZE // 16) ** -0.5, 0.75, ((0, 4),)),
        "norm2_gain": jnp.clip(1.0 + 0.15 * jax.random.normal(splits[6], (D,), jnp.float32), 0.25, 1.75).astype(jnp.bfloat16),
        "w_gate": scatter_about(splits[7], (D, FF), D ** -0.5, 0.1875, ((0, 4),)),
        "w_up": scatter_about(splits[8], (D, FF), D ** -0.5, 0.1875, ((0, 4),)),
        "w_down": scatter_about(splits[9], (FF, D), (FF // 4) ** -0.5, 0.15625, ((0, 4),)),
        "cotangent": scatter_about(splits[10], (TOKENS, D), 1.0, 6.0, ((0, 32),)),
    }


@jax.custom_vjp
def low(v):
    return lax.optimization_barrier(v.astype(jnp.bfloat16)).astype(jnp.float32)

@jax.custom_vjp
def low_back(v):
    return v

def low_keep(v):
    return (low(v), None)

def low_pass(kept, grad):
    return (grad,)

def back_keep(v):
    return (v, None)

def back_low(kept, grad):
    return (low(grad),)
low.defvjp(low_keep, low_pass)
low_back.defvjp(back_keep, back_low)
EPS = 1e-06
THETA = 1000000.0
HIGH = lax.Precision.HIGHEST

def matmul(left, right):
    return jnp.dot(left, right, precision=HIGH)

def rope_tables(seg):
    sequence_length = seg.shape[0]
    index = jnp.arange(sequence_length, dtype=jnp.int32)
    before = jnp.concatenate([seg[:1] - 1, seg[:-1]])
    starts = jnp.where(seg != before, index, jnp.zeros_like(index))
    first = lax.cummax(starts, axis=0)
    position = (index - first).astype(jnp.float32)
    half = HEAD_SIZE // 2
    freq = THETA ** (-(jnp.arange(half, dtype=jnp.float32) * 2.0 / HEAD_SIZE))
    angle = position[:, None] * freq[None, :]
    return (jnp.cos(angle)[:, None, :], jnp.sin(angle)[:, None, :])

def apply_rotary(value, cosine_table, sine_table):
    half = HEAD_SIZE // 2
    first, second = (value[..., :half], value[..., half:])
    return jnp.concatenate([first * cosine_table - second * sine_table, second * cosine_table + first * sine_table], axis=-1)

def layer(params, x, seg):
    gain_one, wqkv, bqkv, wout, gain_two, wgate, wup, wdown = params
    sequence_length = x.shape[0]
    group_factor = QUERY_HEADS // KEY_VALUE_HEADS
    r_one = lax.rsqrt(lax.optimization_barrier(jnp.mean(x * x, axis=1, keepdims=True)) + EPS)
    n_one = low(x * r_one * gain_one)
    joined_heads = low_back(matmul(n_one, wqkv) + bqkv)
    cosine_table, sine_table = rope_tables(seg)
    query_rows = apply_rotary(joined_heads[:, :QUERY_HEADS * HEAD_SIZE].reshape(sequence_length, QUERY_HEADS, HEAD_SIZE), cosine_table, sine_table)
    key_rows = apply_rotary(joined_heads[:, QUERY_HEADS * HEAD_SIZE:(QUERY_HEADS + KEY_VALUE_HEADS) * HEAD_SIZE].reshape(sequence_length, KEY_VALUE_HEADS, HEAD_SIZE), cosine_table, sine_table)
    value_rows = joined_heads[:, (QUERY_HEADS + KEY_VALUE_HEADS) * HEAD_SIZE:].reshape(sequence_length, KEY_VALUE_HEADS, HEAD_SIZE)
    query_rows, key_rows, value_rows = (low(query_rows), low(key_rows), low(value_rows))
    grouped_heads = query_rows.reshape(sequence_length, KEY_VALUE_HEADS, group_factor, HEAD_SIZE)
    scores = jnp.einsum('qhgd,khd->hgqk', grouped_heads, key_rows, precision=HIGH) * HEAD_SIZE ** (-0.5)
    scores = low_back(scores)
    index = jnp.arange(sequence_length)
    allowed = (index[None, :] <= index[:, None]) & (seg[None, :] == seg[:, None])
    scores = jnp.where(allowed, scores, -1e+30)
    probs = low(jax.nn.softmax(scores, axis=-1))
    mixed = jnp.einsum('hgqk,khd->qhgd', probs, value_rows, precision=HIGH).reshape(sequence_length, QUERY_HEADS * HEAD_SIZE)
    mixed = low(low_back(mixed))
    hidden = x + low_back(matmul(mixed, wout))
    r_two = lax.rsqrt(lax.optimization_barrier(jnp.mean(hidden * hidden, axis=1, keepdims=True)) + EPS)
    n_two = low(hidden * r_two * gain_two)
    gate = low_back(matmul(n_two, wgate))
    up_val = low_back(matmul(n_two, wup))
    act = low(jax.nn.silu(gate) * up_val)
    return hidden + low_back(matmul(act, wdown))

def reference(tokens, seg_ids, norm1_gain, w_qkv, b_qkv, w_out, norm2_gain, w_gate, w_up, w_down, cotangent):
    params = tuple((a.astype(jnp.float32) for a in (norm1_gain, w_qkv, b_qkv, w_out, norm2_gain, w_gate, w_up, w_down)))
    inputs = tokens.astype(jnp.float32).reshape(SEQS, TOK_DEV, D)

    def forward(weights, xs):

        def one_seq(pair):
            return layer(weights, pair[0], pair[1])
        return lax.map(jax.checkpoint(one_seq), (xs, seg_ids))
    outputs, pull = jax.vjp(forward, params, inputs)
    grads, dinputs = pull(cotangent.astype(jnp.float32).reshape(SEQS, TOK_DEV, D))
    return (outputs.reshape(TOKENS, D).astype(jnp.bfloat16), dinputs.reshape(TOKENS, D), grads[0], grads[1], grads[2], grads[3], grads[4], grads[5], grads[6], grads[7])
```

```python
import jax
import jax.numpy as jnp
from jax import lax
from jax.sharding import PartitionSpec as P

QUERY_HEADS = 14
KEY_VALUE_HEADS = 2
HEAD_SIZE = 64

EPS = 1e-06
THETA = 1000000.0
BF = jnp.bfloat16
F32 = jnp.float32


def rope_tables(seg):
    sequence_length = seg.shape[0]
    index = jnp.arange(sequence_length, dtype=jnp.int32)
    before = jnp.concatenate([seg[:1] - 1, seg[:-1]])
    starts = jnp.where(seg != before, index, jnp.zeros_like(index))
    first = lax.cummax(starts, axis=0)
    position = (index - first).astype(jnp.float32)
    half = HEAD_SIZE // 2
    freq = THETA ** (-(jnp.arange(half, dtype=jnp.float32) * 2.0 / HEAD_SIZE))
    angle = position[:, None] * freq[None, :]
    return (jnp.cos(angle)[:, None, :], jnp.sin(angle)[:, None, :])


def apply_rotary(value, cosine_table, sine_table):
    half = HEAD_SIZE // 2
    first, second = (value[..., :half], value[..., half:])
    return jnp.concatenate(
        [first * cosine_table - second * sine_table, second * cosine_table + first * sine_table],
        axis=-1,
    )


def rotate_back(grad, cosine_table, sine_table):
    half = HEAD_SIZE // 2
    first, second = (grad[..., :half], grad[..., half:])
    return jnp.concatenate(
        [first * cosine_table + second * sine_table, second * cosine_table - first * sine_table],
        axis=-1,
    )


def norm_back(value, inv_root, gain, dnormed):
    scaled = dnormed * gain
    dgain = jnp.sum(dnormed * value * inv_root, axis=0)
    dvalue = inv_root * scaled - value * inv_root**3 * jnp.mean(
        scaled * value, axis=1, keepdims=True
    )
    return (dvalue, dgain)


def masked_scores(grouped_heads, key_rows, allowed):
    scores = jnp.einsum(
        "qhgd,khd->hgqk", grouped_heads, key_rows, preferred_element_type=jnp.float32
    ) * HEAD_SIZE ** (-0.5)
    return jnp.where(allowed, scores, -1e30)


def weighted_rows(left, right):
    return jnp.einsum("tr,tc->rc", left, right, preferred_element_type=jnp.float32)


def dot(a, b):
    return jnp.dot(a, b, preferred_element_type=F32)


def dot_t(a, b):
    return lax.dot_general(a, b, (((1,), (1,)), ((), ())), preferred_element_type=F32)


def swap_core(x):
    n = lax.axis_size("replica")
    return lax.ppermute(x, "replica", [(i, i ^ 1) for i in range(n)])


def exchange(x):
    return lax.all_to_all(x, "shard", split_axis=0, concat_axis=0, tiled=True)


def spread(x):
    n = lax.axis_size("shard")
    return exchange(jnp.concatenate([x] * n, axis=0))


def reduce_shards(x):
    n = lax.axis_size("shard")
    return jnp.sum(exchange(x).reshape(n, x.shape[0] // n, x.shape[1]).astype(F32), axis=0)


def line_sum(x):
    line = lax.axis_size("replica") // 2
    half = line // 2
    place = lax.axis_index("replica") // 2

    def pairs(chips):
        return [(2 * a + k, 2 * b + k) for a, b in chips for k in range(2)]

    total = x
    for i in range(half - 1):
        inward = pairs([(i, i + 1), (line - 1 - i, line - 2 - i)])
        total = total + lax.ppermute(total, "replica", inward)
    middle = pairs([(half - 1, half), (half, half - 1)])
    total = total + lax.ppermute(total, "replica", middle)
    for i in reversed(range(half - 1)):
        outward = pairs([(i + 1, i), (line - 2 - i, line - 1 - i)])
        arrived = lax.ppermute(total, "replica", outward)
        total = jnp.where((place > i) & (place < line - 1 - i), total, arrived)
    return total


def both_cores(x, core):
    other = swap_core(x)
    return jnp.where(core == 0, x, other), jnp.where(core == 0, other, x)


def body(
    tokens, seg_ids, norm1_gain, w_qkv, b_qkv, w_out, norm2_gain, w_gate, w_up, w_down, cotangent
):
    shards = lax.axis_size("shard")
    core = lax.axis_index("replica") % 2
    sequence_length, width = tokens.shape
    rows = norm1_gain.shape[0]
    half_rows = rows // 2
    joined = w_qkv.shape[1]
    bias_rows = b_qkv.shape[0]
    ff = w_gate.shape[1]
    slab = ff // (2 * shards)
    group_factor = QUERY_HEADS // KEY_VALUE_HEADS
    seg = seg_ids[0]
    x_val = tokens.astype(F32)

    vector = jnp.concatenate([norm1_gain, norm2_gain, b_qkv])
    extra = jnp.zeros((8, joined), BF).at[0, : vector.shape[0]].set(vector)
    mine = lax.dynamic_slice_in_dim(w_qkv, core * half_rows, half_rows, 0)
    block = half_rows + 8
    qkv0, qkv1 = both_cores(spread(jnp.concatenate([mine, extra], axis=0)), core)
    qkv0 = qkv0.reshape(shards, block, joined)
    qkv1 = qkv1.reshape(shards, block, joined)
    wqkv = jnp.stack([qkv0[:, :half_rows], qkv1[:, :half_rows]], axis=1).reshape(width, joined)
    vectors = qkv0[:, half_rows]
    gain_one = vectors[:, :rows].reshape(width).astype(F32)
    gain_two = vectors[:, rows : 2 * rows].reshape(width).astype(F32)
    bqkv = vectors[:, 2 * rows : 2 * rows + bias_rows].reshape(joined).astype(F32)
    out0, out1 = both_cores(
        spread(lax.dynamic_slice_in_dim(w_out, core * half_rows, half_rows, 0)), core
    )
    wout = jnp.stack(
        [out0.reshape(shards, half_rows, width), out1.reshape(shards, half_rows, width)], axis=1
    ).reshape(width, width)

    def columns(w):
        return jnp.concatenate(
            [
                jnp.where(
                    core == 0,
                    w[:, 2 * j * slab : (2 * j + 1) * slab],
                    w[:, (2 * j + 1) * slab : (2 * j + 2) * slab],
                )
                for j in range(shards)
            ],
            axis=0,
        )

    wgate = exchange(columns(w_gate))
    wup = exchange(columns(w_up))
    wdown = lax.dynamic_slice_in_dim(w_down, core * slab, slab, 0)
    dy_mine = spread(cotangent)
    dy_all = jnp.concatenate([dy_mine, swap_core(dy_mine)], axis=0)

    r_one = lax.rsqrt(jnp.mean(x_val * x_val, axis=1, keepdims=True) + EPS)
    n_one = (x_val * r_one * gain_one).astype(BF)
    joined_heads = dot(n_one, wqkv) + bqkv
    cosine_table, sine_table = rope_tables(seg)
    query_rows = apply_rotary(
        joined_heads[:, : QUERY_HEADS * HEAD_SIZE].reshape(sequence_length, QUERY_HEADS, HEAD_SIZE),
        cosine_table,
        sine_table,
    ).astype(BF)
    key_rows = apply_rotary(
        joined_heads[
            :, QUERY_HEADS * HEAD_SIZE : (QUERY_HEADS + KEY_VALUE_HEADS) * HEAD_SIZE
        ].reshape(sequence_length, KEY_VALUE_HEADS, HEAD_SIZE),
        cosine_table,
        sine_table,
    ).astype(BF)
    value_rows = (
        joined_heads[:, (QUERY_HEADS + KEY_VALUE_HEADS) * HEAD_SIZE :]
        .reshape(sequence_length, KEY_VALUE_HEADS, HEAD_SIZE)
        .astype(BF)
    )
    grouped_heads = query_rows.reshape(sequence_length, KEY_VALUE_HEADS, group_factor, HEAD_SIZE)
    index = jnp.arange(sequence_length)
    allowed = (index[None, :] <= index[:, None]) & (seg[None, :] == seg[:, None])
    scores = masked_scores(grouped_heads, key_rows, allowed)
    top = jnp.max(scores, axis=-1, keepdims=True)
    logsum = top + jnp.log(jnp.sum(jnp.exp(scores - top), axis=-1, keepdims=True))
    probs = jnp.exp(scores - logsum)
    probs_low = probs.astype(BF)
    mixed = jnp.einsum("hgqk,khd->qhgd", probs_low, value_rows, preferred_element_type=F32)
    mixed = mixed.reshape(sequence_length, QUERY_HEADS * HEAD_SIZE).astype(BF)
    hidden = x_val + dot(mixed, wout)
    r_two = lax.rsqrt(jnp.mean(hidden * hidden, axis=1, keepdims=True) + EPS)
    n_two = (hidden * r_two * gain_two).astype(BF)

    n_mine = spread(n_two)
    n_all = jnp.concatenate([n_mine, swap_core(n_mine)], axis=0)
    gate = dot(n_all, wgate)
    up_val = dot(n_all, wup)
    sigma = jax.nn.sigmoid(gate)
    swish = gate * sigma
    act = (swish * up_val).astype(BF)
    grad_down = weighted_rows(act, dy_all).astype(BF)
    d_act = dot_t(dy_all, wdown)
    d_gate = (d_act * up_val * sigma * (1.0 + gate * (1.0 - sigma))).astype(BF)
    d_up = (d_act * swish).astype(BF)
    grad_gate = exchange(weighted_rows(n_all, d_gate).astype(BF))
    grad_up = exchange(weighted_rows(n_all, d_up).astype(BF))

    def plane_sum(partial):
        count = partial.shape[0] // 2
        both = partial[:count] + swap_core(partial[count:].astype(BF)).astype(F32)
        return reduce_shards(both.astype(BF))

    d_ntwo = plane_sum(dot_t(d_gate, wgate) + dot_t(d_up, wup))
    layer_out = (hidden + plane_sum(dot(act, wdown))).astype(BF)

    def rows_of_cores(x):
        first, second = both_cores(x, core)
        return jnp.concatenate([first, second], axis=0)

    def columns_of_cores(x):
        first, second = both_cores(x, core)
        pieces = []
        for j in range(shards):
            pieces += [first[j * rows : (j + 1) * rows], second[j * rows : (j + 1) * rows]]
        return jnp.concatenate([p.astype(F32) for p in pieces], axis=1)

    down_part = rows_of_cores(line_sum(grad_down)).astype(F32)
    gate_part = columns_of_cores(line_sum(grad_gate))
    up_part = columns_of_cores(line_sum(grad_up))

    d_out = cotangent.astype(F32)
    d_hid, d_gain_two = norm_back(hidden, r_two, gain_two, d_ntwo)
    d_hidden = d_out + d_hid
    d_attn = d_hidden.astype(BF)
    mixed_gradient = dot_t(d_attn, wout).astype(BF)
    grouped_gradient = mixed_gradient.reshape(
        sequence_length, KEY_VALUE_HEADS, group_factor, HEAD_SIZE
    )
    d_probs = jnp.einsum(
        "qhgd,khd->hgqk", grouped_gradient, value_rows, preferred_element_type=F32
    )
    value_gradient = jnp.einsum(
        "hgqk,qhgd->khd", probs_low, grouped_gradient, preferred_element_type=F32
    )
    d_scores = (probs * (d_probs - jnp.sum(d_probs * probs, axis=-1, keepdims=True))).astype(BF)
    d_query = jnp.einsum(
        "hgqk,khd->qhgd", d_scores, key_rows, preferred_element_type=F32
    ) * HEAD_SIZE ** (-0.5)
    key_gradient = jnp.einsum(
        "hgqk,qhgd->khd", d_scores, grouped_heads, preferred_element_type=F32
    ) * HEAD_SIZE ** (-0.5)
    d_query = rotate_back(
        d_query.reshape(sequence_length, QUERY_HEADS, HEAD_SIZE), cosine_table, sine_table
    )
    key_gradient = rotate_back(key_gradient, cosine_table, sine_table)
    d_joined = jnp.concatenate(
        [
            d_query.reshape(sequence_length, QUERY_HEADS * HEAD_SIZE),
            key_gradient.reshape(sequence_length, KEY_VALUE_HEADS * HEAD_SIZE),
            value_gradient.reshape(sequence_length, KEY_VALUE_HEADS * HEAD_SIZE),
        ],
        axis=1,
    ).astype(BF)
    d_bias = jnp.sum(d_joined.astype(F32), axis=0)
    d_none = dot_t(d_joined, wqkv)
    d_x, d_gain_one = norm_back(x_val, r_one, gain_one, d_none)
    grad_tokens = d_hidden + d_x

    def core_half(partial):
        split = partial.reshape(shards, 2, partial.shape[0] // (2 * shards), partial.shape[1])
        keep = jnp.where(core == 0, split[:, 0], split[:, 1])
        give = jnp.where(core == 0, split[:, 1], split[:, 0])
        kept = keep + swap_core(give.astype(BF)).astype(F32)
        return kept.astype(BF).reshape(-1, partial.shape[1])

    out_half = line_sum(reduce_shards(core_half(weighted_rows(mixed, d_attn))).astype(BF))
    out_part = rows_of_cores(out_half).astype(F32)
    vector = jnp.concatenate(
        [
            d_gain_one.reshape(shards, rows),
            d_gain_two.reshape(shards, rows),
            d_bias.reshape(shards, bias_rows),
        ],
        axis=1,
    )
    extra = jnp.zeros((shards, 2, 8, joined), F32).at[:, 0, 0, : vector.shape[1]].set(vector)
    qkv_partial = jnp.concatenate(
        [weighted_rows(n_one, d_joined).reshape(shards, 2, half_rows, joined), extra], axis=2
    ).reshape(-1, joined)
    qkv_half = line_sum(reduce_shards(core_half(qkv_partial)).astype(BF))
    first, second = both_cores(qkv_half, core)
    qkv_part = jnp.concatenate([first[:half_rows], second[:half_rows]], axis=0).astype(F32)
    vector = first[half_rows].astype(F32)
    one_part = vector[:rows]
    two_part = vector[rows : 2 * rows]
    bias_part = vector[2 * rows : 2 * rows + bias_rows]
    return (
        layer_out,
        grad_tokens,
        one_part,
        qkv_part,
        bias_part,
        out_part,
        two_part,
        gate_part,
        up_part,
        down_part,
    )


def solution(mesh):
    split = P(("shard", "replica"), None)
    matrix = P("shard", None)
    vector = P("shard")
    in_specs = (
        split, split, vector, matrix, vector, matrix, vector, matrix, matrix, matrix, split,
    )
    out_specs = (split, split, vector, matrix, vector, matrix, vector, matrix, matrix, matrix)
    return jax.shard_map(body, mesh=mesh, in_specs=in_specs, out_specs=out_specs, check_vma=False)
```

```python
import functools
import jax
import jax.numpy as jnp
from jax import lax
from jax.experimental import pallas as pl
from jax.experimental.pallas import tpu as pltpu
from jax.sharding import PartitionSpec as P

QUERY_HEADS = 14
KEY_VALUE_HEADS = 2
HEAD_SIZE = 64
HALF = HEAD_SIZE // 2
GROUP = QUERY_HEADS // KEY_VALUE_HEADS
PAIRS = QUERY_HEADS // 2
LANES = 128

EPS = 1e-06
THETA = 1000000.0
SCALE = HEAD_SIZE ** (-0.5)
BF = jnp.bfloat16
F32 = jnp.float32


def swap_core(x, tag):
    n = lax.axis_size("replica")
    with jax.named_scope(tag):
        return lax.ppermute(x, "replica", [(i, i ^ 1) for i in range(n)])


def shard_swap(x, k, tag):
    n = lax.axis_size("shard")
    with jax.named_scope(f"{tag}{k}"):
        return lax.ppermute(x, "shard", [(i, i ^ k) for i in range(n)])


def spread(x, tag):
    return [x] + [shard_swap(x, k, tag) for k in range(1, lax.axis_size("shard"))]


def line_sum(x, tag):
    line = lax.axis_size("replica") // 2
    half = line // 2
    place = lax.axis_index("replica") // 2

    def hop(value, chips, name):
        links = [(2 * a + k, 2 * b + k) for a, b in chips for k in range(2)]
        with jax.named_scope(f"{tag}{name}"):
            return lax.ppermute(value, "replica", links)

    total = x
    for i in range(half - 1):
        total = total + hop(total, [(i, i + 1), (line - 1 - i, line - 2 - i)], f"in{i}")
    total = total + hop(total, [(half - 1, half), (half, half - 1)], "mid")
    for i in reversed(range(half - 1)):
        arrived = hop(total, [(i + 1, i), (line - 2 - i, line - 1 - i)], f"out{i}")
        total = jnp.where((place > i) & (place < line - 1 - i), total, arrived)
    return total


def dot(a, b):
    return jnp.dot(a, b, preferred_element_type=F32)


def dot_t(a, b):
    return lax.dot_general(a, b, (((1,), (1,)), ((), ())), preferred_element_type=F32)


def t_dot(a, b):
    return lax.dot_general(a, b, (((0,), (0,)), ((), ())), preferred_element_type=F32)


def call(kernel, name, outs, where, args, scratch=(), flops=0, spare=8):
    total = sum(a.size * a.dtype.itemsize for a in args)
    total += sum(o.size * jnp.dtype(o.dtype).itemsize for o in outs)
    grant = total * 17 // 16 + sum(b.inner_aval.size * b.dtype.itemsize for b in scratch)
    vmem = pl.BlockSpec(memory_space=pltpu.VMEM)
    return pl.pallas_call(
        kernel,
        out_shape=outs,
        in_specs=[pl.BlockSpec(memory_space=pltpu.SMEM)] + [vmem] * len(args),
        out_specs=[vmem] * len(outs),
        scratch_shapes=list(scratch),
        cost_estimate=pl.CostEstimate(flops=flops, bytes_accessed=total, transcendentals=0),
        compiler_params=pltpu.CompilerParams(vmem_limit_bytes=grant + (spare << 20)),
        name=name,
    )(where, *args)


def shape(dims, dtype=BF):
    return jax.ShapeDtypeStruct(dims, dtype)


def rows_at(start, size):
    return pl.ds(pl.multiple_of(start, 8 if size % 16 else 16), size)


def pack_kernel(shards, where, gate, up, *rest):
    outs, stage = rest[:shards], rest[shards]
    rows, slab = gate.shape[0], stage.shape[2]
    s, c = where[0], where[1]
    for j in range(2 * shards):

        @pl.when(c == j % 2)
        def _(j=j):
            k = (j // 2) ^ s
            stage[k, :rows] = gate[:, j * slab : (j + 1) * slab]
            stage[k, rows:] = up[:, j * slab : (j + 1) * slab]

    for k in range(shards):
        outs[k][...] = stage[k]


def pack(where, gate, up, shards):
    rows, ff = gate.shape
    slab = ff // (2 * shards)
    piece = (2 * rows, slab)
    return call(
        functools.partial(pack_kernel, shards), "pack", [shape(piece)] * shards, where,
        [gate, up], [pltpu.VMEM((shards,) + piece, BF)],
    )


def place_rows(dst, s, c, own, mine, other):
    rows = own.shape[0]
    half = rows // 2
    dst[rows_at(s * rows, rows)] = own[...]
    for k in range(1, len(mine) + 1):
        base = (s ^ k) * rows
        dst[rows_at(base + c * half, half)] = mine[k - 1][:half]
        dst[rows_at(base + (1 - c) * half, half)] = other[k - 1][:half]


def lane_kinds(x):
    lane = lax.broadcasted_iota(jnp.int32, x.shape, 1)
    low = lane < HEAD_SIZE
    zero = jnp.zeros_like(x)
    turned = pltpu.roll(x, HEAD_SIZE, 1)
    return [
        [jnp.where(low, x, zero), jnp.where(low, zero, turned)],
        [jnp.where(low, turned, zero), jnp.where(low, zero, x)],
    ]


def swap_halves(x):
    lane = lax.broadcasted_iota(jnp.int32, x.shape, 1)
    first = (lane % HEAD_SIZE) < HALF
    return jnp.where(first, pltpu.roll(x, LANES - HALF, 1), pltpu.roll(x, HALF, 1))


def attend_kernel(shards, where, x, cos, sin, mask, own, extra, *rest):
    n = shards - 1
    mine, other = rest[:n], rest[n : 2 * n]
    n1_ref, q_ref, k_ref, v_ref, p_ref, o_ref, w_ref, vec_ref = rest[2 * n :]
    s, c = where[0], where[1]
    width = x.shape[1]
    half = own.shape[0] // 2
    place_rows(w_ref, s, c, own, mine, other)
    vec = extra[...].astype(F32)
    for piece in mine:
        vec = vec + piece[half:].astype(F32)
    vec_ref[...] = vec
    xf = x[...].astype(F32)
    root = lax.rsqrt(jnp.mean(xf * xf, axis=1, keepdims=True) + EPS)
    n1 = (xf * root * vec[0:1, :width]).astype(BF)
    n1_ref[...] = n1
    joined = dot(n1, w_ref[...]) + vec[2:3]
    cosine, sine, allowed = cos[...], sin[...], mask[...] > 0.5

    def turn(v):
        return v * cosine + swap_halves(v) * sine

    keys = turn(joined[:, width : width + LANES])
    values = joined[:, width + LANES : width + 2 * LANES]
    keys_low = keys.astype(BF)
    values_low = values.astype(BF)
    k_ref[...] = keys_low
    v_ref[...] = values_low
    key_kinds = lane_kinds(keys_low.astype(F32))
    value_kinds = lane_kinds(values_low.astype(F32))
    key_kinds = [[k.astype(BF) for k in ks] for ks in key_kinds]
    value_kinds = [[v.astype(BF) for v in vs] for vs in value_kinds]
    for i in range(PAIRS):
        q = turn(joined[:, i * LANES : (i + 1) * LANES]).astype(BF)
        q_ref[:, i * LANES : (i + 1) * LANES] = q
        mixed = jnp.zeros(q.shape, F32)
        for side in range(2):
            h = 2 * i + side
            g = h // GROUP
            scores = dot_t(q, key_kinds[g][side]) * SCALE
            scores = jnp.where(allowed, scores, -1e30)
            top = jnp.max(scores, axis=-1, keepdims=True)
            e = jnp.exp(scores - top)
            p = e / jnp.sum(e, axis=-1, keepdims=True)
            p_ref[h] = p
            mixed = mixed + dot(p.astype(BF), value_kinds[g][side])
        o_ref[:, i * LANES : (i + 1) * LANES] = mixed.astype(BF)


def attend(where, x, tables, own, extra, mine, other, shards):
    tokens, width = x.shape
    joined = own.shape[1]
    outs = [
        shape((tokens, width)), shape((tokens, width)), shape((tokens, LANES)),
        shape((tokens, LANES)), shape((QUERY_HEADS, tokens, tokens), F32),
        shape((tokens, width)), shape((width, joined)), shape(extra.shape, F32),
    ]
    return call(
        functools.partial(attend_kernel, shards), "attend", outs, where,
        [x, *tables, own, extra, *mine, *other],
        flops=2 * tokens * width * joined + 8 * QUERY_HEADS * tokens * tokens * LANES,
    )


def mix_kernel(shards, where, x, o, vec, own, *rest):
    n = shards - 1
    mine, other = rest[:n], rest[n : 2 * n]
    h_ref, n2_ref, w_ref = rest[2 * n :]
    place_rows(w_ref, where[0], where[1], own, mine, other)
    width = x.shape[1]
    h = x[...].astype(F32) + dot(o[...], w_ref[...])
    h_ref[...] = h
    root = lax.rsqrt(jnp.mean(h * h, axis=1, keepdims=True) + EPS)
    n2_ref[...] = (h * root * vec[1:2, :width]).astype(BF)


def mix(where, x, o, vec, own, mine, other, shards):
    tokens, width = x.shape
    outs = [shape(x.shape, F32), shape(x.shape), shape((width, width))]
    return call(
        functools.partial(mix_kernel, shards), "mix", outs, where,
        [x, o, vec, own, *mine, *other], flops=2 * tokens * width * width,
    )


def down_back_kernel(pieces, where, down, *rest):
    parts, (dact_ref, dy_ref) = rest[:pieces], rest[pieces:]
    tokens = parts[0].shape[0]
    for i in range(pieces):
        dy_ref[i * tokens : (i + 1) * tokens] = parts[i][...]
    slab = dact_ref.shape[1]
    w = down[rows_at(where[1] * slab, slab)]
    step = 2 * tokens

    @pl.loop(0, pieces // 2)
    def _(i):
        at = pl.ds(pl.multiple_of(i * step, step), step)
        dact_ref[at] = dot_t(dy_ref[at], w)


def down_back(where, down, parts, slab):
    tokens, width = parts[0].shape
    total = tokens * len(parts)
    outs = [shape((total, slab), F32), shape((total, width))]
    return call(
        functools.partial(down_back_kernel, len(parts)), "down_back", outs, where,
        [down, *parts], flops=2 * total * width * slab,
    )


def feed_kernel(shards, where, dact, dy, *rest):
    pieces = 2 * shards
    parts, rest = rest[:pieces], rest[pieces:]
    weights, rest = rest[:shards], rest[shards:]
    d1_ref, d2_ref, act_ref, dgate_ref, dup_ref, n_ref, wg_ref, wu_ref = rest
    s = where[0]
    tokens = parts[0].shape[0]
    rows = weights[0].shape[0] // 2
    for k in range(shards):
        at = rows_at((s ^ k) * rows, rows)
        wg_ref[at] = weights[k][:rows]
        wu_ref[at] = weights[k][rows:]
    for i in range(pieces):
        n_ref[i * tokens : (i + 1) * tokens] = parts[i][...]
    step = 2 * tokens

    @pl.loop(0, pieces // 2)
    def _(i):
        at = pl.ds(pl.multiple_of(i * step, step), step)
        block = n_ref[at]
        gate = dot(block, wg_ref[...])
        up = dot(block, wu_ref[...])
        sigma = jax.nn.sigmoid(gate)
        swish = gate * sigma
        act_ref[at] = (swish * up).astype(BF)
        da = dact[at]
        dgate_ref[at] = (da * up * sigma * (1.0 + gate * (1.0 - sigma))).astype(BF)
        dup_ref[at] = (da * swish).astype(BF)

    cut = d1_ref.shape[0]
    grad = t_dot(act_ref[...], dy[...])
    d1_ref[...] = grad[:cut].astype(BF)
    d2_ref[...] = grad[cut:].astype(BF)


def feed(where, dact, dy, parts, weights):
    shards = len(weights)
    total, slab = dact.shape
    width = dy.shape[1]
    cut = slab // 32 * 16
    outs = [
        shape((cut, width)), shape((slab - cut, width)), shape((total, slab)),
        shape((total, slab)), shape((total, slab)), shape((total, width)),
        shape((width, slab)), shape((width, slab)),
    ]
    return call(
        functools.partial(feed_kernel, shards), "feed", outs, where,
        [dact, dy, *parts, *weights], flops=6 * total * width * slab,
    )


def wide_kernel(shards, where, n, dgate, dup, *rest):
    outs, acc = rest[:shards], rest[shards]
    rows = outs[0].shape[0] // 2
    s = where[0]
    acc[...] = t_dot(n[...], dgate[...])
    for k in range(shards):
        outs[k][:rows] = acc[rows_at((s ^ k) * rows, rows)].astype(BF)
    acc[...] = t_dot(n[...], dup[...])
    for k in range(shards):
        outs[k][rows:] = acc[rows_at((s ^ k) * rows, rows)].astype(BF)


def wide(where, n, dgate, dup, shards):
    total, width = n.shape
    slab = dgate.shape[1]
    outs = [shape((2 * width // shards, slab))] * shards
    return call(
        functools.partial(wide_kernel, shards), "wide", outs, where, [n, dgate, dup],
        [pltpu.VMEM((width, slab), F32)], flops=4 * total * width * slab,
    )


def lay_kernel(shards, where, *rest):
    mine, other = rest[:shards], rest[shards : 2 * shards]
    gate_ref, up_ref, stage = rest[2 * shards :]
    rows, slab = gate_ref.shape[0], stage.shape[2]
    s, c = where[0], where[1]
    for k in range(shards):
        stage[k] = mine[k][...]
        stage[shards + k] = other[k][...]
    for j in range(2 * shards):
        at = ((j // 2) ^ s) + jnp.where(c == j % 2, 0, shards)
        gate_ref[:, j * slab : (j + 1) * slab] = stage[at, :rows].astype(F32)
        up_ref[:, j * slab : (j + 1) * slab] = stage[at, rows:].astype(F32)


def lay(where, mine, other):
    shards = len(mine)
    rows, slab = mine[0].shape[0] // 2, mine[0].shape[1]
    outs = [shape((rows, 2 * shards * slab), F32)] * 2
    return call(
        functools.partial(lay_kernel, shards), "lay", outs, where, [*mine, *other],
        [pltpu.VMEM((2 * shards, 2 * rows, slab), BF)],
    )


def narrow_kernel(where, dgate, dup, wg, wu, keep, give):
    count = keep.shape[0]
    step = count // 2

    def block(i):
        at = pl.ds(pl.multiple_of(i * step, step), step)
        return dot_t(dgate[at], wg[...]) + dot_t(dup[at], wu[...])

    @pl.loop(0, 2)
    def _(i):
        give[pl.ds(pl.multiple_of(i * step, step), step)] = block(i + 2).astype(BF)

    @pl.loop(0, 2)
    def _(i):
        keep[pl.ds(pl.multiple_of(i * step, step), step)] = block(i)


def narrow(where, dgate, dup, wg, wu):
    total, slab = dgate.shape
    width = wg.shape[0]
    outs = [shape((total // 2, width), F32), shape((total // 2, width))]
    return call(
        narrow_kernel, "narrow", outs, where, [dgate, dup, wg, wu],
        flops=4 * total * width * slab,
    )


def back_kernel(shards, blocks, where, *rest):
    dn, rest = rest[:shards], rest[shards:]
    hidden, ct, x, vec, wout, wqkv, mixed, n1, query, keys, values, probs, cos, sin, y = rest[:15]
    gt_ref, keep, give, da_ref, acc_q, acc_o, dob_ref = rest[15:]
    s, c = where[0], where[1]
    tokens, width = x.shape
    joined = wqkv.shape[1]
    rows = width // shards
    half = rows // 2
    tall, flat = blocks
    cosine, sine = cos[...], sin[...]
    gain1, gain2 = vec[0:1, :width], vec[1:2, :width]

    dn2 = dn[0][...]
    for k in range(1, shards):
        dn2 = dn2 + dn[k][...].astype(F32)
    h = hidden[...]
    root = lax.rsqrt(jnp.mean(h * h, axis=1, keepdims=True) + EPS)
    g_norm2 = jnp.sum(dn2 * h * root, axis=0, keepdims=True)
    e = dn2 * gain2
    mean = jnp.mean(e * h, axis=1, keepdims=True)
    dh = ct[...].astype(F32) + root * e - h * (root * root * root * mean)
    dab = dh.astype(BF)
    gt_ref[...] = dh
    acc_o[...] = t_dot(mixed[...], dab)
    dob_ref[...] = dot_t(dab, wout[...]).astype(BF)

    key_kinds = [[k.astype(BF) for k in ks] for ks in lane_kinds(keys[...].astype(F32))]
    value_kinds = [[v.astype(BF) for v in vs] for vs in lane_kinds(values[...].astype(F32))]
    zero = jnp.zeros((tokens, LANES), F32)
    d_key = [[zero, zero], [zero, zero]]
    d_value = [[zero, zero], [zero, zero]]

    def turn_back(v):
        return v * cosine - swap_halves(v) * sine

    for i in range(PAIRS):
        q = query[:, i * LANES : (i + 1) * LANES]
        do = dob_ref[:, i * LANES : (i + 1) * LANES]
        dq = zero
        for side in range(2):
            head = 2 * i + side
            g = head // GROUP
            p = probs[head]
            dp = dot_t(do, value_kinds[g][side])
            d_value[g][side] = d_value[g][side] + t_dot(p.astype(BF), do)
            ds = (p * (dp - jnp.sum(p * dp, axis=-1, keepdims=True))).astype(BF)
            dq = dq + dot(ds, key_kinds[g][side])
            d_key[g][side] = d_key[g][side] + t_dot(ds, q)
        da_ref[:, i * LANES : (i + 1) * LANES] = turn_back(dq * SCALE).astype(BF)

    low = lax.broadcasted_iota(jnp.int32, (tokens, LANES), 1) < HEAD_SIZE

    def collect(parts):
        first = jnp.where(low, parts[0][0], parts[1][1])
        second = jnp.where(low, parts[1][0], parts[0][1])
        return first + pltpu.roll(second, HEAD_SIZE, 1)

    da_ref[:, width : width + LANES] = turn_back(collect(d_key) * SCALE).astype(BF)
    da_ref[:, width + LANES :] = collect(d_value).astype(BF)
    da = da_ref[...]
    acc_q[...] = t_dot(n1[...], da)
    g_bias = jnp.sum(da.astype(F32), axis=0, keepdims=True)
    dn1 = dot_t(da, wqkv[...])
    xf = x[...].astype(F32)
    root = lax.rsqrt(jnp.mean(xf * xf, axis=1, keepdims=True) + EPS)
    g_norm1 = jnp.sum(dn1 * xf * root, axis=0, keepdims=True)
    e = dn1 * gain1
    mean = jnp.mean(e * xf, axis=1, keepdims=True)
    gt_ref[...] = gt_ref[...] + root * e - xf * (root * root * root * mean)

    blank = jnp.zeros((5, LANES), F32)
    for target, side in ((keep, c), (give, 1 - c)):
        for k in range(shards):
            at = rows_at((s ^ k) * rows + side * half, half)
            for b in range(joined // LANES):
                lanes = slice(b * LANES, (b + 1) * LANES)
                base = b * (half + 8)
                target[k, base : base + half] = acc_q[at, lanes].astype(target.dtype)
                if (b + 1) * LANES <= width:
                    head = [g_norm1[:, lanes], g_norm2[:, lanes]]
                else:
                    head = [blank[:2]]
                tail = jnp.concatenate(head + [g_bias[:, lanes], blank], axis=0)
                target[k, base + half : base + half + 8] = tail.astype(target.dtype)
            for b in range(width // LANES):
                lanes = slice(b * LANES, (b + 1) * LANES)
                base = tall + b * half
                target[k, base : base + half] = acc_o[at, lanes].astype(target.dtype)
    for target, first in ((keep, 0), (give, shards)):
        for k in range(shards):
            at = slice((first + k) * tokens, (first + k + 1) * tokens)
            for b in range(width // LANES):
                base = flat + b * tokens
                value = y[at, b * LANES : (b + 1) * LANES]
                target[k, base : base + tokens] = value.astype(target.dtype)


def layout_of(width, joined, rows, tokens):
    half = rows // 2
    tall = joined // LANES * (half + 8)
    flat = tall + width // LANES * half
    return tall, flat, flat + width // LANES * tokens


def back(where, dn, hidden, ct, x, vec, wout, wqkv, mixed, n1, query, keys, values, probs, cos, sin, y):
    shards = len(dn)
    tokens, width = x.shape
    joined = wqkv.shape[1]
    tall, flat, whole = layout_of(width, joined, width // shards, tokens)
    outs = [
        shape(x.shape, F32), shape((shards, whole, LANES), F32), shape((shards, whole, LANES)),
    ]
    return call(
        functools.partial(back_kernel, shards, (tall, flat)), "back", outs, where,
        [*dn, hidden, ct, x, vec, wout, wqkv, mixed, n1, query, keys, values, probs, cos, sin, y],
        [
            pltpu.VMEM((tokens, joined), BF), pltpu.VMEM((width, joined), F32),
            pltpu.VMEM((width, width), F32), pltpu.VMEM((tokens, width), BF),
        ],
        flops=4 * tokens * width * (joined + width),
    )


def merge_kernel(shards, where, keep, arrived, *outs):
    for k in range(shards):
        total = keep[k] + arrived[k].astype(F32)
        outs[k][...] = total.astype(outs[k].dtype)


def merge(where, keep, arrived):
    shards = keep.shape[0]
    outs = [shape(keep.shape[1:], F32)] + [shape(keep.shape[1:])] * (shards - 1)
    return call(functools.partial(merge_kernel, shards), "merge", outs, where, [keep, arrived])


def finish_kernel(flat, where, hidden, own, *rest):
    arrived, (item, out_ref) = rest[:-2], rest[-2:]
    tokens, width = hidden.shape

    def total(at):
        value = own[at]
        for piece in arrived:
            value = value + piece[at].astype(F32)
        return value

    item[...] = total(slice(0, flat)).astype(BF)
    for b in range(width // LANES):
        lanes = slice(b * LANES, (b + 1) * LANES)
        value = total(slice(flat + b * tokens, flat + (b + 1) * tokens))
        out_ref[:, lanes] = (hidden[:, lanes] + value).astype(BF)


def finish(where, hidden, parts, flat):
    outs = [shape((flat, LANES)), shape(hidden.shape)]
    return call(
        functools.partial(finish_kernel, flat), "finish", outs, where, [hidden, *parts]
    )


def close_kernel(tall, where, mine, other, qkv_ref, out_ref, vec_ref):
    c = where[1]
    half = qkv_ref.shape[0] // 2
    for source, side in ((mine, c), (other, 1 - c)):
        at = pl.ds(pl.multiple_of(side * half, 8), half)
        for b in range(qkv_ref.shape[1] // LANES):
            base = b * (half + 8)
            qkv_ref[at, b * LANES : (b + 1) * LANES] = source[base : base + half].astype(F32)
        for b in range(out_ref.shape[1] // LANES):
            base = tall + b * half
            out_ref[at, b * LANES : (b + 1) * LANES] = source[base : base + half].astype(F32)
    for b in range(qkv_ref.shape[1] // LANES):
        base = b * (half + 8) + half
        vec_ref[:, b * LANES : (b + 1) * LANES] = mine[base : base + 8].astype(F32)


def close(where, mine, other, rows, width, joined, tall):
    outs = [shape((rows, joined), F32), shape((rows, width), F32), shape((8, joined), F32)]
    return call(functools.partial(close_kernel, tall), "close", outs, where, [mine, other])


def body(
    tokens, seg_ids, norm1_gain, w_qkv, b_qkv, w_out, norm2_gain, w_gate, w_up, w_down, cotangent
):
    shards = lax.axis_size("shard")
    shard = lax.axis_index("shard")
    replica = lax.axis_index("replica")
    core = replica % 2
    where = jnp.stack([shard, core, replica // 2]).astype(jnp.int32)
    count, width = tokens.shape
    rows = norm1_gain.shape[0]
    half_rows = rows // 2
    joined = w_qkv.shape[1]
    bias_rows = b_qkv.shape[0]
    slab = w_gate.shape[1] // (2 * shards)
    seg = seg_ids[0]

    extra = jnp.zeros((8, joined), BF)
    extra = lax.dynamic_update_slice(extra, norm1_gain[None], (0, shard * rows))
    extra = lax.dynamic_update_slice(extra, norm2_gain[None], (1, shard * rows))
    extra = lax.dynamic_update_slice(extra, b_qkv[None], (2, shard * bias_rows))
    half = lax.dynamic_slice_in_dim(w_qkv, core * half_rows, half_rows, 0)
    qkv_mine = spread(jnp.concatenate([half, extra], axis=0), "qkv")[1:]
    qkv_other = [swap_core(p, f"qkvc{k + 1}") for k, p in enumerate(qkv_mine)]
    out_mine = spread(lax.dynamic_slice_in_dim(w_out, core * half_rows, half_rows, 0), "wo")[1:]
    out_other = [swap_core(p, f"woc{k + 1}") for k, p in enumerate(out_mine)]

    packed = pack(where, w_gate, w_up, shards)
    weights = [packed[0]] + [shard_swap(packed[k], k, "wt") for k in range(1, shards)]
    dy = spread(cotangent, "dy")
    dy = dy + [swap_core(p, f"dyc{k}") for k, p in enumerate(dy)]

    index = jnp.arange(count, dtype=jnp.int32)
    first = jnp.sum((seg[None, :] < seg[:, None]).astype(jnp.int32), axis=1)
    position = (index - first).astype(F32)
    freq = THETA ** (-(jnp.arange(HALF, dtype=F32) * 2.0 / HEAD_SIZE))
    angle = position[:, None] * freq[None, :]
    cosine, sine = jnp.cos(angle), jnp.sin(angle)
    cosine_wide = jnp.tile(cosine, (1, 4))
    sine_wide = jnp.concatenate([-sine, sine, -sine, sine], axis=1)
    allowed = (index[None, :] <= index[:, None]) & (seg[None, :] == seg[:, None])

    n_one, query, keys, values, probs, mixed, wqkv, vec = attend(
        where, tokens, (cosine_wide, sine_wide, allowed.astype(F32)),
        w_qkv, extra, qkv_mine, qkv_other, shards,
    )
    hidden, n_two, wout = mix(where, tokens, mixed, vec, w_out, out_mine, out_other, shards)
    n_parts = spread(n_two, "nn")
    n_parts = n_parts + [swap_core(p, f"nnc{k}") for k, p in enumerate(n_parts)]

    dact, dy_all = down_back(where, w_down, dy, slab)
    down_one, down_two, act, d_gate, d_up, n_all, wgate, wup = feed(
        where, dact, dy_all, n_parts, weights
    )
    down_one, down_two = line_sum(down_one, "da"), line_sum(down_two, "db")

    dn_keep, dn_give = narrow(where, d_gate, d_up, wgate, wup)
    dn_sum = dn_keep + swap_core(dn_give, "dnc").astype(F32)
    dn = [dn_sum[:count]]
    for k in range(1, shards):
        send = dn_sum[k * count : (k + 1) * count].astype(BF)
        dn.append(shard_swap(send, k, "dn"))

    grads = wide(where, n_all, d_gate, d_up, shards)
    grads = [grads[0]] + [shard_swap(grads[k], k, "gx") for k in range(1, shards)]
    grads = [line_sum(g, f"i{k}") for k, g in enumerate(grads)]
    gate_part, up_part = lay(
        where, grads, [swap_core(g, f"ic{k}") for k, g in enumerate(grads)]
    )

    def both_cores(x, tag):
        other = swap_core(x, tag)
        return jnp.where(core == 0, x, other), jnp.where(core == 0, other, x)

    one, two = both_cores(down_one, "dac"), both_cores(down_two, "dbc")
    down_part = jnp.concatenate([one[0], two[0], one[1], two[1]], axis=0).astype(F32)

    wdown = lax.dynamic_slice_in_dim(w_down, core * slab, slab, 0)
    with jax.named_scope("ydot"):
        y = dot(act, wdown)
    grad_tokens, keep, give = back(
        where, dn, hidden, cotangent, tokens, vec, wout, wqkv, mixed, n_one, query, keys, values,
        probs, cosine_wide, sine_wide, y,
    )
    parts = merge(where, keep, swap_core(give, "atc"))
    parts = [parts[0]] + [shard_swap(parts[k], k, "at") for k in range(1, shards)]
    tall, flat, _ = layout_of(width, joined, rows, count)
    item, layer_out = finish(where, hidden, parts, flat)
    item = line_sum(item, "it")
    qkv_part, out_part, vec_grads = close(
        where, item, swap_core(item, "itc"), rows, width, joined, tall
    )
    one_part = lax.dynamic_slice(vec_grads[0], (shard * rows,), (rows,))
    two_part = lax.dynamic_slice(vec_grads[1], (shard * rows,), (rows,))
    bias_part = lax.dynamic_slice(vec_grads[2], (shard * bias_rows,), (bias_rows,))
    return (
        layer_out,
        grad_tokens,
        one_part,
        qkv_part,
        bias_part,
        out_part,
        two_part,
        gate_part,
        up_part,
        down_part,
    )


def solution(mesh):
    split = P(("shard", "replica"), None)
    matrix = P("shard", None)
    vector = P("shard")
    in_specs = (
        split, split, vector, matrix, vector, matrix, vector, matrix, matrix, matrix, split,
    )
    out_specs = (split, split, vector, matrix, vector, matrix, vector, matrix, matrix, matrix)
    return jax.shard_map(body, mesh=mesh, in_specs=in_specs, out_specs=out_specs, check_vma=False)
```

```python
import functools
import math
import jax
import jax.numpy as jnp
from jax import lax
from jax.experimental import pallas as pl
from jax.experimental.pallas import tpu as pltpu
from jax.sharding import PartitionSpec as P


QUERY_HEADS = 14
KEY_VALUE_HEADS = 2
HEAD_SIZE = 64
HALF = HEAD_SIZE // 2
GROUP = QUERY_HEADS // KEY_VALUE_HEADS
PAIRS = QUERY_HEADS // 2
LANES = 128

EPS = 1e-06
THETA = 1000000.0
SCALE = HEAD_SIZE ** (-0.5)
BF = jnp.bfloat16
F32 = jnp.float32


def swap_core(x):
    n = lax.axis_size("replica")
    return lax.ppermute(x, "replica", [(i, i ^ 1) for i in range(n)])


def shard_swap(x, k):
    n = lax.axis_size("shard")
    return lax.ppermute(x, "shard", [(i, i ^ k) for i in range(n)])


def pair_swap(x):
    n = lax.axis_size("replica")
    return lax.ppermute(x, "replica", [(i, i ^ 2) for i in range(n)])


def spread(x):
    return [x] + [shard_swap(x, k) for k in range(1, lax.axis_size("shard"))]


def line_sum(where, x):
    line = lax.axis_size("replica") // 2
    half = line // 2

    def hop(value, chips):
        links = [(2 * a + k, 2 * b + k) for a, b in chips for k in range(2)]
        return lax.ppermute(value, "replica", links)

    total = x
    for i in range(half - 1):
        arrived = hop(total, [(i, i + 1), (line - 1 - i, line - 2 - i)])
        total = total + arrived
    arrived = hop(total, [(half - 1, half), (half, half - 1)])
    total = total + arrived
    for i in reversed(range(half - 1)):
        arrived = hop(total, [(i + 1, i), (line - 2 - i, line - 1 - i)])
        total = pick(where, total, arrived, i, line - 1 - i)
    return total


def dot(a, b):
    return jnp.dot(a, b, preferred_element_type=F32)


def dot_t(a, b):
    return lax.dot_general(a, b, (((1,), (1,)), ((), ())), preferred_element_type=F32)


def t_dot(a, b):
    return lax.dot_general(a, b, (((0,), (0,)), ((), ())), preferred_element_type=F32)


GRANTS = {'pack': 12, 'attend': 3, 'mix': 4, 'down_back': 5, 'feed': 9, 'narrow': 4, 'back': 18, 'wide': 8, 'merge': 5, 'finish': 4, 'lay': 18, 'close': 6, 'ydown': 4, 'yout': 4, 'pick': 4, 'stack': 8}


def call(kernel, name, outs, where, args, scratch=(), flops=0, space=pltpu.VMEM):
    grant = GRANTS[name]
    total = sum(a.size * a.dtype.itemsize for a in args)
    total += sum(o.size * jnp.dtype(o.dtype).itemsize for o in outs)
    vmem = pl.BlockSpec(memory_space=pltpu.VMEM)
    return pl.pallas_call(
        kernel,
        out_shape=outs,
        in_specs=[pl.BlockSpec(memory_space=pltpu.SMEM)] + [pl.BlockSpec(memory_space=space)] * len(args),
        out_specs=[vmem] * len(outs),
        scratch_shapes=list(scratch),
        cost_estimate=pl.CostEstimate(flops=flops, bytes_accessed=total, transcendentals=0),
        compiler_params=pltpu.CompilerParams(vmem_limit_bytes=grant << 20),
    )(where, *args)


def shape(dims, dtype=BF):
    return jax.ShapeDtypeStruct(dims, dtype)


def rows_at(start, size):
    return pl.ds(pl.multiple_of(start, 8 if size % 16 else 16), size)


def pack_kernel(shards, where, gate, up, *rest):
    outs, (stage, gate_buf, up_buf, sems) = rest[:shards], rest[shards:]
    rows, slab = gate.shape[0], stage.shape[3]
    step = rows // 2
    s, c = where[0], where[1]
    copies = []
    for i in range(2):
        at = pl.ds(i * step, step)
        for m, (src, dst) in enumerate(((gate, gate_buf), (up, up_buf))):
            copy = pltpu.make_async_copy(src.at[at], dst.at[at], sems.at[i, m])
            copy.start()
            copies.append(copy)
    for i in range(2):
        for m, buf in enumerate((gate_buf, up_buf)):
            copies[2 * i + m].wait()
            for j in range(2 * shards):

                @pl.when(c == j % 2)
                def _(i=i, j=j, m=m, buf=buf):
                    at = slice(i * step, (i + 1) * step)
                    stage[(j // 2) ^ s, m, at] = buf[at, j * slab : (j + 1) * slab]

    outs[0][:rows] = stage[0, 0]
    outs[0][rows:] = stage[0, 1]
    for k in range(1, shards):
        outs[k][...] = stage[k, where[2] & 1]


def pack(where, gate, up, shards):
    rows, ff = gate.shape
    slab = ff // (2 * shards)
    outs = [shape((2 * rows, slab))] + [shape((rows, slab))] * (shards - 1)
    return call(
        functools.partial(pack_kernel, shards), "pack", outs, where, [gate, up],
        [
            pltpu.VMEM((shards, 2, rows, slab), BF), pltpu.VMEM((rows, ff), BF),
            pltpu.VMEM((rows, ff), BF), pltpu.SemaphoreType.DMA((2, 2)),
        ],
        space=pltpu.HBM,
    )


def place_rows(dst, s, c, own, mine, other):
    rows = own.shape[0]
    half = rows // 2
    dst[rows_at(s * rows, rows)] = own[...]
    for k in range(1, len(mine) + 1):
        base = (s ^ k) * rows
        dst[rows_at(base + c * half, half)] = mine[k - 1][:half]
        dst[rows_at(base + (1 - c) * half, half)] = other[k - 1][:half]


def lane_kinds(x):
    lane = lax.broadcasted_iota(jnp.int32, x.shape, 1)
    low = lane < HEAD_SIZE
    zero = jnp.zeros_like(x)
    turned = pltpu.roll(x, HEAD_SIZE, 1)
    return [
        [jnp.where(low, x, zero), jnp.where(low, zero, turned)],
        [jnp.where(low, turned, zero), jnp.where(low, zero, x)],
    ]


def swap_halves(x):
    lane = lax.broadcasted_iota(jnp.int32, x.shape, 1)
    first = (lane % HEAD_SIZE) < HALF
    return jnp.where(first, pltpu.roll(x, LANES - HALF, 1), pltpu.roll(x, HALF, 1))


def attend_kernel(shards, where, x, seg, own, extra, *rest):
    n = shards - 1
    vectors, mine, other = rest[:n], rest[n : 2 * n], rest[2 * n : 3 * n]
    n1_ref, q_ref, k_ref, v_ref, p_ref, o_ref, w_ref, vec_ref, cos_ref, sin_ref = rest[3 * n :]
    s, c = where[0], where[1]
    width, joined_width = x.shape[1], own.shape[1]
    place_rows(w_ref, s, c, own, mine, other)
    is_gain = lax.broadcasted_iota(jnp.int32, extra.shape, 0) < 2
    vec = jnp.zeros(extra.shape, F32)
    for k, piece in enumerate((extra,) + tuple(vectors)):
        value = piece[...].astype(F32)
        gains = pltpu.roll(value, (s ^ k) * (width // shards), 1)
        biases = pltpu.roll(value, (s ^ k) * (joined_width // shards), 1)
        vec = vec + jnp.where(is_gain, gains, biases)
    vec_ref[...] = vec
    xf = x[...].astype(F32)
    root = lax.rsqrt(jnp.mean(xf * xf, axis=1, keepdims=True) + EPS)
    n1 = (xf * root * vec[0:1, :width]).astype(BF)
    n1_ref[...] = n1
    joined = dot(n1, w_ref[...]) + vec[2:3]
    tokens = x.shape[0]
    square = (tokens, LANES)
    down = lax.broadcasted_iota(jnp.int32, square, 0)
    along = lax.broadcasted_iota(jnp.int32, square, 1)
    of_key = jnp.broadcast_to(seg[...], square).astype(F32)
    of_query = of_key.T
    allowed = (along <= down) & (of_key == of_query)
    before = jnp.where(of_key < of_query, 1.0, 0.0)
    position = down.astype(F32) - jnp.sum(before, axis=1, keepdims=True)
    power = (along % HALF).astype(F32) * (2.0 / HEAD_SIZE)
    angle = position * jnp.exp(power * -math.log(THETA))
    cosine = jnp.cos(angle)
    sine = jnp.sin(angle)
    sine = jnp.where((along % HEAD_SIZE) < HALF, -sine, sine)
    cos_ref[...] = cosine
    sin_ref[...] = sine

    def turn(v):
        return v * cosine + swap_halves(v) * sine

    keys = turn(joined[:, width : width + LANES])
    values = joined[:, width + LANES : width + 2 * LANES]
    keys_low = keys.astype(BF)
    values_low = values.astype(BF)
    k_ref[...] = keys_low
    v_ref[...] = values_low
    key_kinds = lane_kinds(keys_low.astype(F32))
    value_kinds = lane_kinds(values_low.astype(F32))
    key_kinds = [[k.astype(BF) for k in ks] for ks in key_kinds]
    value_kinds = [[v.astype(BF) for v in vs] for vs in value_kinds]
    for i in range(PAIRS):
        q = turn(joined[:, i * LANES : (i + 1) * LANES]).astype(BF)
        q_ref[:, i * LANES : (i + 1) * LANES] = q
        mixed = jnp.zeros(q.shape, F32)
        for side in range(2):
            h = 2 * i + side
            g = h // GROUP
            scores = dot_t(q, key_kinds[g][side]) * SCALE
            scores = jnp.where(allowed, scores, -1e30)
            top = jnp.max(scores, axis=-1, keepdims=True)
            e = jnp.exp(scores - top)
            p = e / jnp.sum(e, axis=-1, keepdims=True)
            p_ref[h] = p
            mixed = mixed + dot(p.astype(BF), value_kinds[g][side])
        o_ref[:, i * LANES : (i + 1) * LANES] = mixed.astype(BF)


def attend(where, x, seg, own, vectors, mine, other, shards):
    tokens, width = x.shape
    joined = own.shape[1]
    outs = [
        shape((tokens, width)), shape((tokens, width)), shape((tokens, LANES)),
        shape((tokens, LANES)), shape((QUERY_HEADS, tokens, tokens), F32),
        shape((tokens, width)), shape((width, joined)), shape(vectors[0].shape, F32),
        shape((tokens, LANES), F32), shape((tokens, LANES), F32),
    ]
    return call(
        functools.partial(attend_kernel, shards), "attend", outs, where,
        [x, seg, own, *vectors, *mine, *other],
        flops=2 * tokens * width * joined + 8 * QUERY_HEADS * tokens * tokens * LANES,
    )


def mix_kernel(shards, where, x, o, vec, own, *rest):
    n = shards - 1
    mine, other = rest[:n], rest[n : 2 * n]
    h_ref, n2_ref, w_ref = rest[2 * n :]
    place_rows(w_ref, where[0], where[1], own, mine, other)
    width = x.shape[1]
    h = x[...].astype(F32) + dot(o[...], w_ref[...])
    h_ref[...] = h
    root = lax.rsqrt(jnp.mean(h * h, axis=1, keepdims=True) + EPS)
    n2_ref[...] = (h * root * vec[1:2, :width]).astype(BF)


def mix(where, x, o, vec, own, mine, other, shards):
    tokens, width = x.shape
    outs = [shape(x.shape, F32), shape(x.shape), shape((width, width))]
    return call(
        functools.partial(mix_kernel, shards), "mix", outs, where,
        [x, o, vec, own, *mine, *other], flops=2 * tokens * width * width,
    )


def down_back_kernel(pieces, where, down, *rest):
    parts, (dact_ref, dy_ref) = rest[:pieces], rest[pieces:]
    tokens = parts[0].shape[0]
    for i in range(pieces):
        dy_ref[i * tokens : (i + 1) * tokens] = parts[i][...]
    slab = dact_ref.shape[1]
    w = down[rows_at(where[1] * slab, slab)]
    step = 2 * tokens

    @pl.loop(0, pieces // 2)
    def _(i):
        at = pl.ds(pl.multiple_of(i * step, step), step)
        dact_ref[at] = dot_t(dy_ref[at], w)


def down_back(where, down, parts, slab):
    tokens, width = parts[0].shape
    total = tokens * len(parts)
    outs = [shape((total, slab), F32), shape((total, width))]
    return call(
        functools.partial(down_back_kernel, len(parts)), "down_back", outs, where,
        [down, *parts], flops=2 * total * width * slab,
    )


def feed_kernel(shards, where, dact, dy, *rest):
    pieces = 2 * shards
    parts, rest = rest[:pieces], rest[pieces:]
    own, direct, passed = rest[0], rest[1:shards], rest[shards : 2 * shards - 1]
    rest = rest[2 * shards - 1 :]
    d1_ref, d2_ref, act_ref, dgate_ref, dup_ref, n_ref, wg_ref, wu_ref = rest
    s = where[0]
    tokens = parts[0].shape[0]
    rows = own.shape[0] // 2
    wg_ref[rows_at(s * rows, rows)] = own[:rows]
    wu_ref[rows_at(s * rows, rows)] = own[rows:]
    for parity, (first, second) in enumerate(((wg_ref, wu_ref), (wu_ref, wg_ref))):

        @pl.when((where[2] & 1) == parity)
        def _(first=first, second=second):
            for k in range(1, shards):
                at = rows_at((s ^ k) * rows, rows)
                first[at] = direct[k - 1][...]
                second[at] = passed[k - 1][...]

    for i in range(pieces):
        n_ref[i * tokens : (i + 1) * tokens] = parts[i][...]
    step = 2 * tokens

    @pl.loop(0, pieces // 2)
    def _(i):
        at = pl.ds(pl.multiple_of(i * step, step), step)
        block = n_ref[at]
        gate = dot(block, wg_ref[...])
        up = dot(block, wu_ref[...])
        sigma = jax.nn.sigmoid(gate)
        swish = gate * sigma
        act_ref[at] = (swish * up).astype(BF)
        da = dact[at]
        dgate_ref[at] = (da * up * sigma * (1.0 + gate * (1.0 - sigma))).astype(BF)
        dup_ref[at] = (da * swish).astype(BF)

    cut = d1_ref.shape[0]
    grad = t_dot(act_ref[...], dy[...])
    d1_ref[...] = grad[:cut].astype(BF)
    d2_ref[...] = grad[cut:].astype(BF)


def feed(where, dact, dy, parts, weights, shards):
    total, slab = dact.shape
    width = dy.shape[1]
    cut = slab // 32 * 16
    outs = [
        shape((cut, width)), shape((slab - cut, width)), shape((total, slab)),
        shape((total, slab)), shape((total, slab)), shape((total, width)),
        shape((width, slab)), shape((width, slab)),
    ]
    return call(
        functools.partial(feed_kernel, shards), "feed", outs, where,
        [dact, dy, *parts, *weights], flops=6 * total * width * slab,
    )


def wide_kernel(shards, where, n, dgate, dup, *rest):
    outs, acc = rest[:shards], rest[shards]
    rows = outs[0].shape[0] // 2
    s = where[0]
    acc[...] = t_dot(n[...], dgate[...])
    for k in range(shards):
        outs[k][:rows] = acc[rows_at((s ^ k) * rows, rows)].astype(BF)
    acc[...] = t_dot(n[...], dup[...])
    for k in range(shards):
        outs[k][rows:] = acc[rows_at((s ^ k) * rows, rows)].astype(BF)


def wide(where, n, dgate, dup, shards):
    total, width = n.shape
    slab = dgate.shape[1]
    outs = [shape((2 * width // shards, slab))] * shards
    return call(
        functools.partial(wide_kernel, shards), "wide", outs, where, [n, dgate, dup],
        [pltpu.VMEM((width, slab), F32)], flops=4 * total * width * slab,
    )


def lay_kernel(shards, where, *rest):
    mine, other = rest[:shards], rest[shards : 2 * shards]
    gate_ref, up_ref, stage = rest[2 * shards :]
    rows, slab = gate_ref.shape[0], stage.shape[2]
    s, c = where[0], where[1]
    for k in range(shards):
        stage[k] = mine[k][...]
        stage[shards + k] = other[k][...]
    for j in range(2 * shards):
        at = ((j // 2) ^ s) + jnp.where(c == j % 2, 0, shards)
        gate_ref[:, j * slab : (j + 1) * slab] = stage[at, :rows].astype(F32)
        up_ref[:, j * slab : (j + 1) * slab] = stage[at, rows:].astype(F32)


def lay(where, mine, other):
    shards = len(mine)
    rows, slab = mine[0].shape[0] // 2, mine[0].shape[1]
    outs = [shape((rows, 2 * shards * slab), F32)] * 2
    return call(
        functools.partial(lay_kernel, shards), "lay", outs, where, [*mine, *other],
        [pltpu.VMEM((2 * shards, 2 * rows, slab), BF)],
    )


def narrow_kernel(where, dgate, dup, wg, wu, keep, give):
    count = keep.shape[0]
    step = count // 2

    def block(i):
        at = pl.ds(pl.multiple_of(i * step, step), step)
        return dot_t(dgate[at], wg[...]) + dot_t(dup[at], wu[...])

    @pl.loop(0, 2)
    def _(i):
        give[pl.ds(pl.multiple_of(i * step, step), step)] = block(i + 2).astype(BF)

    @pl.loop(0, 2)
    def _(i):
        keep[pl.ds(pl.multiple_of(i * step, step), step)] = block(i)


def narrow(where, dgate, dup, wg, wu):
    total, slab = dgate.shape
    width = wg.shape[0]
    outs = [shape((total // 2, width), F32), shape((total // 2, width))]
    return call(
        narrow_kernel, "narrow", outs, where, [dgate, dup, wg, wu],
        flops=4 * total * width * slab,
    )


def back_kernel(shards, tall, where, *rest):
    dn, rest = rest[:shards], rest[shards:]
    hidden, ct, x, vec, wout, wqkv, mixed, n1, query, keys, values, probs, cos, sin = rest[:14]
    gt_ref, keep, give, da_ref, acc_q, acc_o, dob_ref = rest[14:]
    s, c = where[0], where[1]
    tokens, width = x.shape
    joined = wqkv.shape[1]
    rows = width // shards
    half = rows // 2
    cosine, sine = cos[...], sin[...]
    gain1, gain2 = vec[0:1, :width], vec[1:2, :width]

    dn2 = dn[0][...]
    for k in range(1, shards):
        dn2 = dn2 + dn[k][...].astype(F32)
    h = hidden[...]
    root = lax.rsqrt(jnp.mean(h * h, axis=1, keepdims=True) + EPS)
    g_norm2 = jnp.sum(dn2 * h * root, axis=0, keepdims=True)
    e = dn2 * gain2
    mean = jnp.mean(e * h, axis=1, keepdims=True)
    dh = ct[...].astype(F32) + root * e - h * (root * root * root * mean)
    dab = dh.astype(BF)
    gt_ref[...] = dh
    acc_o[...] = t_dot(mixed[...], dab)
    dob_ref[...] = dot_t(dab, wout[...]).astype(BF)

    key_kinds = [[k.astype(BF) for k in ks] for ks in lane_kinds(keys[...].astype(F32))]
    value_kinds = [[v.astype(BF) for v in vs] for vs in lane_kinds(values[...].astype(F32))]
    zero = jnp.zeros((tokens, LANES), F32)
    d_key = [[zero, zero], [zero, zero]]
    d_value = [[zero, zero], [zero, zero]]

    def turn_back(v):
        return v * cosine - swap_halves(v) * sine

    for i in range(PAIRS):
        q = query[:, i * LANES : (i + 1) * LANES]
        do = dob_ref[:, i * LANES : (i + 1) * LANES]
        dq = zero
        for side in range(2):
            head = 2 * i + side
            g = head // GROUP
            p = probs[head]
            dp = dot_t(do, value_kinds[g][side])
            d_value[g][side] = d_value[g][side] + t_dot(p.astype(BF), do)
            ds = (p * (dp - jnp.sum(p * dp, axis=-1, keepdims=True))).astype(BF)
            dq = dq + dot(ds, key_kinds[g][side])
            d_key[g][side] = d_key[g][side] + t_dot(ds, q)
        da_ref[:, i * LANES : (i + 1) * LANES] = turn_back(dq * SCALE).astype(BF)

    low = lax.broadcasted_iota(jnp.int32, (tokens, LANES), 1) < HEAD_SIZE

    def collect(parts):
        first = jnp.where(low, parts[0][0], parts[1][1])
        second = jnp.where(low, parts[1][0], parts[0][1])
        return first + pltpu.roll(second, HEAD_SIZE, 1)

    da_ref[:, width : width + LANES] = turn_back(collect(d_key) * SCALE).astype(BF)
    da_ref[:, width + LANES :] = collect(d_value).astype(BF)
    da = da_ref[...]
    acc_q[...] = t_dot(n1[...], da)
    g_bias = jnp.sum(da.astype(F32), axis=0, keepdims=True)
    dn1 = dot_t(da, wqkv[...])
    xf = x[...].astype(F32)
    root = lax.rsqrt(jnp.mean(xf * xf, axis=1, keepdims=True) + EPS)
    g_norm1 = jnp.sum(dn1 * xf * root, axis=0, keepdims=True)
    e = dn1 * gain1
    mean = jnp.mean(e * xf, axis=1, keepdims=True)
    gt_ref[...] = gt_ref[...] + root * e - xf * (root * root * root * mean)

    blank = jnp.zeros((5, LANES), F32)
    for target, side in ((keep, c), (give, 1 - c)):
        for k in range(shards):
            at = rows_at((s ^ k) * rows + side * half, half)
            for b in range(joined // LANES):
                lanes = slice(b * LANES, (b + 1) * LANES)
                base = b * (half + 8)
                target[k, base : base + half] = acc_q[at, lanes].astype(target.dtype)
                if (b + 1) * LANES <= width:
                    head = [g_norm1[:, lanes], g_norm2[:, lanes]]
                else:
                    head = [blank[:2]]
                tail = jnp.concatenate(head + [g_bias[:, lanes], blank], axis=0)
                target[k, base + half : base + half + 8] = tail.astype(target.dtype)
            for b in range(width // LANES):
                lanes = slice(b * LANES, (b + 1) * LANES)
                base = tall + b * half
                target[k, base : base + half] = acc_o[at, lanes].astype(target.dtype)


def layout_of(width, joined, rows):
    half = rows // 2
    tall = joined // LANES * (half + 8)
    return tall, tall + width // LANES * half


def down_kernel(where, act, down, keep, give):
    count = keep.shape[0]
    step = count // 2
    slab = act.shape[1]
    w = down[rows_at(where[1] * slab, slab)]

    @pl.loop(0, 2)
    def _(i):
        at = pl.multiple_of(i * step, step)
        give[pl.ds(at, step)] = dot(act[pl.ds(at + count, step)], w).astype(BF)
        keep[pl.ds(at, step)] = dot(act[pl.ds(at, step)], w)


def down_project(where, act, down):
    total, slab = act.shape
    width = down.shape[1]
    outs = [shape((total // 2, width), F32), shape((total // 2, width))]
    return call(
        down_kernel, "ydown", outs, where, [act, down], flops=2 * total * width * slab
    )


def pick_kernel(low, high, where, total, arrived, out):
    inside = (where[2] > low) & (where[2] < high)

    @pl.when(inside)
    def _():
        out[...] = total[...]

    @pl.when(jnp.logical_not(inside))
    def _():
        out[...] = arrived[...]


def pick(where, total, arrived, low, high):
    return call(
        functools.partial(pick_kernel, low, high), "pick", [shape(total.shape)], where,
        [total, arrived],
    )[0]


def stack_kernel(where, *rest):
    mine, other, out = rest[: len(rest) // 2], rest[len(rest) // 2 : -1], rest[-1]
    slab = out.shape[0] // 2
    for parts, side in ((mine, where[1]), (other, 1 - where[1])):
        start = side * slab
        for part in parts:
            out[rows_at(start, part.shape[0])] = part[...].astype(F32)
            start = start + part.shape[0]


def stack(where, mine, other):
    rows = 2 * sum(p.shape[0] for p in mine)
    outs = [shape((rows, mine[0].shape[1]), F32)]
    return call(stack_kernel, "stack", outs, where, [*mine, *other])[0]


def back(where, dn, hidden, ct, x, vec, wout, wqkv, mixed, n1, query, keys, values, probs, cos, sin):
    shards = len(dn)
    tokens, width = x.shape
    joined = wqkv.shape[1]
    tall, whole = layout_of(width, joined, width // shards)
    outs = [
        shape(x.shape, F32), shape((shards, whole, LANES), F32), shape((shards, whole, LANES)),
    ]
    return call(
        functools.partial(back_kernel, shards, tall), "back", outs, where,
        [*dn, hidden, ct, x, vec, wout, wqkv, mixed, n1, query, keys, values, probs, cos, sin],
        [
            pltpu.VMEM((tokens, joined), BF), pltpu.VMEM((width, joined), F32),
            pltpu.VMEM((width, width), F32), pltpu.VMEM((tokens, width), BF),
        ],
        flops=4 * tokens * width * (joined + width),
    )


def merge_kernel(shards, where, keep, arrived, *outs):
    for k in range(shards):
        total = keep[k] + arrived[k].astype(F32)
        outs[k][...] = total.astype(outs[k].dtype)


def merge(where, keep, arrived):
    shards = keep.shape[0]
    outs = [shape(keep.shape[1:], F32)] + [shape(keep.shape[1:])] * (shards - 1)
    return call(functools.partial(merge_kernel, shards), "merge", outs, where, [keep, arrived])


def finish_kernel(where, own, *rest):
    value = own[...]
    for piece in rest[:-1]:
        value = value + piece[...].astype(F32)
    rest[-1][...] = value.astype(BF)


def finish(where, parts):
    return call(finish_kernel, "finish", [shape(parts[0].shape)], where, parts)[0]


def close_kernel(tall, where, mine, other, qkv_ref, out_ref, vec_ref):
    c = where[1]
    half = qkv_ref.shape[0] // 2
    for source, side in ((mine, c), (other, 1 - c)):
        at = pl.ds(pl.multiple_of(side * half, 8), half)
        for b in range(qkv_ref.shape[1] // LANES):
            base = b * (half + 8)
            qkv_ref[at, b * LANES : (b + 1) * LANES] = source[base : base + half].astype(F32)
        for b in range(out_ref.shape[1] // LANES):
            base = tall + b * half
            out_ref[at, b * LANES : (b + 1) * LANES] = source[base : base + half].astype(F32)
    for b in range(qkv_ref.shape[1] // LANES):
        base = b * (half + 8) + half
        vec_ref[:, b * LANES : (b + 1) * LANES] = mine[base : base + 8].astype(F32)


def close(where, mine, other, rows, width, joined, tall):
    outs = [shape((rows, joined), F32), shape((rows, width), F32), shape((8, joined), F32)]
    return call(functools.partial(close_kernel, tall), "close", outs, where, [mine, other])


def body(
    tokens, seg_ids, norm1_gain, w_qkv, b_qkv, w_out, norm2_gain, w_gate, w_up, w_down, cotangent
):
    shards = lax.axis_size("shard")
    shard = lax.axis_index("shard")
    replica = lax.axis_index("replica")
    core = replica & 1
    where = jnp.stack([shard, core, replica >> 1]).astype(jnp.int32)
    count, width = tokens.shape
    rows = norm1_gain.shape[0]
    half_rows = rows // 2
    joined = w_qkv.shape[1]
    bias_rows = b_qkv.shape[0]
    slab = w_gate.shape[1] // (2 * shards)
    half = lax.dynamic_slice_in_dim(w_qkv, core * half_rows, half_rows, 0)
    qkv_mine = spread(half)[1:]
    vectors = [
        jnp.pad(v[None], ((0, 0), (0, joined - v.shape[0])))
        for v in (norm1_gain, norm2_gain, b_qkv)
    ]
    vectors = jnp.concatenate(vectors + [jnp.zeros((5, joined), BF)], axis=0)
    vectors = spread(vectors)
    qkv_other = [swap_core(p) for p in qkv_mine]
    out_mine = spread(lax.dynamic_slice_in_dim(w_out, core * half_rows, half_rows, 0))[1:]
    out_other = [swap_core(p) for p in out_mine]

    packed = pack(where, w_gate, w_up, shards)
    direct = [shard_swap(packed[k], k) for k in range(1, shards)]
    passed = [pair_swap(w) for w in direct]
    dy = spread(cotangent)
    dy = dy + [swap_core(p) for p in dy]

    n_one, query, keys, values, probs, mixed, wqkv, vec, cosine, sine = attend(
        where, tokens, seg_ids,
        w_qkv, vectors, qkv_mine, qkv_other, shards,
    )
    hidden, n_two, wout = mix(where, tokens, mixed, vec, w_out, out_mine, out_other, shards)
    n_parts = spread(n_two)
    n_parts = n_parts + [swap_core(p) for p in n_parts]

    dact, dy_all = down_back(where, w_down, dy, slab)
    down_one, down_two, act, d_gate, d_up, n_all, wgate, wup = feed(
        where, dact, dy_all, n_parts, [packed[0], *direct, *passed], shards
    )
    down_one, down_two = line_sum(where, down_one), line_sum(where, down_two)

    def plane_sum(keep, give):
        arrived = swap_core(give)
        total = keep + arrived.astype(F32)
        parts = [total[:count]]
        for k in range(1, shards):
            send = total[k * count : (k + 1) * count].astype(BF)
            parts.append(shard_swap(send, k))
        return parts

    dn = plane_sum(*narrow(where, d_gate, d_up, wgate, wup))

    grads = wide(where, n_all, d_gate, d_up, shards)
    grads = [grads[0]] + [shard_swap(grads[k], k) for k in range(1, shards)]
    grads = [line_sum(where, g) for g in grads]
    gate_part, up_part = lay(where, grads, [swap_core(g) for g in grads])

    down_part = stack(where, [down_one, down_two], [swap_core(down_one), swap_core(down_two)])
    y = plane_sum(*down_project(where, act, w_down))
    layer_out = call(finish_kernel, "yout", [shape(hidden.shape)], where, [hidden, *y])[0]

    grad_tokens, keep, give = back(
        where, dn, hidden, cotangent, tokens, vec, wout, wqkv, mixed, n_one, query, keys, values,
        probs, cosine, sine,
    )
    parts = merge(where, keep, swap_core(give))
    parts = [parts[0]] + [shard_swap(parts[k], k) for k in range(1, shards)]
    tall, _ = layout_of(width, joined, rows)
    item = line_sum(where, finish(where, parts))
    qkv_part, out_part, vec_grads = close(where, item, swap_core(item), rows, width, joined, tall)
    one_part = lax.dynamic_slice(vec_grads[0], (shard * rows,), (rows,))
    two_part = lax.dynamic_slice(vec_grads[1], (shard * rows,), (rows,))
    bias_part = lax.dynamic_slice(vec_grads[2], (shard * bias_rows,), (bias_rows,))
    return (
        layer_out,
        grad_tokens,
        one_part,
        qkv_part,
        bias_part,
        out_part,
        two_part,
        gate_part,
        up_part,
        down_part,
    )


def solution(mesh):
    split = P(("shard", "replica"), None)
    matrix = P("shard", None)
    vector = P("shard")
    in_specs = (
        split, split, vector, matrix, vector, matrix, vector, matrix, matrix, matrix, split,
    )
    out_specs = (split, split, vector, matrix, vector, matrix, vector, matrix, matrix, matrix)
    return jax.shard_map(body, mesh=mesh, in_specs=in_specs, out_specs=out_specs, check_vma=False)
```

```python
import functools
import math
import jax
import jax.numpy as jnp
from jax import lax
from jax.experimental import pallas as pl
from jax.experimental.pallas import tpu as pltpu
from jax.sharding import PartitionSpec as P


QUERY_HEADS = 14
KEY_VALUE_HEADS = 2
HEAD_SIZE = 64
HALF = HEAD_SIZE // 2
GROUP = QUERY_HEADS // KEY_VALUE_HEADS
PAIRS = QUERY_HEADS // 2
LANES = 128

EPS = 1e-06
THETA = 1000000.0
SCALE = HEAD_SIZE ** (-0.5)
BF = jnp.bfloat16
F32 = jnp.float32


def swap_core(x):
    n = lax.axis_size("replica")
    return lax.ppermute(x, "replica", [(i, i ^ 1) for i in range(n)])


def shard_swap(x, k):
    n = lax.axis_size("shard")
    return lax.ppermute(x, "shard", [(i, i ^ k) for i in range(n)])


def pair_swap(x):
    n = lax.axis_size("replica")
    return lax.ppermute(x, "replica", [(i, i ^ 2) for i in range(n)])


def spread(x):
    return [x] + [shard_swap(x, k) for k in range(1, lax.axis_size("shard"))]


def line_sum(where, x):
    line = lax.axis_size("replica") // 2
    half = line // 2

    def hop(value, chips):
        links = [(2 * a + k, 2 * b + k) for a, b in chips for k in range(2)]
        return lax.ppermute(value, "replica", links)

    total = x
    for i in range(half - 1):
        arrived = hop(total, [(i, i + 1), (line - 1 - i, line - 2 - i)])
        total = total + arrived
    arrived = hop(total, [(half - 1, half), (half, half - 1)])
    total = total + arrived
    for i in reversed(range(half - 1)):
        arrived = hop(total, [(i + 1, i), (line - 2 - i, line - 1 - i)])
        total = pick(where, total, arrived, i, line - 1 - i)
    return total


def dot(a, b):
    return jnp.dot(a, b, preferred_element_type=F32)


def dot_t(a, b):
    return lax.dot_general(a, b, (((1,), (1,)), ((), ())), preferred_element_type=F32)


def t_dot(a, b):
    return lax.dot_general(a, b, (((0,), (0,)), ((), ())), preferred_element_type=F32)


GRANTS = {'pack': 12, 'attend': 3, 'mix': 4, 'down_back': 5, 'feed': 9, 'narrow': 4, 'back': 18, 'wide': 8, 'merge': 5, 'finish': 4, 'lay': 18, 'close': 6, 'ydown': 4, 'open': 3, 'yout': 4, 'pick': 4, 'stack': 8}


def call(kernel, name, outs, where, args, scratch=(), flops=0, space=pltpu.VMEM):
    grant = GRANTS[name]
    total = sum(a.size * a.dtype.itemsize for a in args)
    total += sum(o.size * jnp.dtype(o.dtype).itemsize for o in outs)
    vmem = pl.BlockSpec(memory_space=pltpu.VMEM)
    return pl.pallas_call(
        kernel,
        out_shape=outs,
        in_specs=[pl.BlockSpec(memory_space=pltpu.SMEM)] + [pl.BlockSpec(memory_space=space)] * len(args),
        out_specs=[vmem] * len(outs),
        scratch_shapes=list(scratch),
        cost_estimate=pl.CostEstimate(flops=flops, bytes_accessed=total, transcendentals=0),
        compiler_params=pltpu.CompilerParams(vmem_limit_bytes=grant << 20),
    )(where, *args)


def shape(dims, dtype=BF):
    return jax.ShapeDtypeStruct(dims, dtype)


def rows_at(start, size):
    return pl.ds(pl.multiple_of(start, 8 if size % 16 else 16), size)


def pack_kernel(shards, where, gate, up, *rest):
    outs, (stage, gate_buf, up_buf, sems) = rest[:shards], rest[shards:]
    rows, slab = gate.shape[0], stage.shape[3]
    step = rows // 2
    s, c = where[0], where[1]
    copies = []
    for i in range(2):
        at = pl.ds(i * step, step)
        for m, (src, dst) in enumerate(((gate, gate_buf), (up, up_buf))):
            copy = pltpu.make_async_copy(src.at[at], dst.at[at], sems.at[i, m])
            copy.start()
            copies.append(copy)
    for i in range(2):
        for m, buf in enumerate((gate_buf, up_buf)):
            copies[2 * i + m].wait()
            for j in range(2 * shards):

                @pl.when(c == j % 2)
                def _(i=i, j=j, m=m, buf=buf):
                    at = slice(i * step, (i + 1) * step)
                    stage[(j // 2) ^ s, m, at] = buf[at, j * slab : (j + 1) * slab]

    outs[0][:rows] = stage[0, 0]
    outs[0][rows:] = stage[0, 1]
    for k in range(1, shards):
        outs[k][...] = stage[k, where[2] & 1]


def pack(where, gate, up, shards):
    rows, ff = gate.shape
    slab = ff // (2 * shards)
    outs = [shape((2 * rows, slab))] + [shape((rows, slab))] * (shards - 1)
    return call(
        functools.partial(pack_kernel, shards), "pack", outs, where, [gate, up],
        [
            pltpu.VMEM((shards, 2, rows, slab), BF), pltpu.VMEM((rows, ff), BF),
            pltpu.VMEM((rows, ff), BF), pltpu.SemaphoreType.DMA((2, 2)),
        ],
        space=pltpu.HBM,
    )


def open_kernel(where, w, g1, g2, b, block, extra):
    half = w.shape[0] // 2
    width = w.shape[1]
    block[:half] = w[rows_at(where[1] * half, half)]
    line = lax.broadcasted_iota(jnp.int32, extra.shape, 0)
    value = jnp.zeros(extra.shape, F32)
    for i, ref in enumerate((g1, g2, b)):
        row = ref[...].astype(F32)[None]
        row = jnp.concatenate([row, jnp.zeros((1, width - row.shape[1]), F32)], axis=1)
        value = jnp.where(line == i, row, value)
    extra[...] = value.astype(BF)
    block[half:] = value.astype(BF)


def open_rows(where, w, g1, g2, b):
    half, width = w.shape[0] // 2, w.shape[1]
    return call(
        open_kernel, "open", [shape((half + 8, width)), shape((8, width))], where, [w, g1, g2, b]
    )


def place_rows(dst, s, c, own, mine, other):
    rows = own.shape[0]
    half = rows // 2
    dst[rows_at(s * rows, rows)] = own[...]
    for k in range(1, len(mine) + 1):
        base = (s ^ k) * rows
        dst[rows_at(base + c * half, half)] = mine[k - 1][:half]
        dst[rows_at(base + (1 - c) * half, half)] = other[k - 1][:half]


def lane_kinds(x):
    lane = lax.broadcasted_iota(jnp.int32, x.shape, 1)
    low = lane < HEAD_SIZE
    zero = jnp.zeros_like(x)
    turned = pltpu.roll(x, HEAD_SIZE, 1)
    return [
        [jnp.where(low, x, zero), jnp.where(low, zero, turned)],
        [jnp.where(low, turned, zero), jnp.where(low, zero, x)],
    ]


def swap_halves(x):
    lane = lax.broadcasted_iota(jnp.int32, x.shape, 1)
    first = (lane % HEAD_SIZE) < HALF
    return jnp.where(first, pltpu.roll(x, LANES - HALF, 1), pltpu.roll(x, HALF, 1))


def attend_kernel(shards, where, x, seg, own, extra, *rest):
    n = shards - 1
    riders, mine, other = rest[:n], rest[n : 2 * n], rest[2 * n : 3 * n]
    n1_ref, q_ref, k_ref, v_ref, p_ref, o_ref, w_ref, vec_ref, cos_ref, sin_ref = rest[3 * n :]
    s, c = where[0], where[1]
    width, joined_width = x.shape[1], own.shape[1]
    place_rows(w_ref, s, c, own, mine, other)
    lines = extra.shape[0]
    is_gain = lax.broadcasted_iota(jnp.int32, vec_ref.shape, 0) < 2
    vec = jnp.zeros(vec_ref.shape, F32)
    gap = jnp.zeros((lines, joined_width - width), F32)
    for k, piece in enumerate((extra,) + tuple(riders)):
        value = piece[piece.shape[0] - lines :].astype(F32)
        value = jnp.concatenate([value, gap], axis=1)
        gains = pltpu.roll(value, (s ^ k) * (width // shards), 1)
        biases = pltpu.roll(value, (s ^ k) * (joined_width // shards), 1)
        vec = vec + jnp.where(is_gain, gains, biases)
    vec_ref[...] = vec
    xf = x[...].astype(F32)
    root = lax.rsqrt(jnp.mean(xf * xf, axis=1, keepdims=True) + EPS)
    n1 = (xf * root * vec[0:1, :width]).astype(BF)
    n1_ref[...] = n1
    joined = dot(n1, w_ref[...]) + vec[2:3]
    tokens = x.shape[0]
    square = (tokens, LANES)
    down = lax.broadcasted_iota(jnp.int32, square, 0)
    along = lax.broadcasted_iota(jnp.int32, square, 1)
    of_key = jnp.broadcast_to(seg[...], square).astype(F32)
    of_query = of_key.T
    allowed = (along <= down) & (of_key == of_query)
    before = jnp.where(of_key < of_query, 1.0, 0.0)
    position = down.astype(F32) - jnp.sum(before, axis=1, keepdims=True)
    power = (along % HALF).astype(F32) * (2.0 / HEAD_SIZE)
    angle = position * jnp.exp(power * -math.log(THETA))
    cosine = jnp.cos(angle)
    sine = jnp.sin(angle)
    sine = jnp.where((along % HEAD_SIZE) < HALF, -sine, sine)
    cos_ref[...] = cosine
    sin_ref[...] = sine

    def turn(v):
        return v * cosine + swap_halves(v) * sine

    keys = turn(joined[:, width : width + LANES])
    values = joined[:, width + LANES : width + 2 * LANES]
    keys_low = keys.astype(BF)
    values_low = values.astype(BF)
    k_ref[...] = keys_low
    v_ref[...] = values_low
    key_kinds = lane_kinds(keys_low.astype(F32))
    value_kinds = lane_kinds(values_low.astype(F32))
    key_kinds = [[k.astype(BF) for k in ks] for ks in key_kinds]
    value_kinds = [[v.astype(BF) for v in vs] for vs in value_kinds]
    for i in range(PAIRS):
        q = turn(joined[:, i * LANES : (i + 1) * LANES]).astype(BF)
        q_ref[:, i * LANES : (i + 1) * LANES] = q
        mixed = jnp.zeros(q.shape, F32)
        for side in range(2):
            h = 2 * i + side
            g = h // GROUP
            scores = dot_t(q, key_kinds[g][side]) * SCALE
            scores = jnp.where(allowed, scores, -1e30)
            top = jnp.max(scores, axis=-1, keepdims=True)
            e = jnp.exp(scores - top)
            p = e / jnp.sum(e, axis=-1, keepdims=True)
            p_ref[h] = p
            mixed = mixed + dot(p.astype(BF), value_kinds[g][side])
        o_ref[:, i * LANES : (i + 1) * LANES] = mixed.astype(BF)


def attend(where, x, seg, own, extra, riders, mine, other, shards):
    tokens, width = x.shape
    joined = own.shape[1]
    outs = [
        shape((tokens, width)), shape((tokens, width)), shape((tokens, LANES)),
        shape((tokens, LANES)), shape((QUERY_HEADS, tokens, tokens), F32),
        shape((tokens, width)), shape((width, joined)), shape((extra.shape[0], joined), F32),
        shape((tokens, LANES), F32), shape((tokens, LANES), F32),
    ]
    return call(
        functools.partial(attend_kernel, shards), "attend", outs, where,
        [x, seg, own, extra, *riders, *mine, *other],
        flops=2 * tokens * width * joined + 8 * QUERY_HEADS * tokens * tokens * LANES,
    )


def mix_kernel(shards, where, x, o, vec, own, *rest):
    n = shards - 1
    mine, other = rest[:n], rest[n : 2 * n]
    h_ref, n2_ref, w_ref = rest[2 * n :]
    place_rows(w_ref, where[0], where[1], own, mine, other)
    width = x.shape[1]
    h = x[...].astype(F32) + dot(o[...], w_ref[...])
    h_ref[...] = h
    root = lax.rsqrt(jnp.mean(h * h, axis=1, keepdims=True) + EPS)
    n2_ref[...] = (h * root * vec[1:2, :width]).astype(BF)


def mix(where, x, o, vec, own, mine, other, shards):
    tokens, width = x.shape
    outs = [shape(x.shape, F32), shape(x.shape), shape((width, width))]
    return call(
        functools.partial(mix_kernel, shards), "mix", outs, where,
        [x, o, vec, own, *mine, *other], flops=2 * tokens * width * width,
    )


def down_back_kernel(pieces, where, down, *rest):
    parts, (dact_ref, dy_ref) = rest[:pieces], rest[pieces:]
    tokens = parts[0].shape[0]
    for i in range(pieces):
        dy_ref[i * tokens : (i + 1) * tokens] = parts[i][...]
    slab = dact_ref.shape[1]
    w = down[rows_at(where[1] * slab, slab)]
    step = 2 * tokens

    @pl.loop(0, pieces // 2)
    def _(i):
        at = pl.ds(pl.multiple_of(i * step, step), step)
        dact_ref[at] = dot_t(dy_ref[at], w)


def down_back(where, down, parts, slab):
    tokens, width = parts[0].shape
    total = tokens * len(parts)
    outs = [shape((total, slab), F32), shape((total, width))]
    return call(
        functools.partial(down_back_kernel, len(parts)), "down_back", outs, where,
        [down, *parts], flops=2 * total * width * slab,
    )


def feed_kernel(shards, where, dact, dy, *rest):
    pieces = 2 * shards
    parts, rest = rest[:pieces], rest[pieces:]
    own, direct, passed = rest[0], rest[1:shards], rest[shards : 2 * shards - 1]
    rest = rest[2 * shards - 1 :]
    d1_ref, d2_ref, act_ref, dgate_ref, dup_ref, n_ref, wg_ref, wu_ref = rest
    s = where[0]
    tokens = parts[0].shape[0]
    rows = own.shape[0] // 2
    wg_ref[rows_at(s * rows, rows)] = own[:rows]
    wu_ref[rows_at(s * rows, rows)] = own[rows:]
    for parity, (first, second) in enumerate(((wg_ref, wu_ref), (wu_ref, wg_ref))):

        @pl.when((where[2] & 1) == parity)
        def _(first=first, second=second):
            for k in range(1, shards):
                at = rows_at((s ^ k) * rows, rows)
                first[at] = direct[k - 1][...]
                second[at] = passed[k - 1][...]

    for i in range(pieces):
        n_ref[i * tokens : (i + 1) * tokens] = parts[i][...]
    step = 2 * tokens

    @pl.loop(0, pieces // 2)
    def _(i):
        at = pl.ds(pl.multiple_of(i * step, step), step)
        block = n_ref[at]
        gate = dot(block, wg_ref[...])
        up = dot(block, wu_ref[...])
        sigma = jax.nn.sigmoid(gate)
        swish = gate * sigma
        act_ref[at] = (swish * up).astype(BF)
        da = dact[at]
        dgate_ref[at] = (da * up * sigma * (1.0 + gate * (1.0 - sigma))).astype(BF)
        dup_ref[at] = (da * swish).astype(BF)

    cut = d1_ref.shape[0]
    grad = t_dot(act_ref[...], dy[...])
    d1_ref[...] = grad[:cut].astype(BF)
    d2_ref[...] = grad[cut:].astype(BF)


def feed(where, dact, dy, parts, weights, shards):
    total, slab = dact.shape
    width = dy.shape[1]
    cut = slab // 32 * 16
    outs = [
        shape((cut, width)), shape((slab - cut, width)), shape((total, slab)),
        shape((total, slab)), shape((total, slab)), shape((total, width)),
        shape((width, slab)), shape((width, slab)),
    ]
    return call(
        functools.partial(feed_kernel, shards), "feed", outs, where,
        [dact, dy, *parts, *weights], flops=6 * total * width * slab,
    )


def wide_kernel(shards, where, n, dgate, dup, *rest):
    outs, acc = rest[:shards], rest[shards]
    rows = outs[0].shape[0] // 2
    s = where[0]
    acc[...] = t_dot(n[...], dgate[...])
    for k in range(shards):
        outs[k][:rows] = acc[rows_at((s ^ k) * rows, rows)].astype(BF)
    acc[...] = t_dot(n[...], dup[...])
    for k in range(shards):
        outs[k][rows:] = acc[rows_at((s ^ k) * rows, rows)].astype(BF)


def wide(where, n, dgate, dup, shards):
    total, width = n.shape
    slab = dgate.shape[1]
    outs = [shape((2 * width // shards, slab))] * shards
    return call(
        functools.partial(wide_kernel, shards), "wide", outs, where, [n, dgate, dup],
        [pltpu.VMEM((width, slab), F32)], flops=4 * total * width * slab,
    )


def lay_kernel(shards, where, *rest):
    mine, other = rest[:shards], rest[shards : 2 * shards]
    gate_ref, up_ref, stage = rest[2 * shards :]
    rows, slab = gate_ref.shape[0], stage.shape[2]
    s, c = where[0], where[1]
    for k in range(shards):
        stage[k] = mine[k][...]
        stage[shards + k] = other[k][...]
    for j in range(2 * shards):
        at = ((j // 2) ^ s) + jnp.where(c == j % 2, 0, shards)
        gate_ref[:, j * slab : (j + 1) * slab] = stage[at, :rows].astype(F32)
        up_ref[:, j * slab : (j + 1) * slab] = stage[at, rows:].astype(F32)


def lay(where, mine, other):
    shards = len(mine)
    rows, slab = mine[0].shape[0] // 2, mine[0].shape[1]
    outs = [shape((rows, 2 * shards * slab), F32)] * 2
    return call(
        functools.partial(lay_kernel, shards), "lay", outs, where, [*mine, *other],
        [pltpu.VMEM((2 * shards, 2 * rows, slab), BF)],
    )


def narrow_kernel(where, dgate, dup, wg, wu, keep, give):
    count = keep.shape[0]
    step = count // 2

    def block(i):
        at = pl.ds(pl.multiple_of(i * step, step), step)
        return dot_t(dgate[at], wg[...]) + dot_t(dup[at], wu[...])

    @pl.loop(0, 2)
    def _(i):
        give[pl.ds(pl.multiple_of(i * step, step), step)] = block(i + 2).astype(BF)

    @pl.loop(0, 2)
    def _(i):
        keep[pl.ds(pl.multiple_of(i * step, step), step)] = block(i)


def narrow(where, dgate, dup, wg, wu):
    total, slab = dgate.shape
    width = wg.shape[0]
    outs = [shape((total // 2, width), F32), shape((total // 2, width))]
    return call(
        narrow_kernel, "narrow", outs, where, [dgate, dup, wg, wu],
        flops=4 * total * width * slab,
    )


def back_kernel(shards, tall, where, *rest):
    dn, rest = rest[:shards], rest[shards:]
    hidden, ct, x, vec, wout, wqkv, mixed, n1, query, keys, values, probs, cos, sin = rest[:14]
    gt_ref, keep, give, da_ref, acc_q, acc_o, dob_ref = rest[14:]
    s, c = where[0], where[1]
    tokens, width = x.shape
    joined = wqkv.shape[1]
    rows = width // shards
    half = rows // 2
    cosine, sine = cos[...], sin[...]
    gain1, gain2 = vec[0:1, :width], vec[1:2, :width]

    dn2 = dn[0][...]
    for k in range(1, shards):
        dn2 = dn2 + dn[k][...].astype(F32)
    h = hidden[...]
    root = lax.rsqrt(jnp.mean(h * h, axis=1, keepdims=True) + EPS)
    g_norm2 = jnp.sum(dn2 * h * root, axis=0, keepdims=True)
    e = dn2 * gain2
    mean = jnp.mean(e * h, axis=1, keepdims=True)
    dh = ct[...].astype(F32) + root * e - h * (root * root * root * mean)
    dab = dh.astype(BF)
    gt_ref[...] = dh
    acc_o[...] = t_dot(mixed[...], dab)
    dob_ref[...] = dot_t(dab, wout[...]).astype(BF)

    key_kinds = [[k.astype(BF) for k in ks] for ks in lane_kinds(keys[...].astype(F32))]
    value_kinds = [[v.astype(BF) for v in vs] for vs in lane_kinds(values[...].astype(F32))]
    zero = jnp.zeros((tokens, LANES), F32)
    d_key = [[zero, zero], [zero, zero]]
    d_value = [[zero, zero], [zero, zero]]

    def turn_back(v):
        return v * cosine - swap_halves(v) * sine

    for i in range(PAIRS):
        q = query[:, i * LANES : (i + 1) * LANES]
        do = dob_ref[:, i * LANES : (i + 1) * LANES]
        dq = zero
        for side in range(2):
            head = 2 * i + side
            g = head // GROUP
            p = probs[head]
            dp = dot_t(do, value_kinds[g][side])
            d_value[g][side] = d_value[g][side] + t_dot(p.astype(BF), do)
            ds = (p * (dp - jnp.sum(p * dp, axis=-1, keepdims=True))).astype(BF)
            dq = dq + dot(ds, key_kinds[g][side])
            d_key[g][side] = d_key[g][side] + t_dot(ds, q)
        da_ref[:, i * LANES : (i + 1) * LANES] = turn_back(dq * SCALE).astype(BF)

    low = lax.broadcasted_iota(jnp.int32, (tokens, LANES), 1) < HEAD_SIZE

    def collect(parts):
        first = jnp.where(low, parts[0][0], parts[1][1])
        second = jnp.where(low, parts[1][0], parts[0][1])
        return first + pltpu.roll(second, HEAD_SIZE, 1)

    da_ref[:, width : width + LANES] = turn_back(collect(d_key) * SCALE).astype(BF)
    da_ref[:, width + LANES :] = collect(d_value).astype(BF)
    da = da_ref[...]
    acc_q[...] = t_dot(n1[...], da)
    g_bias = jnp.sum(da.astype(F32), axis=0, keepdims=True)
    dn1 = dot_t(da, wqkv[...])
    xf = x[...].astype(F32)
    root = lax.rsqrt(jnp.mean(xf * xf, axis=1, keepdims=True) + EPS)
    g_norm1 = jnp.sum(dn1 * xf * root, axis=0, keepdims=True)
    e = dn1 * gain1
    mean = jnp.mean(e * xf, axis=1, keepdims=True)
    gt_ref[...] = gt_ref[...] + root * e - xf * (root * root * root * mean)

    blank = jnp.zeros((5, LANES), F32)
    for target, side in ((keep, c), (give, 1 - c)):
        for k in range(shards):
            at = rows_at((s ^ k) * rows + side * half, half)
            for b in range(joined // LANES):
                lanes = slice(b * LANES, (b + 1) * LANES)
                base = b * (half + 8)
                target[k, base : base + half] = acc_q[at, lanes].astype(target.dtype)
                if (b + 1) * LANES <= width:
                    head = [g_norm1[:, lanes], g_norm2[:, lanes]]
                else:
                    head = [blank[:2]]
                tail = jnp.concatenate(head + [g_bias[:, lanes], blank], axis=0)
                target[k, base + half : base + half + 8] = tail.astype(target.dtype)
            for b in range(width // LANES):
                lanes = slice(b * LANES, (b + 1) * LANES)
                base = tall + b * half
                target[k, base : base + half] = acc_o[at, lanes].astype(target.dtype)


def layout_of(width, joined, rows):
    half = rows // 2
    tall = joined // LANES * (half + 8)
    return tall, tall + width // LANES * half


def down_kernel(where, act, down, keep, give):
    count = keep.shape[0]
    step = count // 2
    slab = act.shape[1]
    w = down[rows_at(where[1] * slab, slab)]

    @pl.loop(0, 2)
    def _(i):
        at = pl.multiple_of(i * step, step)
        give[pl.ds(at, step)] = dot(act[pl.ds(at + count, step)], w).astype(BF)
        keep[pl.ds(at, step)] = dot(act[pl.ds(at, step)], w)


def down_project(where, act, down):
    total, slab = act.shape
    width = down.shape[1]
    outs = [shape((total // 2, width), F32), shape((total // 2, width))]
    return call(
        down_kernel, "ydown", outs, where, [act, down], flops=2 * total * width * slab
    )


def pick_kernel(low, high, where, total, arrived, out):
    inside = (where[2] > low) & (where[2] < high)

    @pl.when(inside)
    def _():
        out[...] = total[...]

    @pl.when(jnp.logical_not(inside))
    def _():
        out[...] = arrived[...]


def pick(where, total, arrived, low, high):
    return call(
        functools.partial(pick_kernel, low, high), "pick", [shape(total.shape)], where,
        [total, arrived],
    )[0]


def stack_kernel(where, *rest):
    mine, other, out = rest[: len(rest) // 2], rest[len(rest) // 2 : -1], rest[-1]
    slab = out.shape[0] // 2
    for parts, side in ((mine, where[1]), (other, 1 - where[1])):
        start = side * slab
        for part in parts:
            out[rows_at(start, part.shape[0])] = part[...].astype(F32)
            start = start + part.shape[0]


def stack(where, mine, other):
    rows = 2 * sum(p.shape[0] for p in mine)
    outs = [shape((rows, mine[0].shape[1]), F32)]
    return call(stack_kernel, "stack", outs, where, [*mine, *other])[0]


def back(where, dn, hidden, ct, x, vec, wout, wqkv, mixed, n1, query, keys, values, probs, cos, sin):
    shards = len(dn)
    tokens, width = x.shape
    joined = wqkv.shape[1]
    tall, whole = layout_of(width, joined, width // shards)
    outs = [
        shape(x.shape, F32), shape((shards, whole, LANES), F32), shape((shards, whole, LANES)),
    ]
    return call(
        functools.partial(back_kernel, shards, tall), "back", outs, where,
        [*dn, hidden, ct, x, vec, wout, wqkv, mixed, n1, query, keys, values, probs, cos, sin],
        [
            pltpu.VMEM((tokens, joined), BF), pltpu.VMEM((width, joined), F32),
            pltpu.VMEM((width, width), F32), pltpu.VMEM((tokens, width), BF),
        ],
        flops=4 * tokens * width * (joined + width),
    )


def merge_kernel(shards, where, keep, arrived, *outs):
    for k in range(shards):
        total = keep[k] + arrived[k].astype(F32)
        outs[k][...] = total.astype(outs[k].dtype)


def merge(where, keep, arrived):
    shards = keep.shape[0]
    outs = [shape(keep.shape[1:], F32)] + [shape(keep.shape[1:])] * (shards - 1)
    return call(functools.partial(merge_kernel, shards), "merge", outs, where, [keep, arrived])


def finish_kernel(where, own, *rest):
    value = own[...]
    for piece in rest[:-1]:
        value = value + piece[...].astype(F32)
    rest[-1][...] = value.astype(BF)


def finish(where, parts):
    return call(finish_kernel, "finish", [shape(parts[0].shape)], where, parts)[0]


def close_kernel(tall, where, mine, other, qkv_ref, out_ref, vec_ref):
    c = where[1]
    half = qkv_ref.shape[0] // 2
    for source, side in ((mine, c), (other, 1 - c)):
        at = pl.ds(pl.multiple_of(side * half, 8), half)
        for b in range(qkv_ref.shape[1] // LANES):
            base = b * (half + 8)
            qkv_ref[at, b * LANES : (b + 1) * LANES] = source[base : base + half].astype(F32)
        for b in range(out_ref.shape[1] // LANES):
            base = tall + b * half
            out_ref[at, b * LANES : (b + 1) * LANES] = source[base : base + half].astype(F32)
    for b in range(qkv_ref.shape[1] // LANES):
        base = b * (half + 8) + half
        vec_ref[:, b * LANES : (b + 1) * LANES] = mine[base : base + 8].astype(F32)


def close(where, mine, other, rows, width, joined, tall):
    outs = [shape((rows, joined), F32), shape((rows, width), F32), shape((8, joined), F32)]
    return call(functools.partial(close_kernel, tall), "close", outs, where, [mine, other])


def body(
    tokens, seg_ids, norm1_gain, w_qkv, b_qkv, w_out, norm2_gain, w_gate, w_up, w_down, cotangent
):
    shards = lax.axis_size("shard")
    shard = lax.axis_index("shard")
    replica = lax.axis_index("replica")
    core = replica & 1
    where = jnp.stack([shard, core, replica >> 1]).astype(jnp.int32)
    _, width = tokens.shape
    rows = norm1_gain.shape[0]
    half_rows = rows // 2
    joined = w_qkv.shape[1]
    bias_rows = b_qkv.shape[0]
    slab = w_gate.shape[1] // (2 * shards)
    half = lax.dynamic_slice_in_dim(w_qkv, core * half_rows, half_rows, 0)
    qkv_mine = spread(half)[1:]
    qkv_other = [swap_core(p) for p in qkv_mine]
    out_block, extra = open_rows(where, w_out, norm1_gain, norm2_gain, b_qkv)
    out_mine = spread(out_block)[1:]
    out_other = [swap_core(p) for p in out_mine]

    packed = pack(
        where, *(pltpu.with_memory_space_constraint(w, pltpu.HBM) for w in (w_gate, w_up)), shards
    )
    direct = [shard_swap(packed[k], k) for k in range(1, shards)]
    passed = [pair_swap(w) for w in direct]
    dy = spread(cotangent)
    dy = dy + [swap_core(p) for p in dy]

    n_one, query, keys, values, probs, mixed, wqkv, vec, cosine, sine = attend(
        where, tokens, seg_ids,
        w_qkv, extra, out_mine, qkv_mine, qkv_other, shards,
    )
    hidden, n_two, wout = mix(where, tokens, mixed, vec, w_out, out_mine, out_other, shards)
    n_parts = spread(n_two)
    n_parts = n_parts + [swap_core(p) for p in n_parts]

    dact, dy_all = down_back(where, w_down, dy, slab)
    down_one, down_two, act, d_gate, d_up, n_all, wgate, wup = feed(
        where, dact, dy_all, n_parts, [packed[0], *direct, *passed], shards
    )
    down_one, down_two = line_sum(where, down_one), line_sum(where, down_two)

    def plane_sum(keep, give):
        arrived = swap_core(give)
        parts = (shards, -1, keep.shape[-1])
        total = merge(where, keep.reshape(parts), arrived.reshape(parts))
        return [total[0]] + [shard_swap(total[k], k) for k in range(1, shards)]

    dn = plane_sum(*narrow(where, d_gate, d_up, wgate, wup))

    grads = wide(where, n_all, d_gate, d_up, shards)
    grads = [grads[0]] + [shard_swap(grads[k], k) for k in range(1, shards)]
    grads = [line_sum(where, g) for g in grads]
    gate_part, up_part = lay(where, grads, [swap_core(g) for g in grads])

    down_part = stack(where, [down_one, down_two], [swap_core(down_one), swap_core(down_two)])
    y = plane_sum(*down_project(where, act, w_down))
    layer_out = call(finish_kernel, "yout", [shape(hidden.shape)], where, [hidden, *y])[0]

    grad_tokens, keep, give = back(
        where, dn, hidden, cotangent, tokens, vec, wout, wqkv, mixed, n_one, query, keys, values,
        probs, cosine, sine,
    )
    parts = plane_sum(keep, give)
    tall, _ = layout_of(width, joined, rows)
    item = line_sum(where, finish(where, parts))
    qkv_part, out_part, vec_grads = close(where, item, swap_core(item), rows, width, joined, tall)
    one_part = lax.dynamic_slice(vec_grads[0], (shard * rows,), (rows,))
    two_part = lax.dynamic_slice(vec_grads[1], (shard * rows,), (rows,))
    bias_part = lax.dynamic_slice(vec_grads[2], (shard * bias_rows,), (bias_rows,))
    return (
        layer_out,
        grad_tokens,
        one_part,
        qkv_part,
        bias_part,
        out_part,
        two_part,
        gate_part,
        up_part,
        down_part,
    )


def solution(mesh):
    split = P(("shard", "replica"), None)
    matrix = P("shard", None)
    vector = P("shard")
    in_specs = (
        split, split, vector, matrix, vector, matrix, vector, matrix, matrix, matrix, split,
    )
    out_specs = (split, split, vector, matrix, vector, matrix, vector, matrix, matrix, matrix)
    return jax.shard_map(body, mesh=mesh, in_specs=in_specs, out_specs=out_specs, check_vma=False)
```

```python
import functools
import math
import jax
import jax.numpy as jnp
from jax import lax
from jax.experimental import pallas as pl
from jax.experimental.pallas import tpu as pltpu
from jax.sharding import PartitionSpec as P


QUERY_HEADS = 14
KEY_VALUE_HEADS = 2
HEAD_SIZE = 64
HALF = HEAD_SIZE // 2
GROUP = QUERY_HEADS // KEY_VALUE_HEADS
PAIRS = QUERY_HEADS // 2
LANES = 128

EPS = 1e-06
THETA = 1000000.0
SCALE = HEAD_SIZE ** (-0.5)
BF = jnp.bfloat16
F32 = jnp.float32


def swap_core(x):
    n = lax.axis_size("replica")
    return lax.ppermute(x, "replica", [(i, i ^ 1) for i in range(n)])


def shard_swap(x, k):
    n = lax.axis_size("shard")
    return lax.ppermute(x, "shard", [(i, i ^ k) for i in range(n)])


def pair_swap(x):
    n = lax.axis_size("replica")
    return lax.ppermute(x, "replica", [(i, i ^ 2) for i in range(n)])


def spread(x):
    return [x] + [shard_swap(x, k) for k in range(1, lax.axis_size("shard"))]


def line_sum(where, x):
    line = lax.axis_size("replica") // 2
    half = line // 2

    def hop(value, chips):
        links = [(2 * a + k, 2 * b + k) for a, b in chips for k in range(2)]
        return lax.ppermute(value, "replica", links)

    total = x
    for i in range(half - 1):
        arrived = hop(total, [(i, i + 1), (line - 1 - i, line - 2 - i)])
        total = total + arrived
    arrived = hop(total, [(half - 1, half), (half, half - 1)])
    total = total + arrived
    for i in reversed(range(half - 1)):
        arrived = hop(total, [(i + 1, i), (line - 2 - i, line - 1 - i)])
        total = pick(where, total, arrived, i, line - 1 - i)
    return total


def dot(a, b):
    return jnp.dot(a, b, preferred_element_type=F32)


def dot_t(a, b):
    return lax.dot_general(a, b, (((1,), (1,)), ((), ())), preferred_element_type=F32)


def t_dot(a, b):
    return lax.dot_general(a, b, (((0,), (0,)), ((), ())), preferred_element_type=F32)


GRANTS = {'pack': 12, 'attend': 5, 'down_back': 5, 'feed': 9, 'narrow': 4, 'back': 18, 'wide': 8, 'merge': 5, 'finish': 4, 'lay': 18, 'close': 6, 'ydown': 4, 'open': 3, 'yout': 4, 'pick': 4, 'stack': 8}


def call(kernel, name, outs, where, args, scratch=(), flops=0, space=pltpu.VMEM):
    grant = GRANTS[name]
    total = sum(a.size * a.dtype.itemsize for a in args)
    total += sum(o.size * jnp.dtype(o.dtype).itemsize for o in outs)
    vmem = pl.BlockSpec(memory_space=pltpu.VMEM)
    return pl.pallas_call(
        kernel,
        out_shape=outs,
        in_specs=[pl.BlockSpec(memory_space=pltpu.SMEM)] + [pl.BlockSpec(memory_space=space)] * len(args),
        out_specs=[vmem] * len(outs),
        scratch_shapes=list(scratch),
        cost_estimate=pl.CostEstimate(flops=flops, bytes_accessed=total, transcendentals=0),
        compiler_params=pltpu.CompilerParams(vmem_limit_bytes=grant << 20),
    )(where, *args)


def shape(dims, dtype=BF):
    return jax.ShapeDtypeStruct(dims, dtype)


def rows_at(start, size):
    return pl.ds(pl.multiple_of(start, 8 if size % 16 else 16), size)


def mark_kernel(where, out):
    for i in range(out.shape[0]):
        out[i] = where[i]


def mark(where):
    smem = pl.BlockSpec(memory_space=pltpu.SMEM)
    return pl.pallas_call(
        mark_kernel, out_shape=shape(where.shape, jnp.int32), in_specs=[smem], out_specs=smem,
        compiler_params=pltpu.CompilerParams(vmem_limit_bytes=1 << 20),
    )(where)


def pack_kernel(shards, where, gate, up, *rest):
    outs, (stage, gate_buf, up_buf, sems) = rest[:shards], rest[shards:]
    rows, slab = gate.shape[0], stage.shape[3]
    step = rows // 2
    s, c = where[0], where[1]
    copies = []
    for i in range(2):
        at = pl.ds(i * step, step)
        for m, (src, dst) in enumerate(((gate, gate_buf), (up, up_buf))):
            copy = pltpu.make_async_copy(src.at[at], dst.at[at], sems.at[i, m])
            copy.start()
            copies.append(copy)
    for i in range(2):
        for m, buf in enumerate((gate_buf, up_buf)):
            copies[2 * i + m].wait()
            for j in range(2 * shards):

                @pl.when(c == j % 2)
                def _(i=i, j=j, m=m, buf=buf):
                    at = slice(i * step, (i + 1) * step)
                    stage[(j // 2) ^ s, m, at] = buf[at, j * slab : (j + 1) * slab]

    outs[0][:rows] = stage[0, 0]
    outs[0][rows:] = stage[0, 1]
    for k in range(1, shards):
        outs[k][...] = stage[k, where[2] & 1]


def pack(where, gate, up, shards):
    rows, ff = gate.shape
    slab = ff // (2 * shards)
    outs = [shape((2 * rows, slab))] + [shape((rows, slab))] * (shards - 1)
    return call(
        functools.partial(pack_kernel, shards), "pack", outs, where, [gate, up],
        [
            pltpu.VMEM((shards, 2, rows, slab), BF), pltpu.VMEM((rows, ff), BF),
            pltpu.VMEM((rows, ff), BF), pltpu.SemaphoreType.DMA((2, 2)),
        ],
        space=pltpu.HBM,
    )


def open_kernel(where, wq, wo, g1, g2, b, send, extra, one, two, three, sems):
    half = wq.shape[0] // 2
    width = wo.shape[1]
    first = wq.shape[1] // LANES
    count = send.shape[0]
    vectors = ((g1, one), (g2, two), (b, three))
    vector_copies = [
        pltpu.make_async_copy(src, dst, sems.at[count + i]) for i, (src, dst) in enumerate(vectors)
    ]
    for copy in vector_copies:
        copy.start()
    at = rows_at(where[1] * half, half)
    for parity in range(2):

        @pl.when((where[2] & 1) == parity)
        def _(parity=parity):
            copies = []
            for i in range(count):
                block = parity * count + i
                source = wq if block < first else wo
                start = (block if block < first else block - first) * LANES
                copy = pltpu.make_async_copy(
                    source.at[at, pl.ds(start, LANES)], send.at[i, pl.ds(0, half)], sems.at[i]
                )
                copy.start()
                copies.append(copy)
            for copy in copies:
                copy.wait()

    line = lax.broadcasted_iota(jnp.int32, extra.shape, 0)
    value = jnp.zeros(extra.shape, F32)
    for i, copy in enumerate(vector_copies):
        copy.wait()
        row = vectors[i][1][...].astype(F32)[None]
        row = jnp.concatenate([row, jnp.zeros((1, width - row.shape[1]), F32)], axis=1)
        value = jnp.where(line == i, row, value)
    extra[...] = value.astype(BF)
    for parity in range(2):

        @pl.when((where[2] & 1) == parity)
        def _(parity=parity):
            for i in range(count):
                block = parity * count + i - first
                lanes = slice(block * LANES, (block + 1) * LANES)
                tail = jnp.zeros((8, LANES), BF) if block < 0 else extra[:, lanes]
                send[i, half:] = tail


def open_rows(where, wq, wo, g1, g2, b):
    half = wq.shape[0] // 2
    count = (wq.shape[1] + wo.shape[1]) // LANES // 2
    outs = [shape((count, half + 8, LANES)), shape((8, wo.shape[1]))]
    args = [pltpu.with_memory_space_constraint(v, pltpu.HBM) for v in (wq, wo, g1, g2, b)]
    scratch = [pltpu.VMEM(v.shape, BF) for v in (g1, g2, b)]
    scratch.append(pltpu.SemaphoreType.DMA((count + 3,)))
    return call(open_kernel, "open", outs, where, args, scratch, space=pltpu.HBM)


def place_blocks(w_ref, wo_ref, riders, s, low, high, core):
    half = low[0].shape[1] - 8
    rows = 2 * half
    first = w_ref.shape[1] // LANES
    for k in range(1, len(low) + 1):
        at = rows_at((s ^ k) * rows + core * half, half)
        count = low[k - 1].shape[0]
        for block in range(2 * count):
            piece = (low if block < count else high)[k - 1]
            if block < first:
                lanes = slice(block * LANES, (block + 1) * LANES)
                w_ref[at, lanes] = piece[block % count, :half]
            else:
                lanes = slice((block - first) * LANES, (block - first + 1) * LANES)
                wo_ref[at, lanes] = piece[block % count, :half]
                if riders is not None:
                    riders[k - 1, :, lanes] = piece[block % count, half:]


def lane_kinds(x):
    lane = lax.broadcasted_iota(jnp.int32, x.shape, 1)
    low = lane < HEAD_SIZE
    zero = jnp.zeros_like(x)
    turned = pltpu.roll(x, HEAD_SIZE, 1)
    return [
        [jnp.where(low, x, zero), jnp.where(low, zero, turned)],
        [jnp.where(low, turned, zero), jnp.where(low, zero, x)],
    ]


def swap_halves(x):
    lane = lax.broadcasted_iota(jnp.int32, x.shape, 1)
    first = (lane % HEAD_SIZE) < HALF
    return jnp.where(first, pltpu.roll(x, LANES - HALF, 1), pltpu.roll(x, HALF, 1))


def attend_kernel(shards, where, x, seg, own, own_out, extra, *rest):
    n = shards - 1
    direct, passed, direct_other, passed_other = (rest[i * n : (i + 1) * n] for i in range(4))
    n1_ref, q_ref, k_ref, v_ref, p_ref, o_ref, w_ref, vec_ref, cos_ref, sin_ref = rest[
        4 * n : 4 * n + 10
    ]
    h_ref, n2_ref, wo_ref, riders = rest[4 * n + 10 :]
    s, c = where[0], where[1]
    width, joined_width = x.shape[1], own.shape[1]
    w_ref[rows_at(s * own.shape[0], own.shape[0])] = own[...]
    wo_ref[rows_at(s * own.shape[0], own.shape[0])] = own_out[...]
    for parity in range(2):

        @pl.when((where[2] & 1) == parity)
        def _(parity=parity):
            pair = (direct, passed)
            place_blocks(w_ref, wo_ref, riders, s, pair[parity], pair[1 - parity], c)
            pair = (direct_other, passed_other)
            place_blocks(w_ref, wo_ref, None, s, pair[parity], pair[1 - parity], 1 - c)

    lines = extra.shape[0]
    is_gain = lax.broadcasted_iota(jnp.int32, vec_ref.shape, 0) < 2
    vec = jnp.zeros(vec_ref.shape, F32)
    gap = jnp.zeros((lines, joined_width - width), F32)
    for k in range(shards):
        value = (extra[...] if k == 0 else riders[k - 1]).astype(F32)
        value = jnp.concatenate([value, gap], axis=1)
        gains = pltpu.roll(value, (s ^ k) * (width // shards), 1)
        biases = pltpu.roll(value, (s ^ k) * (joined_width // shards), 1)
        vec = vec + jnp.where(is_gain, gains, biases)
    vec_ref[...] = vec
    xf = x[...].astype(F32)
    root = lax.rsqrt(jnp.mean(xf * xf, axis=1, keepdims=True) + EPS)
    n1 = (xf * root * vec[0:1, :width]).astype(BF)
    n1_ref[...] = n1
    joined = dot(n1, w_ref[...]) + vec[2:3]
    tokens = x.shape[0]
    square = (tokens, LANES)
    down = lax.broadcasted_iota(jnp.int32, square, 0)
    along = lax.broadcasted_iota(jnp.int32, square, 1)
    of_key = jnp.broadcast_to(seg[...], square).astype(F32)
    of_query = of_key.T
    allowed = (along <= down) & (of_key == of_query)
    before = jnp.where(of_key < of_query, 1.0, 0.0)
    position = down.astype(F32) - jnp.sum(before, axis=1, keepdims=True)
    power = (along % HALF).astype(F32) * (2.0 / HEAD_SIZE)
    angle = position * jnp.exp(power * -math.log(THETA))
    cosine = jnp.cos(angle)
    sine = jnp.sin(angle)
    sine = jnp.where((along % HEAD_SIZE) < HALF, -sine, sine)
    cos_ref[...] = cosine
    sin_ref[...] = sine

    def turn(v):
        return v * cosine + swap_halves(v) * sine

    keys = turn(joined[:, width : width + LANES])
    values = joined[:, width + LANES : width + 2 * LANES]
    keys_low = keys.astype(BF)
    values_low = values.astype(BF)
    k_ref[...] = keys_low
    v_ref[...] = values_low
    key_kinds = lane_kinds(keys_low.astype(F32))
    value_kinds = lane_kinds(values_low.astype(F32))
    key_kinds = [[k.astype(BF) for k in ks] for ks in key_kinds]
    value_kinds = [[v.astype(BF) for v in vs] for vs in value_kinds]
    for i in range(PAIRS):
        q = turn(joined[:, i * LANES : (i + 1) * LANES]).astype(BF)
        q_ref[:, i * LANES : (i + 1) * LANES] = q
        mixed = jnp.zeros(q.shape, F32)
        for side in range(2):
            h = 2 * i + side
            g = h // GROUP
            scores = dot_t(q, key_kinds[g][side]) * SCALE
            scores = jnp.where(allowed, scores, -1e30)
            top = jnp.max(scores, axis=-1, keepdims=True)
            e = jnp.exp(scores - top)
            p = e / jnp.sum(e, axis=-1, keepdims=True)
            p_ref[h] = p
            mixed = mixed + dot(p.astype(BF), value_kinds[g][side])
        o_ref[:, i * LANES : (i + 1) * LANES] = mixed.astype(BF)

    h = xf + dot(o_ref[...], wo_ref[...])
    h_ref[...] = h
    root = lax.rsqrt(jnp.mean(h * h, axis=1, keepdims=True) + EPS)
    n2_ref[...] = (h * root * vec[1:2, :width]).astype(BF)


def attend(where, x, seg, own, own_out, extra, pieces, shards):
    tokens, width = x.shape
    joined = own.shape[1]
    outs = [
        shape((tokens, width)), shape((tokens, width)), shape((tokens, LANES)),
        shape((tokens, LANES)), shape((QUERY_HEADS, tokens, tokens), F32),
        shape((tokens, width)), shape((width, joined)), shape((extra.shape[0], joined), F32),
        shape((tokens, LANES), F32), shape((tokens, LANES), F32),
        shape(x.shape, F32), shape(x.shape), shape((width, width)),
    ]
    return call(
        functools.partial(attend_kernel, shards), "attend", outs, where,
        [x, seg, own, own_out, extra, *pieces],
        [pltpu.VMEM((shards - 1,) + extra.shape, BF)],
        flops=2 * tokens * width * (joined + width) + 8 * QUERY_HEADS * tokens * tokens * LANES,
    )


def down_back_kernel(pieces, where, down, *rest):
    parts, (dact_ref, dy_ref) = rest[:pieces], rest[pieces:]
    tokens = parts[0].shape[0]
    for i in range(pieces):
        dy_ref[i * tokens : (i + 1) * tokens] = parts[i][...]
    slab = dact_ref.shape[1]
    w = down[rows_at(where[1] * slab, slab)]
    step = 4 * tokens

    @pl.loop(0, pieces // 4)
    def _(i):
        at = pl.ds(pl.multiple_of(i * step, step), step)
        dact_ref[at] = dot_t(dy_ref[at], w)


def down_back(where, down, parts, slab):
    tokens, width = parts[0].shape
    total = tokens * len(parts)
    outs = [shape((total, slab), F32), shape((total, width))]
    return call(
        functools.partial(down_back_kernel, len(parts)), "down_back", outs, where,
        [down, *parts], flops=2 * total * width * slab,
    )


def feed_kernel(shards, where, dact, dy, *rest):
    pieces = 2 * shards
    parts, rest = rest[:pieces], rest[pieces:]
    own, direct, passed = rest[0], rest[1:shards], rest[shards : 2 * shards - 1]
    rest = rest[2 * shards - 1 :]
    d1_ref, d2_ref, act_ref, dgate_ref, dup_ref, n_ref, wg_ref, wu_ref = rest
    s = where[0]
    tokens = parts[0].shape[0]
    rows = own.shape[0] // 2
    wg_ref[rows_at(s * rows, rows)] = own[:rows]
    wu_ref[rows_at(s * rows, rows)] = own[rows:]
    for parity, (first, second) in enumerate(((wg_ref, wu_ref), (wu_ref, wg_ref))):

        @pl.when((where[2] & 1) == parity)
        def _(first=first, second=second):
            for k in range(1, shards):
                at = rows_at((s ^ k) * rows, rows)
                first[at] = direct[k - 1][...]
                second[at] = passed[k - 1][...]

    for i in range(pieces):
        n_ref[i * tokens : (i + 1) * tokens] = parts[i][...]
    step = 4 * tokens

    @pl.loop(0, pieces // 4)
    def _(i):
        at = pl.ds(pl.multiple_of(i * step, step), step)
        block = n_ref[at]
        gate = dot(block, wg_ref[...])
        up = dot(block, wu_ref[...])
        sigma = jax.nn.sigmoid(gate)
        swish = gate * sigma
        act_ref[at] = (swish * up).astype(BF)
        da = dact[at]
        dgate_ref[at] = (da * up * sigma * (1.0 + gate * (1.0 - sigma))).astype(BF)
        dup_ref[at] = (da * swish).astype(BF)

    cut = d1_ref.shape[0]
    grad = t_dot(act_ref[...], dy[...])
    d1_ref[...] = grad[:cut].astype(BF)
    d2_ref[...] = grad[cut:].astype(BF)


def feed(where, dact, dy, parts, weights, shards):
    total, slab = dact.shape
    width = dy.shape[1]
    cut = slab // 32 * 16
    outs = [
        shape((cut, width)), shape((slab - cut, width)), shape((total, slab)),
        shape((total, slab)), shape((total, slab)), shape((total, width)),
        shape((width, slab)), shape((width, slab)),
    ]
    return call(
        functools.partial(feed_kernel, shards), "feed", outs, where,
        [dact, dy, *parts, *weights], flops=6 * total * width * slab,
    )


def wide_kernel(shards, where, n, dgate, dup, *rest):
    outs, acc = rest[:shards], rest[shards]
    rows = outs[0].shape[0] // 2
    s = where[0]
    acc[...] = t_dot(n[...], dgate[...])
    for k in range(shards):
        outs[k][:rows] = acc[rows_at((s ^ k) * rows, rows)].astype(BF)
    acc[...] = t_dot(n[...], dup[...])
    for k in range(shards):
        outs[k][rows:] = acc[rows_at((s ^ k) * rows, rows)].astype(BF)


def wide(where, n, dgate, dup, shards):
    total, width = n.shape
    slab = dgate.shape[1]
    outs = [shape((2 * width // shards, slab))] * shards
    return call(
        functools.partial(wide_kernel, shards), "wide", outs, where, [n, dgate, dup],
        [pltpu.VMEM((width, slab), F32)], flops=4 * total * width * slab,
    )


def lay_kernel(shards, where, *rest):
    mine, other = rest[:shards], rest[shards : 2 * shards]
    gate_ref, up_ref, stage = rest[2 * shards :]
    rows, slab = gate_ref.shape[0], stage.shape[2]
    s, c = where[0], where[1]
    for k in range(shards):
        stage[k] = mine[k][...]
        stage[shards + k] = other[k][...]
    for j in range(2 * shards):
        at = ((j // 2) ^ s) + jnp.where(c == j % 2, 0, shards)
        gate_ref[:, j * slab : (j + 1) * slab] = stage[at, :rows].astype(F32)
        up_ref[:, j * slab : (j + 1) * slab] = stage[at, rows:].astype(F32)


def lay(where, mine, other):
    shards = len(mine)
    rows, slab = mine[0].shape[0] // 2, mine[0].shape[1]
    outs = [shape((rows, 2 * shards * slab), F32)] * 2
    return call(
        functools.partial(lay_kernel, shards), "lay", outs, where, [*mine, *other],
        [pltpu.VMEM((2 * shards, 2 * rows, slab), BF)],
    )


def narrow_kernel(where, dgate, dup, wg, wu, keep, give):
    count = keep.shape[0]

    def block(at):
        return dot_t(dgate[at], wg[...]) + dot_t(dup[at], wu[...])

    give[...] = block(slice(count, 2 * count)).astype(BF)
    keep[...] = block(slice(0, count))


def narrow(where, dgate, dup, wg, wu):
    total, slab = dgate.shape
    width = wg.shape[0]
    outs = [shape((total // 2, width), F32), shape((total // 2, width))]
    return call(
        narrow_kernel, "narrow", outs, where, [dgate, dup, wg, wu],
        flops=4 * total * width * slab,
    )


def back_kernel(shards, tall, where, *rest):
    dn, rest = rest[:shards], rest[shards:]
    hidden, ct, x, vec, wout, wqkv, mixed, n1, query, keys, values, probs, cos, sin = rest[:14]
    gt_ref, keep, give, da_ref, acc_q, acc_o, dob_ref = rest[14:]
    s, c = where[0], where[1]
    tokens, width = x.shape
    joined = wqkv.shape[1]
    rows = width // shards
    half = rows // 2
    cosine, sine = cos[...], sin[...]
    gain1, gain2 = vec[0:1, :width], vec[1:2, :width]

    dn2 = dn[0][...]
    for k in range(1, shards):
        dn2 = dn2 + dn[k][...].astype(F32)
    h = hidden[...]
    root = lax.rsqrt(jnp.mean(h * h, axis=1, keepdims=True) + EPS)
    g_norm2 = jnp.sum(dn2 * h * root, axis=0, keepdims=True)
    e = dn2 * gain2
    mean = jnp.mean(e * h, axis=1, keepdims=True)
    dh = ct[...].astype(F32) + root * e - h * (root * root * root * mean)
    dab = dh.astype(BF)
    gt_ref[...] = dh
    acc_o[...] = t_dot(mixed[...], dab)
    dob_ref[...] = dot_t(dab, wout[...]).astype(BF)

    key_kinds = [[k.astype(BF) for k in ks] for ks in lane_kinds(keys[...].astype(F32))]
    value_kinds = [[v.astype(BF) for v in vs] for vs in lane_kinds(values[...].astype(F32))]
    zero = jnp.zeros((tokens, LANES), F32)
    d_key = [[zero, zero], [zero, zero]]
    d_value = [[zero, zero], [zero, zero]]

    def turn_back(v):
        return v * cosine - swap_halves(v) * sine

    for i in range(PAIRS):
        q = query[:, i * LANES : (i + 1) * LANES]
        do = dob_ref[:, i * LANES : (i + 1) * LANES]
        dq = zero
        for side in range(2):
            head = 2 * i + side
            g = head // GROUP
            p = probs[head]
            dp = dot_t(do, value_kinds[g][side])
            d_value[g][side] = d_value[g][side] + t_dot(p.astype(BF), do)
            ds = (p * (dp - jnp.sum(p * dp, axis=-1, keepdims=True))).astype(BF)
            dq = dq + dot(ds, key_kinds[g][side])
            d_key[g][side] = d_key[g][side] + t_dot(ds, q)
        da_ref[:, i * LANES : (i + 1) * LANES] = turn_back(dq * SCALE).astype(BF)

    low = lax.broadcasted_iota(jnp.int32, (tokens, LANES), 1) < HEAD_SIZE

    def collect(parts):
        first = jnp.where(low, parts[0][0], parts[1][1])
        second = jnp.where(low, parts[1][0], parts[0][1])
        return first + pltpu.roll(second, HEAD_SIZE, 1)

    da_ref[:, width : width + LANES] = turn_back(collect(d_key) * SCALE).astype(BF)
    da_ref[:, width + LANES :] = collect(d_value).astype(BF)
    da = da_ref[...]
    acc_q[...] = t_dot(n1[...], da)
    g_bias = jnp.sum(da.astype(F32), axis=0, keepdims=True)
    dn1 = dot_t(da, wqkv[...])
    xf = x[...].astype(F32)
    root = lax.rsqrt(jnp.mean(xf * xf, axis=1, keepdims=True) + EPS)
    g_norm1 = jnp.sum(dn1 * xf * root, axis=0, keepdims=True)
    e = dn1 * gain1
    mean = jnp.mean(e * xf, axis=1, keepdims=True)
    gt_ref[...] = gt_ref[...] + root * e - xf * (root * root * root * mean)

    blank = jnp.zeros((5, LANES), F32)
    for target, side in ((keep, c), (give, 1 - c)):
        for k in range(shards):
            at = rows_at((s ^ k) * rows + side * half, half)
            for b in range(joined // LANES):
                lanes = slice(b * LANES, (b + 1) * LANES)
                base = b * (half + 8)
                target[k, base : base + half] = acc_q[at, lanes].astype(target.dtype)
                if (b + 1) * LANES <= width:
                    head = [g_norm1[:, lanes], g_norm2[:, lanes]]
                else:
                    head = [blank[:2]]
                tail = jnp.concatenate(head + [g_bias[:, lanes], blank], axis=0)
                target[k, base + half : base + half + 8] = tail.astype(target.dtype)
            for b in range(width // LANES):
                lanes = slice(b * LANES, (b + 1) * LANES)
                base = tall + b * half
                target[k, base : base + half] = acc_o[at, lanes].astype(target.dtype)


def layout_of(width, joined, rows):
    half = rows // 2
    tall = joined // LANES * (half + 8)
    return tall, tall + width // LANES * half


def down_kernel(where, act, down, keep, give):
    count = keep.shape[0]
    slab = act.shape[1]
    w = down[rows_at(where[1] * slab, slab)]
    give[...] = dot(act[count:], w).astype(BF)
    keep[...] = dot(act[:count], w)


def down_project(where, act, down):
    total, slab = act.shape
    width = down.shape[1]
    outs = [shape((total // 2, width), F32), shape((total // 2, width))]
    return call(
        down_kernel, "ydown", outs, where, [act, down], flops=2 * total * width * slab
    )


def pick_kernel(low, high, where, total, arrived, out):
    inside = (where[2] > low) & (where[2] < high)

    @pl.when(inside)
    def _():
        out[...] = total[...]

    @pl.when(jnp.logical_not(inside))
    def _():
        out[...] = arrived[...]


def pick(where, total, arrived, low, high):
    return call(
        functools.partial(pick_kernel, low, high), "pick", [shape(total.shape)], where,
        [total, arrived],
    )[0]


def stack_kernel(where, *rest):
    mine, other, out = rest[: len(rest) // 2], rest[len(rest) // 2 : -1], rest[-1]
    slab = out.shape[0] // 2
    for parts, side in ((mine, where[1]), (other, 1 - where[1])):
        start = side * slab
        for part in parts:
            out[rows_at(start, part.shape[0])] = part[...].astype(F32)
            start = start + part.shape[0]


def stack(where, mine, other):
    rows = 2 * sum(p.shape[0] for p in mine)
    outs = [shape((rows, mine[0].shape[1]), F32)]
    return call(stack_kernel, "stack", outs, where, [*mine, *other])[0]


def back(where, dn, hidden, ct, x, vec, wout, wqkv, mixed, n1, query, keys, values, probs, cos, sin):
    shards = len(dn)
    tokens, width = x.shape
    joined = wqkv.shape[1]
    tall, whole = layout_of(width, joined, width // shards)
    outs = [
        shape(x.shape, F32), shape((shards, whole, LANES), F32), shape((shards, whole, LANES)),
    ]
    return call(
        functools.partial(back_kernel, shards, tall), "back", outs, where,
        [*dn, hidden, ct, x, vec, wout, wqkv, mixed, n1, query, keys, values, probs, cos, sin],
        [
            pltpu.VMEM((tokens, joined), BF), pltpu.VMEM((width, joined), F32),
            pltpu.VMEM((width, width), F32), pltpu.VMEM((tokens, width), BF),
        ],
        flops=4 * tokens * width * (joined + width),
    )


def merge_kernel(shards, where, keep, arrived, *outs):
    for k in range(shards):
        total = keep[k] + arrived[k].astype(F32)
        outs[k][...] = total.astype(outs[k].dtype)


def merge(where, keep, arrived):
    shards = keep.shape[0]
    outs = [shape(keep.shape[1:], F32)] + [shape(keep.shape[1:])] * (shards - 1)
    return call(functools.partial(merge_kernel, shards), "merge", outs, where, [keep, arrived])


def finish_kernel(where, own, *rest):
    value = own[...]
    for piece in rest[:-1]:
        value = value + piece[...].astype(F32)
    rest[-1][...] = value.astype(BF)


def finish(where, parts):
    return call(finish_kernel, "finish", [shape(parts[0].shape)], where, parts)[0]


def close_kernel(tall, where, mine, other, qkv_ref, out_ref, one_ref, two_ref, bias_ref):
    s, c = where[0], where[1]
    half = qkv_ref.shape[0] // 2
    for source, side in ((mine, c), (other, 1 - c)):
        at = pl.ds(pl.multiple_of(side * half, 8), half)
        for b in range(qkv_ref.shape[1] // LANES):
            base = b * (half + 8)
            qkv_ref[at, b * LANES : (b + 1) * LANES] = source[base : base + half].astype(F32)
        for b in range(out_ref.shape[1] // LANES):
            base = tall + b * half
            out_ref[at, b * LANES : (b + 1) * LANES] = source[base : base + half].astype(F32)
    starts = [b * (half + 8) + half for b in range(qkv_ref.shape[1] // LANES)]
    vec = jnp.concatenate([mine[at : at + 8].astype(F32) for at in starts], axis=1)
    width = vec.shape[1]
    for i, ref in enumerate((one_ref, two_ref, bias_ref)):
        turned = pltpu.roll(vec, lax.rem(width - s * ref.shape[0], width), 1)
        ref[...] = turned[i, : ref.shape[0]]


def close(where, mine, other, rows, width, joined, tall):
    outs = [shape((rows, joined), F32), shape((rows, width), F32)]
    outs += [shape((n,), F32) for n in (rows, rows, joined * rows // width)]
    return call(functools.partial(close_kernel, tall), "close", outs, where, [mine, other])


def body(
    tokens, seg_ids, norm1_gain, w_qkv, b_qkv, w_out, norm2_gain, w_gate, w_up, w_down, cotangent
):
    shards = lax.axis_size("shard")
    shard = lax.axis_index("shard")
    replica = lax.axis_index("replica")
    core = replica & 1
    where = jnp.stack([shard, core, replica >> 1]).astype(jnp.int32)
    _, width = tokens.shape
    rows = norm1_gain.shape[0]
    joined = w_qkv.shape[1]
    slab = w_gate.shape[1] // (2 * shards)
    block, extra = open_rows(where, w_qkv, w_out, norm1_gain, norm2_gain, b_qkv)
    pieces = spread(block)[1:]
    pieces += [pair_swap(p) for p in pieces]
    pieces += [swap_core(p) for p in pieces]

    packed = pack(
        where, *(pltpu.with_memory_space_constraint(w, pltpu.HBM) for w in (w_gate, w_up)), shards
    )
    direct = [shard_swap(packed[k], k) for k in range(1, shards)]
    passed = [pair_swap(w) for w in direct]
    dy = spread(cotangent)
    dy = dy + [swap_core(p) for p in dy]

    (
        n_one, query, keys, values, probs, mixed, wqkv, vec, cosine, sine, hidden, n_two, wout
    ) = attend(where, tokens, seg_ids, w_qkv, w_out, extra, pieces, shards)
    n_parts = spread(n_two)
    n_parts = n_parts + [swap_core(p) for p in n_parts]

    dact, dy_all = down_back(where, w_down, dy, slab)
    down_one, down_two, act, d_gate, d_up, n_all, wgate, wup = feed(
        where, dact, dy_all, n_parts, [packed[0], *direct, *passed], shards
    )
    down_one, down_two = line_sum(where, down_one), line_sum(where, down_two)

    def plane_sum(keep, give):
        arrived = swap_core(give)
        parts = (shards, -1, keep.shape[-1])
        total = merge(where, keep.reshape(parts), arrived.reshape(parts))
        return [total[0]] + [shard_swap(total[k], k) for k in range(1, shards)]

    dn = plane_sum(*narrow(where, d_gate, d_up, wgate, wup))

    grads = wide(where, n_all, d_gate, d_up, shards)
    grads = [grads[0]] + [shard_swap(grads[k], k) for k in range(1, shards)]
    grads = [line_sum(where, g) for g in grads]
    marked = mark(where)
    gate_part, up_part = lay(marked, grads, [swap_core(g) for g in grads])

    down_part = stack(where, [down_one, down_two], [swap_core(down_one), swap_core(down_two)])
    y = plane_sum(*down_project(where, act, w_down))
    layer_out = call(finish_kernel, "yout", [shape(hidden.shape)], where, [hidden, *y])[0]

    grad_tokens, keep, give = back(
        where, dn, hidden, cotangent, tokens, vec, wout, wqkv, mixed, n_one, query, keys, values,
        probs, cosine, sine,
    )
    parts = plane_sum(keep, give)
    tall, _ = layout_of(width, joined, rows)
    item = line_sum(where, finish(where, parts))
    qkv_part, out_part, one_part, two_part, bias_part = close(
        where, item, swap_core(item), rows, width, joined, tall
    )
    return (
        layer_out,
        grad_tokens,
        one_part,
        qkv_part,
        bias_part,
        out_part,
        two_part,
        gate_part,
        up_part,
        down_part,
    )


def solution(mesh):
    split = P(("shard", "replica"), None)
    matrix = P("shard", None)
    vector = P("shard")
    in_specs = (
        split, split, vector, matrix, vector, matrix, vector, matrix, matrix, matrix, split,
    )
    out_specs = (split, split, vector, matrix, vector, matrix, vector, matrix, matrix, matrix)
    return jax.shard_map(body, mesh=mesh, in_specs=in_specs, out_specs=out_specs, check_vma=False)
```

```python
import functools
import math
import jax
import jax.numpy as jnp
from jax import lax
from jax.experimental import pallas as pl
from jax.experimental.pallas import tpu as pltpu
from jax.sharding import PartitionSpec as P


QUERY_HEADS = 14
KEY_VALUE_HEADS = 2
HEAD_SIZE = 64
HALF = HEAD_SIZE // 2
GROUP = QUERY_HEADS // KEY_VALUE_HEADS
PAIRS = QUERY_HEADS // 2
LANES = 128

EPS = 1e-06
THETA = 1000000.0
SCALE = HEAD_SIZE ** (-0.5)
BF = jnp.bfloat16
F32 = jnp.float32


def swap_core(x):
    n = lax.axis_size("replica")
    return lax.ppermute(x, "replica", [(i, i ^ 1) for i in range(n)])


def shard_swap(x, k):
    n = lax.axis_size("shard")
    return lax.ppermute(x, "shard", [(i, i ^ k) for i in range(n)])


def pair_swap(x):
    n = lax.axis_size("replica")
    return lax.ppermute(x, "replica", [(i, i ^ 2) for i in range(n)])


def spread(x):
    return [x] + [shard_swap(x, k) for k in range(1, lax.axis_size("shard"))]


def line_sum(where, x):
    line = lax.axis_size("replica") // 2
    half = line // 2

    def hop(value, chips):
        links = [(2 * a + k, 2 * b + k) for a, b in chips for k in range(2)]
        return lax.ppermute(value, "replica", links)

    total = x
    for i in range(half - 1):
        arrived = hop(total, [(i, i + 1), (line - 1 - i, line - 2 - i)])
        total = total + arrived
    arrived = hop(total, [(half - 1, half), (half, half - 1)])
    total = total + arrived
    for i in reversed(range(half - 1)):
        arrived = hop(total, [(i + 1, i), (line - 2 - i, line - 1 - i)])
        total = pick(where, total, arrived, i, line - 1 - i)
    return total


def dot(a, b):
    return jnp.dot(a, b, preferred_element_type=F32)


def dot_t(a, b):
    return lax.dot_general(a, b, (((1,), (1,)), ((), ())), preferred_element_type=F32)


def t_dot(a, b):
    return lax.dot_general(a, b, (((0,), (0,)), ((), ())), preferred_element_type=F32)


GRANTS = {'pack': 12, 'attend': 5, 'down_back': 5, 'feed': 9, 'narrow': 4, 'back': 18, 'wide': 8, 'merge': 5, 'finish': 4, 'lay': 24, 'close': 6, 'ydown': 4, 'open': 3, 'yout': 4, 'pick': 4, 'stack': 8}


def call(kernel, name, outs, where, args, scratch=(), flops=0, space=pltpu.VMEM):
    grant = GRANTS[name]
    total = sum(a.size * a.dtype.itemsize for a in args)
    total += sum(o.size * jnp.dtype(o.dtype).itemsize for o in outs)
    vmem = pl.BlockSpec(memory_space=pltpu.VMEM)
    return pl.pallas_call(
        kernel,
        out_shape=outs,
        in_specs=[pl.BlockSpec(memory_space=pltpu.SMEM)] + [pl.BlockSpec(memory_space=space)] * len(args),
        out_specs=[vmem] * len(outs),
        scratch_shapes=list(scratch),
        cost_estimate=pl.CostEstimate(flops=flops, bytes_accessed=total, transcendentals=0),
        compiler_params=pltpu.CompilerParams(vmem_limit_bytes=grant << 20),
    )(where, *args)


def shape(dims, dtype=BF):
    return jax.ShapeDtypeStruct(dims, dtype)


def rows_at(start, size):
    return pl.ds(pl.multiple_of(start, 8 if size % 16 else 16), size)


def pack_kernel(shards, where, gate, up, *rest):
    outs, (stage, gate_buf, up_buf, sems) = rest[:shards], rest[shards:]
    rows, slab = gate.shape[0], stage.shape[3]
    step = rows // 2
    s, c = where[0], where[1]
    copies = []
    for i in range(2):
        at = pl.ds(i * step, step)
        for m, (src, dst) in enumerate(((gate, gate_buf), (up, up_buf))):
            copy = pltpu.make_async_copy(src.at[at], dst.at[at], sems.at[i, m])
            copy.start()
            copies.append(copy)
    for i in range(2):
        for m, buf in enumerate((gate_buf, up_buf)):
            copies[2 * i + m].wait()
            for j in range(2 * shards):

                @pl.when(c == j % 2)
                def _(i=i, j=j, m=m, buf=buf):
                    at = slice(i * step, (i + 1) * step)
                    stage[(j // 2) ^ s, m, at] = buf[at, j * slab : (j + 1) * slab]

    outs[0][:rows] = stage[0, 0]
    outs[0][rows:] = stage[0, 1]
    for k in range(1, shards):
        outs[k][...] = stage[k, where[2] & 1]


def pack(where, gate, up, shards):
    rows, ff = gate.shape
    slab = ff // (2 * shards)
    outs = [shape((2 * rows, slab))] + [shape((rows, slab))] * (shards - 1)
    return call(
        functools.partial(pack_kernel, shards), "pack", outs, where, [gate, up],
        [
            pltpu.VMEM((shards, 2, rows, slab), BF), pltpu.VMEM((rows, ff), BF),
            pltpu.VMEM((rows, ff), BF), pltpu.SemaphoreType.DMA((2, 2)),
        ],
        space=pltpu.HBM,
    )


def open_kernel(where, wq, wo, g1, g2, b, send, extra, one, two, three, sems):
    half = wq.shape[0] // 2
    width = wo.shape[1]
    first = wq.shape[1] // LANES
    count = send.shape[0]
    vectors = ((g1, one), (g2, two), (b, three))
    vector_copies = [
        pltpu.make_async_copy(src, dst, sems.at[count + i]) for i, (src, dst) in enumerate(vectors)
    ]
    for copy in vector_copies:
        copy.start()
    at = rows_at(where[1] * half, half)
    for parity in range(2):

        @pl.when((where[2] & 1) == parity)
        def _(parity=parity):
            copies = []
            for i in range(count):
                block = parity * count + i
                source = wq if block < first else wo
                start = (block if block < first else block - first) * LANES
                copy = pltpu.make_async_copy(
                    source.at[at, pl.ds(start, LANES)], send.at[i, pl.ds(0, half)], sems.at[i]
                )
                copy.start()
                copies.append(copy)
            for copy in copies:
                copy.wait()

    line = lax.broadcasted_iota(jnp.int32, extra.shape, 0)
    value = jnp.zeros(extra.shape, F32)
    for i, copy in enumerate(vector_copies):
        copy.wait()
        row = vectors[i][1][...].astype(F32)[None]
        row = jnp.concatenate([row, jnp.zeros((1, width - row.shape[1]), F32)], axis=1)
        value = jnp.where(line == i, row, value)
    extra[...] = value.astype(BF)
    for parity in range(2):

        @pl.when((where[2] & 1) == parity)
        def _(parity=parity):
            for i in range(count):
                block = parity * count + i - first
                lanes = slice(block * LANES, (block + 1) * LANES)
                tail = jnp.zeros((8, LANES), BF) if block < 0 else extra[:, lanes]
                send[i, half:] = tail


def open_rows(where, wq, wo, g1, g2, b):
    half = wq.shape[0] // 2
    count = (wq.shape[1] + wo.shape[1]) // LANES // 2
    outs = [shape((count, half + 8, LANES)), shape((8, wo.shape[1]))]
    args = [pltpu.with_memory_space_constraint(v, pltpu.HBM) for v in (wq, wo, g1, g2, b)]
    scratch = [pltpu.VMEM(v.shape, BF) for v in (g1, g2, b)]
    scratch.append(pltpu.SemaphoreType.DMA((count + 3,)))
    return call(open_kernel, "open", outs, where, args, scratch, space=pltpu.HBM)


def place_blocks(w_ref, wo_ref, riders, s, low, high, core):
    half = low[0].shape[1] - 8
    rows = 2 * half
    first = w_ref.shape[1] // LANES
    for k in range(1, len(low) + 1):
        at = rows_at((s ^ k) * rows + core * half, half)
        count = low[k - 1].shape[0]
        for block in range(2 * count):
            piece = (low if block < count else high)[k - 1]
            if block < first:
                lanes = slice(block * LANES, (block + 1) * LANES)
                w_ref[at, lanes] = piece[block % count, :half]
            else:
                lanes = slice((block - first) * LANES, (block - first + 1) * LANES)
                wo_ref[at, lanes] = piece[block % count, :half]
                if riders is not None:
                    riders[k - 1, :, lanes] = piece[block % count, half:]


def lane_kinds(x):
    lane = lax.broadcasted_iota(jnp.int32, x.shape, 1)
    low = lane < HEAD_SIZE
    zero = jnp.zeros_like(x)
    turned = pltpu.roll(x, HEAD_SIZE, 1)
    return [
        [jnp.where(low, x, zero), jnp.where(low, zero, turned)],
        [jnp.where(low, turned, zero), jnp.where(low, zero, x)],
    ]


def swap_halves(x):
    lane = lax.broadcasted_iota(jnp.int32, x.shape, 1)
    first = (lane % HEAD_SIZE) < HALF
    return jnp.where(first, pltpu.roll(x, LANES - HALF, 1), pltpu.roll(x, HALF, 1))


def attend_kernel(shards, where, x, seg, own, own_out, extra, *rest):
    n = shards - 1
    direct, passed, direct_other, passed_other = (rest[i * n : (i + 1) * n] for i in range(4))
    n1_ref, q_ref, k_ref, v_ref, p_ref, o_ref, w_ref, vec_ref, cos_ref, sin_ref = rest[
        4 * n : 4 * n + 10
    ]
    h_ref, n2_ref, wo_ref, riders = rest[4 * n + 10 :]
    s, c = where[0], where[1]
    width, joined_width = x.shape[1], own.shape[1]
    w_ref[rows_at(s * own.shape[0], own.shape[0])] = own[...]
    wo_ref[rows_at(s * own.shape[0], own.shape[0])] = own_out[...]
    for parity in range(2):

        @pl.when((where[2] & 1) == parity)
        def _(parity=parity):
            pair = (direct, passed)
            place_blocks(w_ref, wo_ref, riders, s, pair[parity], pair[1 - parity], c)
            pair = (direct_other, passed_other)
            place_blocks(w_ref, wo_ref, None, s, pair[parity], pair[1 - parity], 1 - c)

    lines = extra.shape[0]
    is_gain = lax.broadcasted_iota(jnp.int32, vec_ref.shape, 0) < 2
    vec = jnp.zeros(vec_ref.shape, F32)
    gap = jnp.zeros((lines, joined_width - width), F32)
    for k in range(shards):
        value = (extra[...] if k == 0 else riders[k - 1]).astype(F32)
        value = jnp.concatenate([value, gap], axis=1)
        gains = pltpu.roll(value, (s ^ k) * (width // shards), 1)
        biases = pltpu.roll(value, (s ^ k) * (joined_width // shards), 1)
        vec = vec + jnp.where(is_gain, gains, biases)
    vec_ref[...] = vec
    xf = x[...].astype(F32)
    root = lax.rsqrt(jnp.mean(xf * xf, axis=1, keepdims=True) + EPS)
    n1 = (xf * root * vec[0:1, :width]).astype(BF)
    n1_ref[...] = n1
    joined = dot(n1, w_ref[...]) + vec[2:3]
    tokens = x.shape[0]
    square = (tokens, LANES)
    down = lax.broadcasted_iota(jnp.int32, square, 0)
    along = lax.broadcasted_iota(jnp.int32, square, 1)
    of_key = jnp.broadcast_to(seg[...], square).astype(F32)
    of_query = of_key.T
    allowed = (along <= down) & (of_key == of_query)
    before = jnp.where(of_key < of_query, 1.0, 0.0)
    position = down.astype(F32) - jnp.sum(before, axis=1, keepdims=True)
    power = (along % HALF).astype(F32) * (2.0 / HEAD_SIZE)
    angle = position * jnp.exp(power * -math.log(THETA))
    cosine = jnp.cos(angle)
    sine = jnp.sin(angle)
    sine = jnp.where((along % HEAD_SIZE) < HALF, -sine, sine)
    cos_ref[...] = cosine
    sin_ref[...] = sine

    def turn(v):
        return v * cosine + swap_halves(v) * sine

    keys = turn(joined[:, width : width + LANES])
    values = joined[:, width + LANES : width + 2 * LANES]
    keys_low = keys.astype(BF)
    values_low = values.astype(BF)
    k_ref[...] = keys_low
    v_ref[...] = values_low
    key_kinds = lane_kinds(keys_low.astype(F32))
    value_kinds = lane_kinds(values_low.astype(F32))
    key_kinds = [[k.astype(BF) for k in ks] for ks in key_kinds]
    value_kinds = [[v.astype(BF) for v in vs] for vs in value_kinds]
    for i in range(PAIRS):
        q = turn(joined[:, i * LANES : (i + 1) * LANES]).astype(BF)
        q_ref[:, i * LANES : (i + 1) * LANES] = q
        mixed = jnp.zeros(q.shape, F32)
        for side in range(2):
            h = 2 * i + side
            g = h // GROUP
            scores = dot_t(q, key_kinds[g][side]) * SCALE
            scores = jnp.where(allowed, scores, -1e30)
            top = jnp.max(scores, axis=-1, keepdims=True)
            e = jnp.exp(scores - top)
            p = e / jnp.sum(e, axis=-1, keepdims=True)
            p_ref[h] = p
            mixed = mixed + dot(p.astype(BF), value_kinds[g][side])
        o_ref[:, i * LANES : (i + 1) * LANES] = mixed.astype(BF)

    h = xf + dot(o_ref[...], wo_ref[...])
    h_ref[...] = h
    root = lax.rsqrt(jnp.mean(h * h, axis=1, keepdims=True) + EPS)
    n2_ref[...] = (h * root * vec[1:2, :width]).astype(BF)


def attend(where, x, seg, own, own_out, extra, pieces, shards):
    tokens, width = x.shape
    joined = own.shape[1]
    outs = [
        shape((tokens, width)), shape((tokens, width)), shape((tokens, LANES)),
        shape((tokens, LANES)), shape((QUERY_HEADS, tokens, tokens), F32),
        shape((tokens, width)), shape((width, joined)), shape((extra.shape[0], joined), F32),
        shape((tokens, LANES), F32), shape((tokens, LANES), F32),
        shape(x.shape, F32), shape(x.shape), shape((width, width)),
    ]
    return call(
        functools.partial(attend_kernel, shards), "attend", outs, where,
        [x, seg, own, own_out, extra, *pieces],
        [pltpu.VMEM((shards - 1,) + extra.shape, BF)],
        flops=2 * tokens * width * (joined + width) + 8 * QUERY_HEADS * tokens * tokens * LANES,
    )


def down_back_kernel(pieces, where, down, *rest):
    parts, (dact_ref, dy_ref) = rest[:pieces], rest[pieces:]
    tokens = parts[0].shape[0]
    for i in range(pieces):
        dy_ref[i * tokens : (i + 1) * tokens] = parts[i][...]
    slab = dact_ref.shape[1]
    w = down[rows_at(where[1] * slab, slab)]
    step = 4 * tokens

    @pl.loop(0, pieces // 4)
    def _(i):
        at = pl.ds(pl.multiple_of(i * step, step), step)
        dact_ref[at] = dot_t(dy_ref[at], w)


def down_back(where, down, parts, slab):
    tokens, width = parts[0].shape
    total = tokens * len(parts)
    outs = [shape((total, slab), F32), shape((total, width))]
    return call(
        functools.partial(down_back_kernel, len(parts)), "down_back", outs, where,
        [down, *parts], flops=2 * total * width * slab,
    )


def feed_kernel(shards, where, dact, dy, *rest):
    pieces = 2 * shards
    parts, rest = rest[:pieces], rest[pieces:]
    own, direct, passed = rest[0], rest[1:shards], rest[shards : 2 * shards - 1]
    rest = rest[2 * shards - 1 :]
    d1_ref, d2_ref, act_ref, dgate_ref, dup_ref, n_ref, wg_ref, wu_ref = rest
    s = where[0]
    tokens = parts[0].shape[0]
    rows = own.shape[0] // 2
    wg_ref[rows_at(s * rows, rows)] = own[:rows]
    wu_ref[rows_at(s * rows, rows)] = own[rows:]
    for parity, (first, second) in enumerate(((wg_ref, wu_ref), (wu_ref, wg_ref))):

        @pl.when((where[2] & 1) == parity)
        def _(first=first, second=second):
            for k in range(1, shards):
                at = rows_at((s ^ k) * rows, rows)
                first[at] = direct[k - 1][...]
                second[at] = passed[k - 1][...]

    for i in range(pieces):
        n_ref[i * tokens : (i + 1) * tokens] = parts[i][...]
    step = 4 * tokens

    @pl.loop(0, pieces // 4)
    def _(i):
        at = pl.ds(pl.multiple_of(i * step, step), step)
        block = n_ref[at]
        gate = dot(block, wg_ref[...])
        up = dot(block, wu_ref[...])
        sigma = jax.nn.sigmoid(gate)
        swish = gate * sigma
        act_ref[at] = (swish * up).astype(BF)
        da = dact[at]
        dgate_ref[at] = (da * up * sigma * (1.0 + gate * (1.0 - sigma))).astype(BF)
        dup_ref[at] = (da * swish).astype(BF)

    cut = d1_ref.shape[0]
    grad = t_dot(act_ref[...], dy[...])
    d1_ref[...] = grad[:cut].astype(BF)
    d2_ref[...] = grad[cut:].astype(BF)


def feed(where, dact, dy, parts, weights, shards):
    total, slab = dact.shape
    width = dy.shape[1]
    cut = slab // 32 * 16
    outs = [
        shape((cut, width)), shape((slab - cut, width)), shape((total, slab)),
        shape((total, slab)), shape((total, slab)), shape((total, width)),
        shape((width, slab)), shape((width, slab)),
    ]
    return call(
        functools.partial(feed_kernel, shards), "feed", outs, where,
        [dact, dy, *parts, *weights], flops=6 * total * width * slab,
    )


def dense_plan(rows, slab):
    whole, rest = slab // LANES, slab % LANES
    fold = LANES // math.gcd(rest, LANES) if rest else 1
    if rest == 0 or rows % (8 * fold):
        fold = 1
    part = rows // fold
    blocks = -(-fold * rest // LANES)
    return whole, rest, fold, part, blocks, whole * rows + blocks * part


def wide_kernel(shards, where, n, dgate, dup, *rest):
    outs, acc = rest[:shards], rest[shards]
    width, slab = acc.shape
    rows = width // shards
    whole, rest, fold, part, blocks, tall = dense_plan(rows, slab)
    s = where[0]
    for m, d in enumerate((dgate, dup)):
        acc[...] = t_dot(n[...], d[...])
        for k in range(shards):
            top = (s ^ k) * rows
            base = m * tall
            for b in range(whole):
                lanes = slice(b * LANES, (b + 1) * LANES)
                outs[k][base : base + rows] = acc[rows_at(top, rows), lanes].astype(BF)
                base += rows
            if rest:
                folded = [
                    acc[pl.ds(pl.multiple_of(top + i * part, 8), part), whole * LANES :]
                    for i in range(fold)
                ]
                gap = blocks * LANES - fold * rest
                if gap:
                    folded.append(jnp.zeros((part, gap), F32))
                folded = jnp.concatenate(folded, axis=1) if len(folded) > 1 else folded[0]
                for b in range(blocks):
                    lanes = slice(b * LANES, (b + 1) * LANES)
                    outs[k][base : base + part] = folded[:, lanes].astype(BF)
                    base += part


def wide(where, n, dgate, dup, shards):
    total, width = n.shape
    slab = dgate.shape[1]
    outs = [shape((2 * dense_plan(width // shards, slab)[-1], LANES))] * shards
    return call(
        functools.partial(wide_kernel, shards), "wide", outs, where, [n, dgate, dup],
        [pltpu.VMEM((width, slab), F32)], flops=4 * total * width * slab,
    )


def lay_kernel(shards, where, *rest):
    mine, other = rest[:shards], rest[shards : 2 * shards]
    gate_ref, up_ref, stage = rest[2 * shards :]
    rows, slab = stage.shape[1] // 2, stage.shape[2]
    whole, rest, fold, part, blocks, tall = dense_plan(rows, slab)
    s, c = where[0], where[1]
    for k, source in enumerate((*mine, *other)):
        for m in range(2):
            base = m * tall
            for b in range(whole):
                lanes = slice(b * LANES, (b + 1) * LANES)
                stage[k, m * rows : (m + 1) * rows, lanes] = source[base : base + rows].astype(F32)
                base += rows
            if rest:
                folded = [
                    source[base + b * part : base + (b + 1) * part].astype(F32)
                    for b in range(blocks)
                ]
                folded = jnp.concatenate(folded, axis=1) if blocks > 1 else folded[0]
                for i in range(fold):
                    at = slice(m * rows + i * part, m * rows + (i + 1) * part)
                    stage[k, at, whole * LANES :] = folded[:, i * rest : (i + 1) * rest]
    step = rows // 4 if rows % 32 == 0 else rows

    @pl.loop(0, rows // step)
    def _(i):
        top = pl.multiple_of(i * step, 8)
        for j in range(2 * shards):
            at = ((j // 2) ^ s) + jnp.where(c == j % 2, 0, shards)
            lanes = slice(j * slab, (j + 1) * slab)
            gate_ref[pl.ds(top, step), lanes] = stage[at, pl.ds(top, step)]
            up_ref[pl.ds(top, step), lanes] = stage[at, pl.ds(pl.multiple_of(top + rows, 8), step)]


def lay(where, mine, other, rows, slab):
    shards = len(mine)
    outs = [shape((rows, 2 * shards * slab), F32)] * 2
    return call(
        functools.partial(lay_kernel, shards), "lay", outs, where, [*mine, *other],
        [pltpu.VMEM((2 * shards, 2 * rows, slab), F32)],
    )


def narrow_kernel(where, dgate, dup, wg, wu, keep, give):
    count = keep.shape[0]

    def block(at):
        return dot_t(dgate[at], wg[...]) + dot_t(dup[at], wu[...])

    give[...] = block(slice(count, 2 * count)).astype(BF)
    keep[...] = block(slice(0, count))


def narrow(where, dgate, dup, wg, wu):
    total, slab = dgate.shape
    width = wg.shape[0]
    outs = [shape((total // 2, width), F32), shape((total // 2, width))]
    return call(
        narrow_kernel, "narrow", outs, where, [dgate, dup, wg, wu],
        flops=4 * total * width * slab,
    )


def back_kernel(shards, tall, where, *rest):
    dn, rest = rest[:shards], rest[shards:]
    hidden, ct, x, vec, wout, wqkv, mixed, n1, query, keys, values, probs, cos, sin = rest[:14]
    gt_ref, keep, give, da_ref, acc_q, acc_o, dob_ref = rest[14:]
    s, c = where[0], where[1]
    tokens, width = x.shape
    joined = wqkv.shape[1]
    rows = width // shards
    half = rows // 2
    cosine, sine = cos[...], sin[...]
    gain1, gain2 = vec[0:1, :width], vec[1:2, :width]

    dn2 = dn[0][...]
    for k in range(1, shards):
        dn2 = dn2 + dn[k][...].astype(F32)
    h = hidden[...]
    root = lax.rsqrt(jnp.mean(h * h, axis=1, keepdims=True) + EPS)
    g_norm2 = jnp.sum(dn2 * h * root, axis=0, keepdims=True)
    e = dn2 * gain2
    mean = jnp.mean(e * h, axis=1, keepdims=True)
    dh = ct[...].astype(F32) + root * e - h * (root * root * root * mean)
    dab = dh.astype(BF)
    gt_ref[...] = dh
    acc_o[...] = t_dot(mixed[...], dab)
    dob_ref[...] = dot_t(dab, wout[...]).astype(BF)

    key_kinds = [[k.astype(BF) for k in ks] for ks in lane_kinds(keys[...].astype(F32))]
    value_kinds = [[v.astype(BF) for v in vs] for vs in lane_kinds(values[...].astype(F32))]
    zero = jnp.zeros((tokens, LANES), F32)
    d_key = [[zero, zero], [zero, zero]]
    d_value = [[zero, zero], [zero, zero]]

    def turn_back(v):
        return v * cosine - swap_halves(v) * sine

    for i in range(PAIRS):
        q = query[:, i * LANES : (i + 1) * LANES]
        do = dob_ref[:, i * LANES : (i + 1) * LANES]
        dq = zero
        for side in range(2):
            head = 2 * i + side
            g = head // GROUP
            p = probs[head]
            dp = dot_t(do, value_kinds[g][side])
            d_value[g][side] = d_value[g][side] + t_dot(p.astype(BF), do)
            ds = (p * (dp - jnp.sum(p * dp, axis=-1, keepdims=True))).astype(BF)
            dq = dq + dot(ds, key_kinds[g][side])
            d_key[g][side] = d_key[g][side] + t_dot(ds, q)
        da_ref[:, i * LANES : (i + 1) * LANES] = turn_back(dq * SCALE).astype(BF)

    low = lax.broadcasted_iota(jnp.int32, (tokens, LANES), 1) < HEAD_SIZE

    def collect(parts):
        first = jnp.where(low, parts[0][0], parts[1][1])
        second = jnp.where(low, parts[1][0], parts[0][1])
        return first + pltpu.roll(second, HEAD_SIZE, 1)

    da_ref[:, width : width + LANES] = turn_back(collect(d_key) * SCALE).astype(BF)
    da_ref[:, width + LANES :] = collect(d_value).astype(BF)
    da = da_ref[...]
    acc_q[...] = t_dot(n1[...], da)
    g_bias = jnp.sum(da.astype(F32), axis=0, keepdims=True)
    dn1 = dot_t(da, wqkv[...])
    xf = x[...].astype(F32)
    root = lax.rsqrt(jnp.mean(xf * xf, axis=1, keepdims=True) + EPS)
    g_norm1 = jnp.sum(dn1 * xf * root, axis=0, keepdims=True)
    e = dn1 * gain1
    mean = jnp.mean(e * xf, axis=1, keepdims=True)
    gt_ref[...] = gt_ref[...] + root * e - xf * (root * root * root * mean)

    blank = jnp.zeros((5, LANES), F32)
    for target, side in ((keep, c), (give, 1 - c)):

        @pl.loop(0, shards)
        def _(k, target=target, side=side):
            at = rows_at((s ^ k) * rows + side * half, half)
            for b in range(joined // LANES):
                lanes = slice(b * LANES, (b + 1) * LANES)
                base = b * (half + 8)
                target[k, base : base + half] = acc_q[at, lanes].astype(target.dtype)
                if (b + 1) * LANES <= width:
                    head = [g_norm1[:, lanes], g_norm2[:, lanes]]
                else:
                    head = [blank[:2]]
                tail = jnp.concatenate(head + [g_bias[:, lanes], blank], axis=0)
                target[k, base + half : base + half + 8] = tail.astype(target.dtype)
            for b in range(width // LANES):
                lanes = slice(b * LANES, (b + 1) * LANES)
                base = tall + b * half
                target[k, base : base + half] = acc_o[at, lanes].astype(target.dtype)


def layout_of(width, joined, rows):
    half = rows // 2
    tall = joined // LANES * (half + 8)
    return tall, tall + width // LANES * half


def down_kernel(where, act, down, keep, give):
    count = keep.shape[0]
    slab = act.shape[1]
    w = down[rows_at(where[1] * slab, slab)]
    give[...] = dot(act[count:], w).astype(BF)
    keep[...] = dot(act[:count], w)


def down_project(where, act, down):
    total, slab = act.shape
    width = down.shape[1]
    outs = [shape((total // 2, width), F32), shape((total // 2, width))]
    return call(
        down_kernel, "ydown", outs, where, [act, down], flops=2 * total * width * slab
    )


def pick_kernel(low, high, where, total, arrived, out):
    inside = (where[2] > low) & (where[2] < high)

    @pl.when(inside)
    def _():
        out[...] = total[...]

    @pl.when(jnp.logical_not(inside))
    def _():
        out[...] = arrived[...]


def pick(where, total, arrived, low, high):
    return call(
        functools.partial(pick_kernel, low, high), "pick", [shape(total.shape)], where,
        [total, arrived],
    )[0]


def stack_kernel(where, *rest):
    mine, other, out = rest[: len(rest) // 2], rest[len(rest) // 2 : -1], rest[-1]
    slab = out.shape[0] // 2
    for parts, side in ((mine, where[1]), (other, 1 - where[1])):
        start = side * slab
        for part in parts:
            out[rows_at(start, part.shape[0])] = part[...].astype(F32)
            start = start + part.shape[0]


def stack(where, mine, other):
    rows = 2 * sum(p.shape[0] for p in mine)
    outs = [shape((rows, mine[0].shape[1]), F32)]
    return call(stack_kernel, "stack", outs, where, [*mine, *other])[0]


def back(where, dn, hidden, ct, x, vec, wout, wqkv, mixed, n1, query, keys, values, probs, cos, sin):
    shards = len(dn)
    tokens, width = x.shape
    joined = wqkv.shape[1]
    tall, whole = layout_of(width, joined, width // shards)
    outs = [
        shape(x.shape, F32), shape((shards, whole, LANES), F32), shape((shards, whole, LANES)),
    ]
    return call(
        functools.partial(back_kernel, shards, tall), "back", outs, where,
        [*dn, hidden, ct, x, vec, wout, wqkv, mixed, n1, query, keys, values, probs, cos, sin],
        [
            pltpu.VMEM((tokens, joined), BF), pltpu.VMEM((width, joined), F32),
            pltpu.VMEM((width, width), F32), pltpu.VMEM((tokens, width), BF),
        ],
        flops=4 * tokens * width * (joined + width),
    )


def merge_kernel(shards, where, keep, arrived, *outs):
    for k in range(shards):
        total = keep[k] + arrived[k].astype(F32)
        outs[k][...] = total.astype(outs[k].dtype)


def merge(where, keep, arrived):
    shards = keep.shape[0]
    outs = [shape(keep.shape[1:], F32)] + [shape(keep.shape[1:])] * (shards - 1)
    return call(functools.partial(merge_kernel, shards), "merge", outs, where, [keep, arrived])


def finish_kernel(where, own, *rest):
    value = own[...]
    for piece in rest[:-1]:
        value = value + piece[...].astype(F32)
    rest[-1][...] = value.astype(BF)


def finish_cut_kernel(tall, where, own, *rest):
    arrived, (first, second) = rest[:-2], rest[-2:]
    for out, at in ((first, slice(0, tall)), (second, slice(tall, own.shape[0]))):
        value = own[at]
        for piece in arrived:
            value = value + piece[at].astype(F32)
        out[...] = value.astype(BF)


def finish(where, parts, tall):
    outs = [shape((tall, LANES)), shape((parts[0].shape[0] - tall, LANES))]
    return call(functools.partial(finish_cut_kernel, tall), "finish", outs, where, parts)


def close_kernel(where, mine, mine_out, other, other_out, *refs):
    qkv_ref, out_ref, one_ref, two_ref, bias_ref = refs
    s, c = where[0], where[1]
    half = qkv_ref.shape[0] // 2
    for source, source_out, side in ((mine, mine_out, c), (other, other_out, 1 - c)):
        at = pl.ds(pl.multiple_of(side * half, 8), half)
        for b in range(qkv_ref.shape[1] // LANES):
            base = b * (half + 8)
            qkv_ref[at, b * LANES : (b + 1) * LANES] = source[base : base + half].astype(F32)
        for b in range(out_ref.shape[1] // LANES):
            base = b * half
            out_ref[at, b * LANES : (b + 1) * LANES] = source_out[base : base + half].astype(F32)
    starts = [b * (half + 8) + half for b in range(qkv_ref.shape[1] // LANES)]
    vec = jnp.concatenate([mine[at : at + 8].astype(F32) for at in starts], axis=1)
    width = vec.shape[1]
    for i, ref in enumerate((one_ref, two_ref, bias_ref)):
        turned = pltpu.roll(vec, lax.rem(width - s * ref.shape[0], width), 1)
        ref[...] = turned[i, : ref.shape[0]]


def close(where, parts, rows, width, joined):
    outs = [shape((rows, joined), F32), shape((rows, width), F32)]
    outs += [shape((n,), F32) for n in (rows, rows, joined * rows // width)]
    return call(close_kernel, "close", outs, where, parts)


def body(
    tokens, seg_ids, norm1_gain, w_qkv, b_qkv, w_out, norm2_gain, w_gate, w_up, w_down, cotangent
):
    shards = lax.axis_size("shard")
    shard = lax.axis_index("shard")
    replica = lax.axis_index("replica")
    core = replica & 1
    where = jnp.stack([shard, core, replica >> 1]).astype(jnp.int32)
    _, width = tokens.shape
    rows = norm1_gain.shape[0]
    joined = w_qkv.shape[1]
    slab = w_gate.shape[1] // (2 * shards)
    block, extra = open_rows(where, w_qkv, w_out, norm1_gain, norm2_gain, b_qkv)
    pieces = spread(block)[1:]
    pieces += [pair_swap(p) for p in pieces]
    pieces += [swap_core(p) for p in pieces]

    packed = pack(
        where, *(pltpu.with_memory_space_constraint(w, pltpu.HBM) for w in (w_gate, w_up)), shards
    )
    direct = [shard_swap(packed[k], k) for k in range(1, shards)]
    passed = [pair_swap(w) for w in direct]
    dy = spread(cotangent)
    dy = dy + [swap_core(p) for p in dy]

    (
        n_one, query, keys, values, probs, mixed, wqkv, vec, cosine, sine, hidden, n_two, wout
    ) = attend(where, tokens, seg_ids, w_qkv, w_out, extra, pieces, shards)
    n_parts = spread(n_two)
    n_parts = n_parts + [swap_core(p) for p in n_parts]

    dact, dy_all = down_back(where, w_down, dy, slab)
    down_one, down_two, act, d_gate, d_up, n_all, wgate, wup = feed(
        where, dact, dy_all, n_parts, [packed[0], *direct, *passed], shards
    )
    down_one, down_two = line_sum(where, down_one), line_sum(where, down_two)

    def plane_sum(keep, give):
        arrived = swap_core(give)
        parts = (shards, -1, keep.shape[-1])
        total = merge(where, keep.reshape(parts), arrived.reshape(parts))
        return [total[0]] + [shard_swap(total[k], k) for k in range(1, shards)]

    dn = plane_sum(*narrow(where, d_gate, d_up, wgate, wup))

    grads = wide(where, n_all, d_gate, d_up, shards)
    grads = [grads[0]] + [shard_swap(grads[k], k) for k in range(1, shards)]
    grads = [line_sum(where, g) for g in grads]
    gate_part, up_part = lay(where, grads, [swap_core(g) for g in grads], rows, slab)

    down_part = stack(where, [down_one, down_two], [swap_core(down_one), swap_core(down_two)])
    y = plane_sum(*down_project(where, act, w_down))
    layer_out = call(finish_kernel, "yout", [shape(hidden.shape)], where, [hidden, *y])[0]

    grad_tokens, keep, give = back(
        where, dn, hidden, cotangent, tokens, vec, wout, wqkv, mixed, n_one, query, keys, values,
        probs, cosine, sine,
    )
    parts = plane_sum(keep, give)
    tall, _ = layout_of(width, joined, rows)
    first, second = finish(where, parts, tall)
    first, second = line_sum(where, first), line_sum(where, second)
    swapped = swap_core(first), swap_core(second)
    qkv_part, out_part, one_part, two_part, bias_part = close(
        where, [first, second, *swapped], rows, width, joined
    )
    return (
        layer_out,
        grad_tokens,
        one_part,
        qkv_part,
        bias_part,
        out_part,
        two_part,
        gate_part,
        up_part,
        down_part,
    )


def solution(mesh):
    split = P(("shard", "replica"), None)
    matrix = P("shard", None)
    vector = P("shard")
    in_specs = (
        split, split, vector, matrix, vector, matrix, vector, matrix, matrix, matrix, split,
    )
    out_specs = (split, split, vector, matrix, vector, matrix, vector, matrix, matrix, matrix)
    return jax.shard_map(body, mesh=mesh, in_specs=in_specs, out_specs=out_specs, check_vma=False)
```

```python
import functools
import math
import jax
import jax.numpy as jnp
from jax import lax
from jax.experimental import pallas as pl
from jax.experimental.pallas import tpu as pltpu
from jax.sharding import PartitionSpec as P


QUERY_HEADS = 14
KEY_VALUE_HEADS = 2
HEAD_SIZE = 64
HALF = HEAD_SIZE // 2
GROUP = QUERY_HEADS // KEY_VALUE_HEADS
PAIRS = QUERY_HEADS // 2
LANES = 128

EPS = 1e-06
THETA = 1000000.0
SCALE = HEAD_SIZE ** (-0.5)
BF = jnp.bfloat16
F32 = jnp.float32


def swap_core(x):
    n = lax.axis_size("replica")
    return lax.ppermute(x, "replica", [(i, i ^ 1) for i in range(n)])


def shard_swap(x, k):
    n = lax.axis_size("shard")
    return lax.ppermute(x, "shard", [(i, i ^ k) for i in range(n)])


def pair_swap(x):
    n = lax.axis_size("replica")
    return lax.ppermute(x, "replica", [(i, i ^ 2) for i in range(n)])


def spread(x):
    return [x] + [shard_swap(x, k) for k in range(1, lax.axis_size("shard"))]


def line_sum(where, x):
    line = lax.axis_size("replica") // 2
    half = line // 2

    def hop(value, chips):
        links = [(2 * a + k, 2 * b + k) for a, b in chips for k in range(2)]
        return lax.ppermute(value, "replica", links)

    total = x
    for i in range(half - 1):
        arrived = hop(total, [(i, i + 1), (line - 1 - i, line - 2 - i)])
        total = total + arrived
    arrived = hop(total, [(half - 1, half), (half, half - 1)])
    total = total + arrived
    for i in reversed(range(half - 1)):
        arrived = hop(total, [(i + 1, i), (line - 2 - i, line - 1 - i)])
        total = pick(where, total, arrived, i, line - 1 - i)
    return total


def dot(a, b):
    return jnp.dot(a, b, preferred_element_type=F32)


def dot_t(a, b):
    return lax.dot_general(a, b, (((1,), (1,)), ((), ())), preferred_element_type=F32)


def t_dot(a, b):
    return lax.dot_general(a, b, (((0,), (0,)), ((), ())), preferred_element_type=F32)


GRANTS = {'pack': 12, 'attend': 5, 'down_back': 5, 'feed': 9, 'narrow': 4, 'back': 18, 'wide': 8, 'merge': 5, 'finish': 4, 'lay': 24, 'close': 6, 'ydown': 4, 'open': 3, 'yout': 4, 'pick': 4, 'stack': 8}


def call(kernel, name, outs, where, args, scratch=(), flops=0, space=pltpu.VMEM, steps=1):
    grant = GRANTS[name]
    total = sum(a.size * a.dtype.itemsize for a in args)
    total += sum(o.size * jnp.dtype(o.dtype).itemsize for o in outs)
    vmem = pl.BlockSpec(memory_space=pltpu.VMEM)
    return pl.pallas_call(
        kernel,
        out_shape=outs,
        in_specs=[pl.BlockSpec(memory_space=pltpu.SMEM)] + [pl.BlockSpec(memory_space=space)] * len(args),
        out_specs=[vmem] * len(outs) if steps == 1 else [
            pl.BlockSpec((o.shape[0] // steps, o.shape[1]), lambda i: (i, 0)) for o in outs
        ],
        grid=() if steps == 1 else (steps,),
        scratch_shapes=list(scratch),
        cost_estimate=pl.CostEstimate(flops=flops, bytes_accessed=total, transcendentals=0),
        compiler_params=pltpu.CompilerParams(vmem_limit_bytes=grant << 20),
    )(where, *args)


def shape(dims, dtype=BF):
    return jax.ShapeDtypeStruct(dims, dtype)


def rows_at(start, size):
    return pl.ds(pl.multiple_of(start, 8 if size % 16 else 16), size)


def pack_kernel(shards, where, gate, up, *rest):
    outs, (stage, gate_buf, up_buf, sems) = rest[:shards], rest[shards:]
    rows, slab = gate.shape[0], stage.shape[3]
    step = rows // 2
    s, c = where[0], where[1]
    copies = []
    for i in range(2):
        at = pl.ds(i * step, step)
        for m, (src, dst) in enumerate(((gate, gate_buf), (up, up_buf))):
            copy = pltpu.make_async_copy(src.at[at], dst.at[at], sems.at[i, m])
            copy.start()
            copies.append(copy)
    for i in range(2):
        for m, buf in enumerate((gate_buf, up_buf)):
            copies[2 * i + m].wait()
            for j in range(2 * shards):

                @pl.when(c == j % 2)
                def _(i=i, j=j, m=m, buf=buf):
                    at = slice(i * step, (i + 1) * step)
                    stage[(j // 2) ^ s, m, at] = buf[at, j * slab : (j + 1) * slab]

    outs[0][:rows] = stage[0, 0]
    outs[0][rows:] = stage[0, 1]
    for k in range(1, shards):
        outs[k][...] = stage[k, where[2] & 1]


def pack(where, gate, up, shards):
    rows, ff = gate.shape
    slab = ff // (2 * shards)
    outs = [shape((2 * rows, slab))] + [shape((rows, slab))] * (shards - 1)
    return call(
        functools.partial(pack_kernel, shards), "pack", outs, where, [gate, up],
        [
            pltpu.VMEM((shards, 2, rows, slab), BF), pltpu.VMEM((rows, ff), BF),
            pltpu.VMEM((rows, ff), BF), pltpu.SemaphoreType.DMA((2, 2)),
        ],
        space=pltpu.HBM,
    )


def open_kernel(where, wq, wo, g1, g2, b, send, extra, one, two, three, sems):
    half = wq.shape[0] // 2
    width = wo.shape[1]
    first = wq.shape[1] // LANES
    count = send.shape[0]
    vectors = ((g1, one), (g2, two), (b, three))
    vector_copies = [
        pltpu.make_async_copy(src, dst, sems.at[count + i]) for i, (src, dst) in enumerate(vectors)
    ]
    for copy in vector_copies:
        copy.start()
    at = rows_at(where[1] * half, half)
    for parity in range(2):

        @pl.when((where[2] & 1) == parity)
        def _(parity=parity):
            copies = []
            for i in range(count):
                block = parity * count + i
                source = wq if block < first else wo
                start = (block if block < first else block - first) * LANES
                copy = pltpu.make_async_copy(
                    source.at[at, pl.ds(start, LANES)], send.at[i, pl.ds(0, half)], sems.at[i]
                )
                copy.start()
                copies.append(copy)
            for copy in copies:
                copy.wait()

    line = lax.broadcasted_iota(jnp.int32, extra.shape, 0)
    value = jnp.zeros(extra.shape, F32)
    for i, copy in enumerate(vector_copies):
        copy.wait()
        row = vectors[i][1][...].astype(F32)[None]
        row = jnp.concatenate([row, jnp.zeros((1, width - row.shape[1]), F32)], axis=1)
        value = jnp.where(line == i, row, value)
    extra[...] = value.astype(BF)
    for parity in range(2):

        @pl.when((where[2] & 1) == parity)
        def _(parity=parity):
            for i in range(count):
                block = parity * count + i - first
                lanes = slice(block * LANES, (block + 1) * LANES)
                tail = jnp.zeros((8, LANES), BF) if block < 0 else extra[:, lanes]
                send[i, half:] = tail


def open_rows(where, wq, wo, g1, g2, b):
    half = wq.shape[0] // 2
    count = (wq.shape[1] + wo.shape[1]) // LANES // 2
    outs = [shape((count, half + 8, LANES)), shape((8, wo.shape[1]))]
    args = [pltpu.with_memory_space_constraint(v, pltpu.HBM) for v in (wq, wo, g1, g2, b)]
    scratch = [pltpu.VMEM(v.shape, BF) for v in (g1, g2, b)]
    scratch.append(pltpu.SemaphoreType.DMA((count + 3,)))
    return call(open_kernel, "open", outs, where, args, scratch, space=pltpu.HBM)


def place_blocks(w_ref, wo_ref, riders, s, low, high, core):
    half = low[0].shape[1] - 8
    rows = 2 * half
    first = w_ref.shape[1] // LANES
    for k in range(1, len(low) + 1):
        at = rows_at((s ^ k) * rows + core * half, half)
        count = low[k - 1].shape[0]
        for block in range(2 * count):
            piece = (low if block < count else high)[k - 1]
            if block < first:
                lanes = slice(block * LANES, (block + 1) * LANES)
                w_ref[at, lanes] = piece[block % count, :half]
            else:
                lanes = slice((block - first) * LANES, (block - first + 1) * LANES)
                wo_ref[at, lanes] = piece[block % count, :half]
                if riders is not None:
                    riders[k - 1, :, lanes] = piece[block % count, half:]


def lane_kinds(x):
    lane = lax.broadcasted_iota(jnp.int32, x.shape, 1)
    low = lane < HEAD_SIZE
    zero = jnp.zeros_like(x)
    turned = pltpu.roll(x, HEAD_SIZE, 1)
    return [
        [jnp.where(low, x, zero), jnp.where(low, zero, turned)],
        [jnp.where(low, turned, zero), jnp.where(low, zero, x)],
    ]


def swap_halves(x):
    lane = lax.broadcasted_iota(jnp.int32, x.shape, 1)
    first = (lane % HEAD_SIZE) < HALF
    return jnp.where(first, pltpu.roll(x, LANES - HALF, 1), pltpu.roll(x, HALF, 1))


def attend_kernel(shards, where, x, seg, own, own_out, extra, *rest):
    n = shards - 1
    direct, passed, direct_other, passed_other = (rest[i * n : (i + 1) * n] for i in range(4))
    n1_ref, q_ref, k_ref, v_ref, p_ref, o_ref, w_ref, vec_ref, cos_ref, sin_ref = rest[
        4 * n : 4 * n + 10
    ]
    h_ref, n2_ref, wo_ref, riders = rest[4 * n + 10 :]
    s, c = where[0], where[1]
    width, joined_width = x.shape[1], own.shape[1]
    w_ref[rows_at(s * own.shape[0], own.shape[0])] = own[...]
    wo_ref[rows_at(s * own.shape[0], own.shape[0])] = own_out[...]
    for parity in range(2):

        @pl.when((where[2] & 1) == parity)
        def _(parity=parity):
            pair = (direct, passed)
            place_blocks(w_ref, wo_ref, riders, s, pair[parity], pair[1 - parity], c)
            pair = (direct_other, passed_other)
            place_blocks(w_ref, wo_ref, None, s, pair[parity], pair[1 - parity], 1 - c)

    lines = extra.shape[0]
    is_gain = lax.broadcasted_iota(jnp.int32, vec_ref.shape, 0) < 2
    vec = jnp.zeros(vec_ref.shape, F32)
    gap = jnp.zeros((lines, joined_width - width), F32)
    for k in range(shards):
        value = (extra[...] if k == 0 else riders[k - 1]).astype(F32)
        value = jnp.concatenate([value, gap], axis=1)
        gains = pltpu.roll(value, (s ^ k) * (width // shards), 1)
        biases = pltpu.roll(value, (s ^ k) * (joined_width // shards), 1)
        vec = vec + jnp.where(is_gain, gains, biases)
    vec_ref[...] = vec
    xf = x[...].astype(F32)
    root = lax.rsqrt(jnp.mean(xf * xf, axis=1, keepdims=True) + EPS)
    n1 = (xf * root * vec[0:1, :width]).astype(BF)
    n1_ref[...] = n1
    joined = dot(n1, w_ref[...]) + vec[2:3]
    tokens = x.shape[0]
    square = (tokens, LANES)
    down = lax.broadcasted_iota(jnp.int32, square, 0)
    along = lax.broadcasted_iota(jnp.int32, square, 1)
    of_key = jnp.broadcast_to(seg[...], square).astype(F32)
    of_query = of_key.T
    allowed = (along <= down) & (of_key == of_query)
    before = jnp.where(of_key < of_query, 1.0, 0.0)
    position = down.astype(F32) - jnp.sum(before, axis=1, keepdims=True)
    power = (along % HALF).astype(F32) * (2.0 / HEAD_SIZE)
    angle = position * jnp.exp(power * -math.log(THETA))
    cosine = jnp.cos(angle)
    sine = jnp.sin(angle)
    sine = jnp.where((along % HEAD_SIZE) < HALF, -sine, sine)
    cos_ref[...] = cosine
    sin_ref[...] = sine

    def turn(v):
        return v * cosine + swap_halves(v) * sine

    keys = turn(joined[:, width : width + LANES])
    values = joined[:, width + LANES : width + 2 * LANES]
    keys_low = keys.astype(BF)
    values_low = values.astype(BF)
    k_ref[...] = keys_low
    v_ref[...] = values_low
    key_kinds = lane_kinds(keys_low.astype(F32))
    value_kinds = lane_kinds(values_low.astype(F32))
    key_kinds = [[k.astype(BF) for k in ks] for ks in key_kinds]
    value_kinds = [[v.astype(BF) for v in vs] for vs in value_kinds]
    for i in range(PAIRS):
        q = turn(joined[:, i * LANES : (i + 1) * LANES]).astype(BF)
        q_ref[:, i * LANES : (i + 1) * LANES] = q
        mixed = jnp.zeros(q.shape, F32)
        for side in range(2):
            h = 2 * i + side
            g = h // GROUP
            scores = dot_t(q, key_kinds[g][side]) * SCALE
            scores = jnp.where(allowed, scores, -1e30)
            top = jnp.max(scores, axis=-1, keepdims=True)
            e = jnp.exp(scores - top)
            p = e / jnp.sum(e, axis=-1, keepdims=True)
            p_ref[h] = p
            mixed = mixed + dot(p.astype(BF), value_kinds[g][side])
        o_ref[:, i * LANES : (i + 1) * LANES] = mixed.astype(BF)

    h = xf + dot(o_ref[...], wo_ref[...])
    h_ref[...] = h
    root = lax.rsqrt(jnp.mean(h * h, axis=1, keepdims=True) + EPS)
    n2_ref[...] = (h * root * vec[1:2, :width]).astype(BF)


def attend(where, x, seg, own, own_out, extra, pieces, shards):
    tokens, width = x.shape
    joined = own.shape[1]
    outs = [
        shape((tokens, width)), shape((tokens, width)), shape((tokens, LANES)),
        shape((tokens, LANES)), shape((QUERY_HEADS, tokens, tokens), F32),
        shape((tokens, width)), shape((width, joined)), shape((extra.shape[0], joined), F32),
        shape((tokens, LANES), F32), shape((tokens, LANES), F32),
        shape(x.shape, F32), shape(x.shape), shape((width, width)),
    ]
    return call(
        functools.partial(attend_kernel, shards), "attend", outs, where,
        [x, seg, own, own_out, extra, *pieces],
        [pltpu.VMEM((shards - 1,) + extra.shape, BF)],
        flops=2 * tokens * width * (joined + width) + 8 * QUERY_HEADS * tokens * tokens * LANES,
    )


def down_back_kernel(pieces, where, down, *rest):
    parts, (dact_ref, dy_ref) = rest[:pieces], rest[pieces:]
    tokens = parts[0].shape[0]
    for i in range(pieces):
        dy_ref[i * tokens : (i + 1) * tokens] = parts[i][...]
    slab = dact_ref.shape[1]
    w = down[rows_at(where[1] * slab, slab)]
    step = 4 * tokens

    @pl.loop(0, pieces // 4)
    def _(i):
        at = pl.ds(pl.multiple_of(i * step, step), step)
        dact_ref[at] = dot_t(dy_ref[at], w)


def down_back(where, down, parts, slab):
    tokens, width = parts[0].shape
    total = tokens * len(parts)
    outs = [shape((total, slab), F32), shape((total, width))]
    return call(
        functools.partial(down_back_kernel, len(parts)), "down_back", outs, where,
        [down, *parts], flops=2 * total * width * slab,
    )


def feed_kernel(shards, where, dact, dy, *rest):
    pieces = 2 * shards
    parts, rest = rest[:pieces], rest[pieces:]
    own, direct, passed = rest[0], rest[1:shards], rest[shards : 2 * shards - 1]
    rest = rest[2 * shards - 1 :]
    d1_ref, d2_ref, act_ref, dgate_ref, dup_ref, n_ref, wg_ref, wu_ref = rest
    s = where[0]
    tokens = parts[0].shape[0]
    rows = own.shape[0] // 2
    wg_ref[rows_at(s * rows, rows)] = own[:rows]
    wu_ref[rows_at(s * rows, rows)] = own[rows:]
    for parity, (first, second) in enumerate(((wg_ref, wu_ref), (wu_ref, wg_ref))):

        @pl.when((where[2] & 1) == parity)
        def _(first=first, second=second):
            for k in range(1, shards):
                at = rows_at((s ^ k) * rows, rows)
                first[at] = direct[k - 1][...]
                second[at] = passed[k - 1][...]

    for i in range(pieces):
        n_ref[i * tokens : (i + 1) * tokens] = parts[i][...]
    step = 4 * tokens

    @pl.loop(0, pieces // 4)
    def _(i):
        at = pl.ds(pl.multiple_of(i * step, step), step)
        block = n_ref[at]
        gate = dot(block, wg_ref[...])
        up = dot(block, wu_ref[...])
        sigma = jax.nn.sigmoid(gate)
        swish = gate * sigma
        act_ref[at] = (swish * up).astype(BF)
        da = dact[at]
        dgate_ref[at] = (da * up * sigma * (1.0 + gate * (1.0 - sigma))).astype(BF)
        dup_ref[at] = (da * swish).astype(BF)

    cut = d1_ref.shape[0]
    grad = t_dot(act_ref[...], dy[...])
    d1_ref[...] = grad[:cut].astype(BF)
    d2_ref[...] = grad[cut:].astype(BF)


def feed(where, dact, dy, parts, weights, shards):
    total, slab = dact.shape
    width = dy.shape[1]
    cut = slab // 32 * 16
    outs = [
        shape((cut, width)), shape((slab - cut, width)), shape((total, slab)),
        shape((total, slab)), shape((total, slab)), shape((total, width)),
        shape((width, slab)), shape((width, slab)),
    ]
    return call(
        functools.partial(feed_kernel, shards), "feed", outs, where,
        [dact, dy, *parts, *weights], flops=6 * total * width * slab,
    )


def dense_plan(rows, slab):
    whole, rest = slab // LANES, slab % LANES
    fold = LANES // math.gcd(rest, LANES) if rest else 1
    if rest == 0 or rows % (8 * fold):
        fold = 1
    part = rows // fold
    blocks = -(-fold * rest // LANES)
    return whole, rest, fold, part, blocks, whole * rows + blocks * part


def wide_kernel(shards, where, n, dgate, dup, *rest):
    outs, acc = rest[:shards], rest[shards]
    width, slab = acc.shape
    rows = width // shards
    whole, rest, fold, part, blocks, tall = dense_plan(rows, slab)
    s = where[0]
    for m, d in enumerate((dgate, dup)):
        acc[...] = t_dot(n[...], d[...])
        for k in range(shards):
            top = (s ^ k) * rows
            base = m * tall
            for b in range(whole):
                lanes = slice(b * LANES, (b + 1) * LANES)
                outs[k][base : base + rows] = acc[rows_at(top, rows), lanes].astype(BF)
                base += rows
            if rest:
                folded = [
                    acc[pl.ds(pl.multiple_of(top + i * part, 8), part), whole * LANES :]
                    for i in range(fold)
                ]
                gap = blocks * LANES - fold * rest
                if gap:
                    folded.append(jnp.zeros((part, gap), F32))
                folded = jnp.concatenate(folded, axis=1) if len(folded) > 1 else folded[0]
                for b in range(blocks):
                    lanes = slice(b * LANES, (b + 1) * LANES)
                    outs[k][base : base + part] = folded[:, lanes].astype(BF)
                    base += part


def wide(where, n, dgate, dup, shards):
    total, width = n.shape
    slab = dgate.shape[1]
    outs = [shape((2 * dense_plan(width // shards, slab)[-1], LANES))] * shards
    return call(
        functools.partial(wide_kernel, shards), "wide", outs, where, [n, dgate, dup],
        [pltpu.VMEM((width, slab), F32)], flops=4 * total * width * slab,
    )


def lay_kernel(shards, where, *rest):
    mine, other = rest[:shards], rest[shards : 2 * shards]
    gate_ref, up_ref, stage = rest[2 * shards :]
    rows, slab = stage.shape[1] // 2, stage.shape[2]
    whole, rest, fold, part, blocks, tall = dense_plan(rows, slab)
    s, c = where[0], where[1]

    @pl.when(pl.program_id(0) == 0)
    def _():
        for k, source in enumerate((*mine, *other)):
            for m in range(2):
                base = m * tall
                for b in range(whole):
                    here = slice(m * rows, (m + 1) * rows)
                    lanes = slice(b * LANES, (b + 1) * LANES)
                    stage[k, here, lanes] = source[base : base + rows].astype(F32)
                    base += rows
                if rest:
                    folded = [
                        source[base + b * part : base + (b + 1) * part].astype(F32)
                        for b in range(blocks)
                    ]
                    folded = jnp.concatenate(folded, axis=1) if blocks > 1 else folded[0]
                    for i in range(fold):
                        at = slice(m * rows + i * part, m * rows + (i + 1) * part)
                        stage[k, at, whole * LANES :] = folded[:, i * rest : (i + 1) * rest]

    step = gate_ref.shape[0]
    top = pl.multiple_of(pl.program_id(0) * step, 8)
    for j in range(2 * shards):
        at = ((j // 2) ^ s) + jnp.where(c == j % 2, 0, shards)
        lanes = slice(j * slab, (j + 1) * slab)
        gate_ref[:, lanes] = stage[at, pl.ds(top, step)]
        up_ref[:, lanes] = stage[at, pl.ds(pl.multiple_of(top + rows, 8), step)]


def lay(where, mine, other, rows, slab):
    shards = len(mine)
    outs = [shape((rows, 2 * shards * slab), F32)] * 2
    return call(
        functools.partial(lay_kernel, shards), "lay", outs, where, [*mine, *other],
        [pltpu.VMEM((2 * shards, 2 * rows, slab), F32)],
        steps=4 if rows % 32 == 0 else 2,
    )


def narrow_kernel(where, dgate, dup, wg, wu, keep, give):
    count = keep.shape[0]

    def block(at):
        return dot_t(dgate[at], wg[...]) + dot_t(dup[at], wu[...])

    give[...] = block(slice(count, 2 * count)).astype(BF)
    keep[...] = block(slice(0, count))


def narrow(where, dgate, dup, wg, wu):
    total, slab = dgate.shape
    width = wg.shape[0]
    outs = [shape((total // 2, width), F32), shape((total // 2, width))]
    return call(
        narrow_kernel, "narrow", outs, where, [dgate, dup, wg, wu],
        flops=4 * total * width * slab,
    )


def back_kernel(shards, tall, where, *rest):
    dn, rest = rest[:shards], rest[shards:]
    hidden, ct, x, vec, wout, wqkv, mixed, n1, query, keys, values, probs, cos, sin = rest[:14]
    gt_ref, keep, give, da_ref, acc_q, acc_o, dob_ref = rest[14:]
    s, c = where[0], where[1]
    tokens, width = x.shape
    joined = wqkv.shape[1]
    rows = width // shards
    half = rows // 2
    cosine, sine = cos[...], sin[...]
    gain1, gain2 = vec[0:1, :width], vec[1:2, :width]

    dn2 = dn[0][...]
    for k in range(1, shards):
        dn2 = dn2 + dn[k][...].astype(F32)
    h = hidden[...]
    root = lax.rsqrt(jnp.mean(h * h, axis=1, keepdims=True) + EPS)
    g_norm2 = jnp.sum(dn2 * h * root, axis=0, keepdims=True)
    e = dn2 * gain2
    mean = jnp.mean(e * h, axis=1, keepdims=True)
    dh = ct[...].astype(F32) + root * e - h * (root * root * root * mean)
    dab = dh.astype(BF)
    gt_ref[...] = dh
    acc_o[...] = t_dot(mixed[...], dab)
    dob_ref[...] = dot_t(dab, wout[...]).astype(BF)

    key_kinds = [[k.astype(BF) for k in ks] for ks in lane_kinds(keys[...].astype(F32))]
    value_kinds = [[v.astype(BF) for v in vs] for vs in lane_kinds(values[...].astype(F32))]
    zero = jnp.zeros((tokens, LANES), F32)
    d_key = [[zero, zero], [zero, zero]]
    d_value = [[zero, zero], [zero, zero]]

    def turn_back(v):
        return v * cosine - swap_halves(v) * sine

    for i in range(PAIRS):
        q = query[:, i * LANES : (i + 1) * LANES]
        do = dob_ref[:, i * LANES : (i + 1) * LANES]
        dq = zero
        for side in range(2):
            head = 2 * i + side
            g = head // GROUP
            p = probs[head]
            dp = dot_t(do, value_kinds[g][side])
            d_value[g][side] = d_value[g][side] + t_dot(p.astype(BF), do)
            ds = (p * (dp - jnp.sum(p * dp, axis=-1, keepdims=True))).astype(BF)
            dq = dq + dot(ds, key_kinds[g][side])
            d_key[g][side] = d_key[g][side] + t_dot(ds, q)
        da_ref[:, i * LANES : (i + 1) * LANES] = turn_back(dq * SCALE).astype(BF)

    low = lax.broadcasted_iota(jnp.int32, (tokens, LANES), 1) < HEAD_SIZE

    def collect(parts):
        first = jnp.where(low, parts[0][0], parts[1][1])
        second = jnp.where(low, parts[1][0], parts[0][1])
        return first + pltpu.roll(second, HEAD_SIZE, 1)

    da_ref[:, width : width + LANES] = turn_back(collect(d_key) * SCALE).astype(BF)
    da_ref[:, width + LANES :] = collect(d_value).astype(BF)
    da = da_ref[...]
    acc_q[...] = t_dot(n1[...], da)
    g_bias = jnp.sum(da.astype(F32), axis=0, keepdims=True)
    dn1 = dot_t(da, wqkv[...])
    xf = x[...].astype(F32)
    root = lax.rsqrt(jnp.mean(xf * xf, axis=1, keepdims=True) + EPS)
    g_norm1 = jnp.sum(dn1 * xf * root, axis=0, keepdims=True)
    e = dn1 * gain1
    mean = jnp.mean(e * xf, axis=1, keepdims=True)
    gt_ref[...] = gt_ref[...] + root * e - xf * (root * root * root * mean)

    blank = jnp.zeros((5, LANES), F32)
    for target, side in ((keep, c), (give, 1 - c)):

        @pl.loop(0, shards)
        def _(k, target=target, side=side):
            at = rows_at((s ^ k) * rows + side * half, half)
            for b in range(joined // LANES):
                lanes = slice(b * LANES, (b + 1) * LANES)
                base = b * (half + 8)
                target[k, base : base + half] = acc_q[at, lanes].astype(target.dtype)
                if (b + 1) * LANES <= width:
                    head = [g_norm1[:, lanes], g_norm2[:, lanes]]
                else:
                    head = [blank[:2]]
                tail = jnp.concatenate(head + [g_bias[:, lanes], blank], axis=0)
                target[k, base + half : base + half + 8] = tail.astype(target.dtype)
            for b in range(width // LANES):
                lanes = slice(b * LANES, (b + 1) * LANES)
                base = tall + b * half
                target[k, base : base + half] = acc_o[at, lanes].astype(target.dtype)


def layout_of(width, joined, rows):
    half = rows // 2
    tall = joined // LANES * (half + 8)
    return tall, tall + width // LANES * half


def down_kernel(where, act, down, keep, give):
    count = keep.shape[0]
    slab = act.shape[1]
    w = down[rows_at(where[1] * slab, slab)]
    give[...] = dot(act[count:], w).astype(BF)
    keep[...] = dot(act[:count], w)


def down_project(where, act, down):
    total, slab = act.shape
    width = down.shape[1]
    outs = [shape((total // 2, width), F32), shape((total // 2, width))]
    return call(
        down_kernel, "ydown", outs, where, [act, down], flops=2 * total * width * slab
    )


def pick_kernel(low, high, where, total, arrived, out):
    inside = (where[2] > low) & (where[2] < high)

    @pl.when(inside)
    def _():
        out[...] = total[...]

    @pl.when(jnp.logical_not(inside))
    def _():
        out[...] = arrived[...]


def pick(where, total, arrived, low, high):
    return call(
        functools.partial(pick_kernel, low, high), "pick", [shape(total.shape)], where,
        [total, arrived],
    )[0]


def stack_kernel(where, *rest):
    mine, other, out = rest[: len(rest) // 2], rest[len(rest) // 2 : -1], rest[-1]
    slab = out.shape[0] // 2
    for parts, side in ((mine, where[1]), (other, 1 - where[1])):
        start = side * slab
        for part in parts:
            out[rows_at(start, part.shape[0])] = part[...].astype(F32)
            start = start + part.shape[0]


def stack(where, mine, other):
    rows = 2 * sum(p.shape[0] for p in mine)
    outs = [shape((rows, mine[0].shape[1]), F32)]
    return call(stack_kernel, "stack", outs, where, [*mine, *other])[0]


def back(where, dn, hidden, ct, x, vec, wout, wqkv, mixed, n1, query, keys, values, probs, cos, sin):
    shards = len(dn)
    tokens, width = x.shape
    joined = wqkv.shape[1]
    tall, whole = layout_of(width, joined, width // shards)
    outs = [
        shape(x.shape, F32), shape((shards, whole, LANES), F32), shape((shards, whole, LANES)),
    ]
    return call(
        functools.partial(back_kernel, shards, tall), "back", outs, where,
        [*dn, hidden, ct, x, vec, wout, wqkv, mixed, n1, query, keys, values, probs, cos, sin],
        [
            pltpu.VMEM((tokens, joined), BF), pltpu.VMEM((width, joined), F32),
            pltpu.VMEM((width, width), F32), pltpu.VMEM((tokens, width), BF),
        ],
        flops=4 * tokens * width * (joined + width),
    )


def merge_kernel(shards, where, keep, arrived, *outs):
    for k in range(shards):
        total = keep[k] + arrived[k].astype(F32)
        outs[k][...] = total.astype(outs[k].dtype)


def merge(where, keep, arrived):
    shards = keep.shape[0]
    outs = [shape(keep.shape[1:], F32)] + [shape(keep.shape[1:])] * (shards - 1)
    return call(functools.partial(merge_kernel, shards), "merge", outs, where, [keep, arrived])


def finish_kernel(where, own, *rest):
    value = own[...]
    for piece in rest[:-1]:
        value = value + piece[...].astype(F32)
    rest[-1][...] = value.astype(BF)


def finish_cut_kernel(tall, where, own, *rest):
    arrived, (first, second) = rest[:-2], rest[-2:]
    for out, at in ((first, slice(0, tall)), (second, slice(tall, own.shape[0]))):
        value = own[at]
        for piece in arrived:
            value = value + piece[at].astype(F32)
        out[...] = value.astype(BF)


def finish(where, parts, tall):
    outs = [shape((tall, LANES)), shape((parts[0].shape[0] - tall, LANES))]
    return call(functools.partial(finish_cut_kernel, tall), "finish", outs, where, parts)


def close_kernel(where, mine, mine_out, other, other_out, *refs):
    qkv_ref, out_ref, one_ref, two_ref, bias_ref = refs
    s, c = where[0], where[1]
    half = qkv_ref.shape[0] // 2
    for source, source_out, side in ((mine, mine_out, c), (other, other_out, 1 - c)):
        at = pl.ds(pl.multiple_of(side * half, 8), half)
        for b in range(qkv_ref.shape[1] // LANES):
            base = b * (half + 8)
            qkv_ref[at, b * LANES : (b + 1) * LANES] = source[base : base + half].astype(F32)
        for b in range(out_ref.shape[1] // LANES):
            base = b * half
            out_ref[at, b * LANES : (b + 1) * LANES] = source_out[base : base + half].astype(F32)
    starts = [b * (half + 8) + half for b in range(qkv_ref.shape[1] // LANES)]
    vec = jnp.concatenate([mine[at : at + 8].astype(F32) for at in starts], axis=1)
    width = vec.shape[1]
    for i, ref in enumerate((one_ref, two_ref, bias_ref)):
        turned = pltpu.roll(vec, lax.rem(width - s * ref.shape[0], width), 1)
        ref[...] = turned[i, : ref.shape[0]]


def close(where, parts, rows, width, joined):
    outs = [shape((rows, joined), F32), shape((rows, width), F32)]
    outs += [shape((n,), F32) for n in (rows, rows, joined * rows // width)]
    return call(close_kernel, "close", outs, where, parts)


def body(
    tokens, seg_ids, norm1_gain, w_qkv, b_qkv, w_out, norm2_gain, w_gate, w_up, w_down, cotangent
):
    shards = lax.axis_size("shard")
    shard = lax.axis_index("shard")
    replica = lax.axis_index("replica")
    core = replica & 1
    where = jnp.stack([shard, core, replica >> 1]).astype(jnp.int32)
    _, width = tokens.shape
    rows = norm1_gain.shape[0]
    joined = w_qkv.shape[1]
    slab = w_gate.shape[1] // (2 * shards)
    block, extra = open_rows(where, w_qkv, w_out, norm1_gain, norm2_gain, b_qkv)
    pieces = spread(block)[1:]
    pieces += [pair_swap(p) for p in pieces]
    pieces += [swap_core(p) for p in pieces]

    packed = pack(
        where, *(pltpu.with_memory_space_constraint(w, pltpu.HBM) for w in (w_gate, w_up)), shards
    )
    direct = [shard_swap(packed[k], k) for k in range(1, shards)]
    passed = [pair_swap(w) for w in direct]
    dy = spread(cotangent)
    dy = dy + [swap_core(p) for p in dy]

    (
        n_one, query, keys, values, probs, mixed, wqkv, vec, cosine, sine, hidden, n_two, wout
    ) = attend(where, tokens, seg_ids, w_qkv, w_out, extra, pieces, shards)
    n_parts = spread(n_two)
    n_parts = n_parts + [swap_core(p) for p in n_parts]

    dact, dy_all = down_back(where, w_down, dy, slab)
    down_one, down_two, act, d_gate, d_up, n_all, wgate, wup = feed(
        where, dact, dy_all, n_parts, [packed[0], *direct, *passed], shards
    )
    down_one, down_two = line_sum(where, down_one), line_sum(where, down_two)

    def plane_sum(keep, give):
        arrived = swap_core(give)
        parts = (shards, -1, keep.shape[-1])
        total = merge(where, keep.reshape(parts), arrived.reshape(parts))
        return [total[0]] + [shard_swap(total[k], k) for k in range(1, shards)]

    dn = plane_sum(*narrow(where, d_gate, d_up, wgate, wup))

    grads = wide(where, n_all, d_gate, d_up, shards)
    grads = [grads[0]] + [shard_swap(grads[k], k) for k in range(1, shards)]
    grads = [line_sum(where, g) for g in grads]
    gate_part, up_part = lay(where, grads, [swap_core(g) for g in grads], rows, slab)

    down_part = stack(where, [down_one, down_two], [swap_core(down_one), swap_core(down_two)])
    y = plane_sum(*down_project(where, act, w_down))
    layer_out = call(finish_kernel, "yout", [shape(hidden.shape)], where, [hidden, *y])[0]

    grad_tokens, keep, give = back(
        where, dn, hidden, cotangent, tokens, vec, wout, wqkv, mixed, n_one, query, keys, values,
        probs, cosine, sine,
    )
    parts = plane_sum(keep, give)
    tall, _ = layout_of(width, joined, rows)
    first, second = finish(where, parts, tall)
    first, second = line_sum(where, first), line_sum(where, second)
    swapped = swap_core(first), swap_core(second)
    qkv_part, out_part, one_part, two_part, bias_part = close(
        where, [first, second, *swapped], rows, width, joined
    )
    return (
        layer_out,
        grad_tokens,
        one_part,
        qkv_part,
        bias_part,
        out_part,
        two_part,
        gate_part,
        up_part,
        down_part,
    )


def solution(mesh):
    split = P(("shard", "replica"), None)
    matrix = P("shard", None)
    vector = P("shard")
    in_specs = (
        split, split, vector, matrix, vector, matrix, vector, matrix, matrix, matrix, split,
    )
    out_specs = (split, split, vector, matrix, vector, matrix, vector, matrix, matrix, matrix)
    return jax.shard_map(body, mesh=mesh, in_specs=in_specs, out_specs=out_specs, check_vma=False)
```
